32 devices in a mesh: ray: 16 (over z, x, core), vox: 2 (over y).
Axes of the slice: x: 2, y: 2, z: 4, core: 2. Of those that a mesh axis runs over, the one named last changes fastest.
Arguments:
- tiles: bfloat16 [16, 2, 32, 128, 128], P('ray', 'vox'), may hold values from -0.1875 to 0.1875
- tile_scale: float32 [16, 2, 32], P('ray', 'vox'), may hold values from 0.25 to 4
- tile_row: int32 [16, 2, 32], P('ray', 'vox'), may hold values from 0 to 7
- tile_col: int32 [16, 2, 32], P('ray', 'vox'), may hold values from 0 to 1023
- tile_count: int32 [16, 2], P('ray', 'vox'), may hold values from 16 to 32, as said below
- delays: float32 [16384], P('ray'), may hold values from -6 to 6
- ray_receiver: int32 [16384], P('ray'), may hold values from 0 to 95
- receiver_weight: float32 [1536], P('ray'), may hold values from 0.5 to 2
- smooth_scale: float32 [64], replicated, may hold values from 0.05 to 0.5
Outputs:
- density: float32 [64, 2, 16, 128], P('ray', None, 'vox')
- rays_vec: float32 [16384], P('ray')
The draws below stay inside these ranges and needn't reach their ends.
Inputs may be any that keep to these rules, and one draw needn't show every extreme that they name: `tile_count`: each ray group and voxel slab has between 16 and 32 live tile slots, and some has all 32 in every draw.
All inputs are finite; a program needn't handle non-finite values.
Results may differ from the reference program's by a relative error of at most 0.013.
Values sent between devices are 32-bit elements; how exact they have to be, the bound alone decides.
No kernel may reach another device: no remote copies, remote signals or barrier semaphores. Data moves between devices by JAX's collectives and lax.ppermute only.
A program may use at most 64 MiB of HBM per device.

```python
import math
import jax
import jax.numpy as jnp
from jax import lax

ALT = 64
EPOCHS = 2
LAT = 128
LON_DEV = 8
RAY_TILE = 128
RT = 8
NT = 32
RECV_DEV = 96
ITERS = 2
LON = 16
RAYS = 16384
RECEIVERS = 1536
LINES = 1024
N_RAY = 16
N_VOX = 2


def draw_tile_count(key, part):
    first_key, second_key = jax.random.split(jax.random.fold_in(key, 11))
    counts = jax.random.randint(first_key, (N_RAY * N_VOX,), NT // 2, NT + 1)
    chosen = jax.random.randint(second_key, (), 0, N_RAY * N_VOX)
    counts = jnp.where(jnp.arange(N_RAY * N_VOX) == chosen, NT, counts)
    return counts.reshape(N_RAY, N_VOX).astype(jnp.int32)


def set_ends(array, key, least, high):
    longest = array.shape.index(max(array.shape))
    spots = []
    for shift in (0, 1):
        where = [jax.random.randint(jax.random.fold_in(key, axis), (), 0, length) for axis, length in enumerate(array.shape)]
        where[longest] = (where[longest] + shift) % array.shape[longest]
        spots.append(tuple(where))
    return array.at[spots[0]].set(least).at[spots[1]].set(high)


def steps_of(stream_key, dims, cuts, least, high):
    factor_of = 1.0
    for axis_at, parts in cuts:
        steps = jax.random.uniform(jax.random.fold_in(jax.random.fold_in(stream_key, 6), axis_at), (parts,), jnp.float32, least / len(cuts), high / len(cuts))
        factor_of = factor_of * jnp.repeat(jnp.exp(steps), dims[axis_at] // parts).reshape((-1,) + (1,) * (len(dims) - 1 - axis_at))
    return factor_of


def scatter_about(own_key, dims, width, limit, shards=(), held_as=jnp.bfloat16):
    array = width * jax.random.normal(own_key, dims, jnp.float32)
    if shards:
        array = array * steps_of(own_key, dims, shards, -0.22, 0.18)
    return jnp.clip(array, -limit, limit).astype(held_as)


def setup_inputs(seed: int = 0) -> dict:
    key_of = jax.random.split(jax.random.key(seed), 10)
    tiles = scatter_about(key_of[0], (N_RAY, N_VOX, NT, RAY_TILE, LAT), (LAT * 8) ** -0.5, 0.1875, ((0, 16), (1, 2)))
    tile_scale = jnp.clip(jnp.exp(math.log(4.0) - 2.7725887 * jax.random.uniform(key_of[1], (N_RAY, N_VOX, NT), jnp.float32) ** steps_of(key_of[1], (N_RAY, N_VOX, NT), ((0, 16), (1, 2)), -0.2, 0.2)), 0.25, 4.0)
    tile_row = set_ends(jax.random.randint(key_of[2], (N_RAY, N_VOX, NT), 0, RT), jax.random.fold_in(key_of[2], 1), 0, RT - 1).astype(jnp.int32)
    tile_col = set_ends(jax.random.randint(key_of[3], (N_RAY, N_VOX, NT), 0, LINES), jax.random.fold_in(key_of[3], 1), 0, LINES - 1).astype(jnp.int32)
    tile_count = draw_tile_count(jax.random.fold_in(key_of[9], 71), 0)
    delays = scatter_about(key_of[5], (RAYS,), 1.0, 6.0, ((0, 16),), jnp.float32)
    ray_receiver = set_ends(jax.random.randint(key_of[6], (RAYS,), 0, RECV_DEV), jax.random.fold_in(key_of[6], 1), 0, RECV_DEV - 1).astype(jnp.int32)
    receiver_weight = jnp.clip(jnp.exp(math.log(2.0) - 1.3862944 * jax.random.uniform(key_of[7], (RECEIVERS,), jnp.float32) ** steps_of(key_of[7], (RECEIVERS,), ((0, 16),), -0.2, 0.2)), 0.5, 2.0)
    smooth_scale = jnp.clip(jnp.exp(jax.random.uniform(key_of[8], (ALT,), jnp.float32, math.log(0.05), math.log(0.5))), 0.05, 0.5)
    return dict(tiles=tiles, tile_scale=tile_scale, tile_row=tile_row, tile_col=tile_col, tile_count=tile_count, delays=delays, ray_receiver=ray_receiver, receiver_weight=receiver_weight, smooth_scale=smooth_scale)


LATERAL = 1.0
VERTICAL = 4.0
TEMPORAL = 0.5

def stencil(padded, field):
    lateral = padded[1:-1, 1:-1, 2:, 1:-1] + padded[1:-1, 1:-1, :-2, 1:-1]
    lateral = lateral + padded[1:-1, 1:-1, 1:-1, 2:] + padded[1:-1, 1:-1, 1:-1, :-2]
    vertical = padded[2:, 1:-1, 1:-1, 1:-1] + padded[:-2, 1:-1, 1:-1, 1:-1]
    temporal = padded[1:-1, 2:, 1:-1, 1:-1] + padded[1:-1, :-2, 1:-1, 1:-1]
    centre = 2.0 * (2.0 * LATERAL + VERTICAL + TEMPORAL)
    return centre * field - LATERAL * lateral - VERTICAL * vertical - TEMPORAL * temporal

def laplace(field):
    return stencil(jnp.pad(field, 1), field)

def to_slabs(field):
    return field.reshape(ALT, EPOCHS, N_VOX, LON_DEV, LAT).transpose(2, 0, 1, 3, 4).reshape(N_VOX, LINES, LAT)

def from_slabs(slabs):
    return slabs.reshape(N_VOX, ALT, EPOCHS, LON_DEV, LAT).transpose(1, 2, 0, 3, 4).reshape(ALT, EPOCHS, N_VOX * LON_DEV, LAT)

def reference(tiles, tile_scale, tile_row, tile_col, tile_count, delays, ray_receiver, receiver_weight, smooth_scale):
    live = (jnp.arange(NT)[None, None, :] < tile_count[:, :, None]).astype(jnp.float32)
    effective = tile_scale * live
    table = receiver_weight.reshape(N_RAY, RECV_DEV)
    local_ids = ray_receiver.reshape(N_RAY, RT * RAY_TILE).astype(jnp.int32)
    ray_weight = jnp.take_along_axis(table, local_ids, axis=1).reshape(RAYS)
    damping = smooth_scale[:, None, None, None]
    slab_index = jnp.arange(N_VOX)[:, None]

    def forward(field):
        slabs = to_slabs(field).astype(jnp.bfloat16).astype(jnp.float32)

        def group(inputs):
            tiles_g, eff_g, row_g, col_g = inputs
            lines = slabs[slab_index, col_g]
            rays = jnp.einsum('sktl,skl->skt', tiles_g.astype(jnp.float32), lines) * eff_g[:, :, None]
            onehot = (row_g[:, :, None] == jnp.arange(RT)[None, None, :]).astype(jnp.float32)
            return jnp.einsum('skt,skr->rt', rays, onehot, precision=lax.Precision.HIGHEST).reshape(RT * RAY_TILE)
        return lax.map(group, (tiles, effective, tile_row, tile_col)).reshape(RAYS)

    def backward(weighted):
        groups = weighted.astype(jnp.float32).reshape(N_RAY, RT, RAY_TILE)

        def group(total, inputs):
            tiles_g, eff_g, row_g, col_g, rays_g = inputs
            picked = rays_g[row_g]
            lines = jnp.einsum('sktl,skt->skl', tiles_g.astype(jnp.float32), picked) * eff_g[:, :, None]
            onehot = (col_g[:, :, None] == jnp.arange(LINES)[None, None, :]).astype(jnp.float32)
            return (total + jnp.einsum('skl,skc->scl', lines, onehot, precision=lax.Precision.HIGHEST), None)
        start = jnp.zeros((N_VOX, LINES, LAT), jnp.float32)
        total, _ = lax.scan(group, start, (tiles, effective, tile_row, tile_col, groups))
        return from_slabs(total)
    rays_vec = ray_weight * delays
    left_norm = jnp.sqrt(jnp.sum(rays_vec * rays_vec))
    rays_vec = rays_vec / left_norm
    smooth_vec = jnp.zeros((ALT, EPOCHS, LON, LAT), jnp.float32)
    right = backward((ray_weight * rays_vec).astype(jnp.bfloat16))
    right_norm = jnp.sqrt(jnp.sum(right * right))
    right = right / right_norm
    search = right
    density = jnp.zeros((ALT, EPOCHS, LON, LAT), jnp.float32)
    resid_bar = left_norm
    diag_bar = right_norm
    for iteration in range(ITERS):
        smooth_vec = damping * laplace(right) - right_norm * smooth_vec
        rays_vec = ray_weight * forward(right) - right_norm * rays_vec
        left_norm = jnp.sqrt(jnp.sum(rays_vec * rays_vec) + jnp.sum(smooth_vec * smooth_vec))
        rays_vec = rays_vec / left_norm
        smooth_vec = smooth_vec / left_norm
        right = backward((ray_weight * rays_vec).astype(jnp.bfloat16)) + laplace(damping * smooth_vec) - left_norm * right
        right_norm = jnp.sqrt(jnp.sum(right * right))
        right = right / right_norm
        diag_new = jnp.sqrt(diag_bar * diag_bar + left_norm * left_norm)
        cosine = diag_bar / diag_new
        sine_value = left_norm / diag_new
        coupling = sine_value * right_norm
        diag_bar = -cosine * right_norm
        step_size = cosine * resid_bar
        resid_bar = sine_value * resid_bar
        density = density + step_size / diag_new * search
        search = right - coupling / diag_new * search
    return (density, rays_vec)
```

```python
import jax
import jax.numpy as jnp
from jax import lax
from jax.sharding import PartitionSpec as P

ALT = 64
EPOCHS = 2
LAT = 128
LON_DEV = 8
RAY_TILE = 128
RT = 8
LINES = ALT * EPOCHS * LON_DEV

LATERAL = 1.0
VERTICAL = 4.0
TEMPORAL = 0.5
CENTRE = 2.0 * (2.0 * LATERAL + VERTICAL + TEMPORAL)


def gather_rays(block, join_last=True):
    count = lax.axis_size("ray")
    if count & (count - 1):
        return lax.all_gather(block, "ray", tiled=True)
    step = count // 2
    while step:
        other = lax.ppermute(block, "ray", [(i, i ^ step) for i in range(count)])
        block = jnp.concatenate([block, other], axis=0)
        step //= 2
    return block


def ray_sum(value):
    count = lax.axis_size("ray")
    if count & (count - 1):
        return lax.psum(value, "ray")
    step = count // 2
    while step:
        value = value + lax.ppermute(value, "ray", [(i, i ^ step) for i in range(count)])
        step //= 2
    return value


def vox_sum(value):
    count = lax.axis_size("vox")
    if count == 1:
        return value
    if count == 2:
        return value + lax.ppermute(value, "vox", [(0, 1), (1, 0)])
    return lax.psum(value, "vox")


def halo_of(low_edge, high_edge):
    count = lax.axis_size("vox")
    if count == 1:
        return jnp.zeros_like(high_edge), jnp.zeros_like(low_edge)
    if count == 2:
        first = lax.axis_index("vox") == 0
        other = lax.ppermute(jnp.where(first, high_edge, low_edge), "vox", [(0, 1), (1, 0)])
        none = jnp.zeros_like(other)
        return jnp.where(first, none, other), jnp.where(first, other, none)
    forward = [(i, i + 1) for i in range(count - 1)]
    backward = [(target, source) for source, target in forward]
    return lax.ppermute(high_edge, "vox", forward), lax.ppermute(low_edge, "vox", backward)


def laplace(field):
    inner = field[:, :, 1:-1]
    padded = jnp.pad(field, ((1, 1), (1, 1), (0, 0), (1, 1)))
    lateral = padded[1:-1, 1:-1, 2:, 1:-1] + padded[1:-1, 1:-1, :-2, 1:-1]
    lateral = lateral + padded[1:-1, 1:-1, 1:-1, 2:] + padded[1:-1, 1:-1, 1:-1, :-2]
    vertical = padded[2:, 1:-1, 1:-1, 1:-1] + padded[:-2, 1:-1, 1:-1, 1:-1]
    temporal = padded[1:-1, 2:, 1:-1, 1:-1] + padded[1:-1, :-2, 1:-1, 1:-1]
    return CENTRE * inner - LATERAL * lateral - VERTICAL * vertical - TEMPORAL * temporal


def on_device(
    tiles,
    tile_scale,
    tile_row,
    tile_col,
    tile_count,
    delays,
    ray_receiver,
    receiver_weight,
    smooth_scale,
):
    block = tiles[0, 0]
    row_index = tile_row[0, 0]
    col_index = tile_col[0, 0]
    slots = block.shape[0]
    rays_n = lax.axis_size("ray")
    live = (jnp.arange(slots) < tile_count[0, 0]).astype(jnp.float32)
    effective = tile_scale[0, 0] * live
    table_size = receiver_weight.shape[0]
    matches = ray_receiver[:, None] == jnp.arange(table_size)[None, :]
    ray_weight = jnp.sum(jnp.where(matches, receiver_weight[None, :], 0.0), axis=1)
    ray_weight = ray_weight.reshape(RT, RAY_TILE)
    damping = smooth_scale[:, None, None, None]
    share_rows = ALT // rays_n
    offset = lax.axis_index("ray") * share_rows
    ray_onehot = (row_index[None, :] == jnp.arange(RT)[:, None]).astype(jnp.float32)
    vox_n = lax.axis_size("vox")
    vox_at = lax.axis_index("vox")
    places = jnp.arange(LON_DEV + 2)[None, None, :, None]
    inside = ((places > 0) | (vox_at > 0)) & ((places < LON_DEV + 1) | (vox_at < vox_n - 1))

    def adjoint_lines(weighted):
        picked = jnp.take(weighted.astype(jnp.bfloat16), row_index, axis=0)
        return (
            jnp.einsum("ktl,kt->kl", block, picked, preferred_element_type=jnp.float32)
            * effective[:, None]
        )

    def forward_share(field):
        lines = jnp.take(field.reshape(LINES, LAT), col_index, axis=0).astype(jnp.bfloat16)
        rays = (
            jnp.einsum("ktl,kl->kt", block, lines, preferred_element_type=jnp.float32)
            * effective[:, None]
        )
        return jnp.dot(ray_onehot, rays, precision=lax.Precision.HIGHEST)

    def row_of(value):
        return jnp.full((1, LAT), value, jnp.float32)

    def scatter(lines, onehot):
        high = lines.astype(jnp.bfloat16)
        low = (lines - high.astype(jnp.float32)).astype(jnp.bfloat16)
        both = jnp.dot(
            onehot, jnp.concatenate([high, low], axis=1), preferred_element_type=jnp.float32
        )
        return (both[:, :LAT] + both[:, LAT:]).reshape(ALT, EPOCHS, LON_DEV, LAT)

    u0 = ray_weight * delays.reshape(RT, RAY_TILE)
    contrib = adjoint_lines(ray_weight * u0)
    names = jnp.pad(col_index.astype(jnp.float32), (0, LAT - slots))[None, :]
    extra = jnp.concatenate([names, row_of(jnp.sum(u0 * u0)), jnp.zeros((6, LAT))], axis=0)
    seen = gather_rays(jnp.concatenate([contrib, extra], axis=0)).reshape(rays_n, slots + 8, LAT)
    cols = seen[:, slots, :slots].astype(jnp.int32).reshape(1, rays_n * slots)
    onehot = (cols == jnp.arange(LINES)[:, None]).astype(jnp.bfloat16)
    left_sq = jnp.sum(seen[:, slots + 1, 0])
    v0 = scatter(seen[:, :slots].reshape(rays_n * slots, LAT), onehot)

    share = forward_share(v0)
    summed = vox_sum(jnp.concatenate([share, jnp.full((8, LAT), jnp.sum(v0 * v0))], axis=0))
    v0_norm = jnp.sqrt(summed[8, 0])
    left0 = jnp.sqrt(left_sq)
    right0 = v0_norm / left0
    v0 = v0 / v0_norm
    r1 = ray_weight * summed[:8] / v0_norm - (right0 / left0) * u0
    contrib1 = adjoint_lines(ray_weight * r1)
    extra1 = jnp.concatenate([row_of(jnp.sum(r1 * r1)), jnp.zeros((7, LAT))], axis=0)
    low2, high2 = halo_of(v0[:, :, :2], v0[:, :, -2:])
    wide = jnp.concatenate([low2, v0, high2], axis=2)
    s1 = jnp.where(inside, damping * laplace(wide), 0.0)
    s1_sq = vox_sum(jnp.full((8, LAT), jnp.sum(s1[:, :, 1:-1] * s1[:, :, 1:-1])))[0, 0]
    smoothing = laplace(damping * s1)
    seen1 = gather_rays(jnp.concatenate([contrib1, extra1], axis=0))
    seen1 = seen1.reshape(rays_n, slots + 8, LAT)
    left1_sq = jnp.sum(seen1[:, slots, 0]) + s1_sq
    left1 = jnp.sqrt(left1_sq)
    pulled = scatter(seen1[:, :slots].reshape(rays_n * slots, LAT), onehot)
    v1 = (pulled + smoothing) / left1 - left1 * v0

    share1 = forward_share(v1)
    summed1 = vox_sum(jnp.concatenate([share1, jnp.full((8, LAT), jnp.sum(v1 * v1))], axis=0))
    right1 = jnp.sqrt(summed1[8, 0])
    low1, high1 = halo_of(v1[:, :, :1], v1[:, :, -1:])
    s2 = damping * laplace(jnp.concatenate([low1, v1, high1], axis=2)) / right1
    s2 = s2 - (right1 / left1) * s1[:, :, 1:-1]
    r2 = ray_weight * summed1[:8] / right1 - (right1 / left1) * r1
    s2_sq = vox_sum(jnp.full((8, LAT), jnp.sum(s2 * s2)))[0, 0]
    left2_sq = ray_sum(jnp.full((8, LAT), jnp.sum(r2 * r2)))[0, 0] + s2_sq
    left2 = jnp.sqrt(left2_sq)

    diag0 = right0
    diag1 = jnp.sqrt(diag0 * diag0 + left1_sq)
    cosine1, sine1 = diag0 / diag1, left1 / diag1
    coupling1 = sine1 * right1
    diag_bar = -cosine1 * right1
    step1 = cosine1 * left0
    resid1 = sine1 * left0
    diag2 = jnp.sqrt(diag_bar * diag_bar + left2_sq)
    step2 = diag_bar / diag2 * resid1
    mine0 = lax.dynamic_slice_in_dim(v0, offset, share_rows, 0)
    mine1 = lax.dynamic_slice_in_dim(v1, offset, share_rows, 0) / right1
    density = step1 / diag1 * mine0 + step2 / diag2 * (mine1 - coupling1 / diag1 * mine0)
    return (density, (r2 / left2).reshape(-1))


def solution(mesh):
    in_specs = (
        P("ray", "vox", None, None, None),
        P("ray", "vox", None),
        P("ray", "vox", None),
        P("ray", "vox", None),
        P("ray", "vox"),
        P("ray"),
        P("ray"),
        P("ray"),
        P(),
    )
    out_specs = (P("ray", None, "vox", None), P("ray"))
    return jax.shard_map(
        on_device, mesh=mesh, in_specs=in_specs, out_specs=out_specs, check_vma=False
    )
```

```python
import functools

import jax
import jax.numpy as jnp
from jax import lax
from jax.experimental import pallas as pl
from jax.experimental.pallas import tpu as pltpu
from jax.sharding import PartitionSpec as P

ALT = 64
EPOCHS = 2
LAT = 128
LON_DEV = 8
RAY_TILE = 128
RT = 8
PAIRS = ALT * EPOCHS
LINES = PAIRS * LON_DEV
PAD = EPOCHS
UNROLL = 8

LATERAL = 1.0
VERTICAL = 4.0
TEMPORAL = 0.5
CENTRE = 2.0 * (2.0 * LATERAL + VERTICAL + TEMPORAL)

F32 = jnp.float32
BF16 = jnp.bfloat16
VM = pl.BlockSpec(memory_space=pltpu.VMEM)
SM = pl.BlockSpec(memory_space=pltpu.SMEM)


def local_call(body, name, in_specs, out_shapes, scratch=()):
    return pl.pallas_call(
        body,
        name=name,
        in_specs=in_specs,
        out_specs=[VM] * len(out_shapes),
        out_shape=[jax.ShapeDtypeStruct(shape, dtype) for shape, dtype in out_shapes],
        scratch_shapes=list(scratch),
        compiler_params=pltpu.CompilerParams(vmem_limit_bytes=32 << 20),
    )


def pairs_of(count, step):
    return [(i, i ^ step) for i in range(count)]


def hops(count):
    steps = []
    while count > 1:
        count //= 2
        steps.append(count)
    return steps


def gather_rays(block, during=()):
    count = lax.axis_size("ray")
    done, given = list(during), None
    if count & (count - 1) or count == 1:
        whole = lax.all_gather(block, "ray", tiled=True)
        half = whole.shape[0] // 2
        block, other = whole[:half], whole[half:]
    else:
        for step in hops(count):
            other = lax.ppermute(block, "ray", pairs_of(count, step))
            if step == 1:
                break
            joined = jnp.concatenate([block, other], axis=0)
            if done:
                given = done.pop(0)(given)
                joined, given = lax.optimization_barrier((joined, given))
            block = joined
    while done:
        given = done.pop(0)(given)
    return block, other, given


def vox_others(value):
    count = lax.axis_size("vox")
    if count == 1:
        return jnp.zeros_like(value)
    if count == 2:
        return lax.ppermute(value, "vox", [(0, 1), (1, 0)])
    return lax.psum(value, "vox") - value


def last_sums(value, step_of):
    count, slabs = lax.axis_size("ray"), lax.axis_size("vox")
    if slabs != 2 or count & (count - 1) or count < 8:
        mine = step_of(None)
        return lax.psum(value, "ray"), mine, vox_others(mine)
    for step in hops(count)[:-2]:
        value = value + lax.ppermute(value, "ray", pairs_of(count, step))
        if step == count // 2:
            mine = step_of(None)
            value, mine = lax.optimization_barrier((value, mine))
    both = jnp.concatenate([value, mine], axis=0)
    both = lax.ppermute(both, ("ray", "vox"), [(i, i ^ 5) for i in range(2 * count)])
    value = value + both[:8]
    return value, lax.ppermute(value, "ray", pairs_of(count, 1)), mine, both[8:]


def halo_of(low_edge, high_edge):
    count = lax.axis_size("vox")
    if count == 1:
        return jnp.zeros_like(high_edge), jnp.zeros_like(low_edge)
    forward = [(i, i + 1) for i in range(count - 1)]
    backward = [(target, source) for source, target in forward]
    return lax.ppermute(high_edge, "vox", forward), lax.ppermute(low_edge, "vox", backward)


def first_halo(sums, field):
    if lax.axis_size("vox") == 2 and lax.axis_size("ray") % 2 == 0:
        other = lax.ppermute(sums, "vox", [(0, 1), (1, 0)])
        column = other[RT + 8 :]
        partner = lax.ppermute(column, "ray", pairs_of(lax.axis_size("ray"), 1))
        return other, (column, partner, column, partner), True
    low = halo_of(field[PAD:-PAD, 0], field[PAD:-PAD, -1])
    far = halo_of(field[PAD:-PAD, 1], field[PAD:-PAD, -2])
    return vox_others(sums), (low[0], far[0], low[1], far[1]), False


def next_halo(sums, field):
    if lax.axis_size("vox") == 2:
        other = lax.ppermute(sums, "vox", [(0, 1), (1, 0)])
        column = other[RT + 8 :]
        return other, (column, column)
    return vox_others(sums), halo_of(field[PAD:-PAD, 0], field[PAD:-PAD, -1])


def total(values):
    return jnp.sum(values, axis=(0, 1), keepdims=True)


def sub_iota(shape=(8, LAT)):
    return lax.broadcasted_iota(jnp.int32, shape, 0)


def lane_iota(shape=(8, LAT)):
    return lax.broadcasted_iota(jnp.int32, shape, 1)


def pull_lines(weighted, tiles_ref, pick_ref, out_ref, slots):
    rays = weighted.astype(BF16)
    for k in range(slots):
        product = jnp.dot(rays, tiles_ref[k], preferred_element_type=F32)
        out_ref[pl.ds(k, 1), :] = jnp.sum(pick_ref[k] * product, axis=0, keepdims=True)


def push_lines(lines, tiles_ref, pick_ref, slots):
    rays = jnp.zeros((RT, RAY_TILE), F32)
    for k in range(slots):
        line = jnp.broadcast_to(lines[k : k + 1], (RT, LAT)).astype(BF16)
        product = lax.dot_general(
            line, tiles_ref[k], (((1,), (1,)), ((), ())), preferred_element_type=F32
        )
        rays = rays + pick_ref[k] * product
    return rays


def both_parts(lines):
    high = lines.astype(BF16)
    low = (lines - high.astype(F32)).astype(BF16)
    return jnp.concatenate([high, low], axis=1)


def across(values, sub, lane):
    up = jnp.where(lane == 0, 0.0, pltpu.roll(values, 1, 1))
    down = jnp.where(lane == LAT - 1, 0.0, pltpu.roll(values, LAT - 1, 1))
    return up + down


def column_stencil(column, beside, lane, sub):
    up = jnp.where(sub < EPOCHS, 0.0, pltpu.roll(column, EPOCHS, 0))
    down = jnp.where(sub >= PAIRS - EPOCHS, 0.0, pltpu.roll(column, PAIRS - EPOCHS, 0))
    later = pltpu.roll(column, PAIRS - 1, 0)
    earlier = pltpu.roll(column, 1, 0)
    epoch = jnp.where(sub % EPOCHS == 0, later, earlier)
    return (
        CENTRE * column
        - LATERAL * (beside + across(column, sub, lane))
        - VERTICAL * (up + down)
        - TEMPORAL * epoch
    )


def slab_stencil(pair, field_ref, low_ref, high_ref, sub, lane):
    here = field_ref[pair + PAD]
    below = jnp.where(sub == 0, low_ref[pl.ds(pair, 1), :], pltpu.roll(here, 1, 0))
    above = jnp.where(sub == LON_DEV - 1, high_ref[pl.ds(pair, 1), :], pltpu.roll(here, LON_DEV - 1, 0))
    epoch = field_ref[(pair ^ 1) + PAD]
    return (
        CENTRE * here
        - LATERAL * (below + above + across(here, sub, lane))
        - VERTICAL * (field_ref[pair] + field_ref[pair + 2 * PAD])
        - TEMPORAL * epoch
    )


def start_body(slots, row_ref, col_ref, scale_ref, count_ref, table_ref, receiver_ref, delays_ref, tiles_ref,
               packet_ref, weight_ref, start_ref, pick_ref, own_ref):
    sub, lane = sub_iota(), lane_iota()
    receivers = receiver_ref[...]
    weight = jnp.zeros((RT, RAY_TILE), F32)
    for j in range(table_ref.shape[0]):
        weight = jnp.where(receivers == j, table_ref[j], weight)
    weight_ref[...] = weight
    start = weight * delays_ref[...]
    start_ref[...] = start
    names = jnp.zeros((8, LAT), jnp.int32)
    for k in range(slots):
        live = jnp.where(k < count_ref[0], scale_ref[k], 0.0)
        pick_ref[k] = jnp.where(sub == row_ref[k], live, 0.0)
        own_ref[pl.ds(k, 1), :] = jnp.full((1, LAT), col_ref[k], jnp.int32)
        names = jnp.where(lane == k, col_ref[k], names)
    pull_lines(weight * start, tiles_ref, pick_ref, packet_ref, slots)
    square = total(start * start)
    packet_ref[slots:, :] = jnp.where(
        sub == 0, names.astype(F32), jnp.where(sub == 1, square, 0.0)
    )


def names_of(ref, slots):
    blocks = ref.shape[0] // (slots + 8)
    per = LAT // slots
    pieces = []
    for first in range(0, blocks, per):
        row = ref[pl.ds(first * (slots + 8) + slots, 1), :]
        for j in range(1, min(per, blocks - first)):
            row = row + pltpu.roll(ref[pl.ds((first + j) * (slots + 8) + slots, 1), :], j * slots, 1)
        if blocks - first < per:
            row = jnp.where(lane_iota((1, LAT)) < (blocks - first) * slots, row, -1.0)
        pieces.append(row.astype(jnp.int32))
    return pieces


def lines_in(ref, slots):
    blocks = ref.shape[0] // (slots + 8)
    return [ref[b * (slots + 8) : b * (slots + 8) + slots, :] for b in range(blocks)]


def padded_lines(ref_a, ref_b, slots):
    per = LAT // slots
    rows = []
    for ref in (ref_a, ref_b):
        lines = lines_in(ref, slots)
        rows += lines
        if len(lines) % per:
            rows.append(jnp.zeros(((per - len(lines) % per) * slots, LAT), F32))
    return jnp.concatenate(rows, axis=0)


def rows_sum(ref, slots, at):
    blocks = ref.shape[0] // (slots + 8)
    out = ref[pl.ds(slots + at, 1), :]
    for b in range(1, blocks):
        out = out + ref[pl.ds(b * (slots + 8) + slots + at, 1), :]
    return out


CHUNK = 128


def onehot_of(names, ids):
    return jnp.concatenate(
        [jnp.where(ids == piece, 1.0, 0.0).astype(BF16) for piece in names], axis=1
    )


def edge_of(field_ref, at):
    return field_ref[PAD : PAIRS + PAD, at, :]


def first_body(slots, mine_ref, other_ref, own_ref, pick_ref, tiles_ref,
               field_ref, lines_ref, out_ref, left_ref, names_ref):
    names = names_of(mine_ref, slots) + names_of(other_ref, slots)
    for j, piece in enumerate(names):
        names_ref[pl.ds(j, 1), :] = piece
    parts = both_parts(padded_lines(mine_ref, other_ref, slots))

    def take(ids):
        found = jnp.dot(onehot_of(names, ids), parts, preferred_element_type=F32)
        return found[:, :LAT] + found[:, LAT:]

    lines = take(own_ref[...])
    lines_ref[...] = lines
    rays = push_lines(lines, tiles_ref, pick_ref, slots)
    zeros = jnp.zeros((PAD, LON_DEV, LAT), F32)
    field_ref[:PAD] = zeros
    field_ref[PAIRS + PAD :] = zeros
    square = jnp.zeros((8, LAT), F32)
    for first in range(0, LINES, CHUNK):
        piece = take(sub_iota((CHUNK, LAT)) + first).reshape(CHUNK // LON_DEV, LON_DEV, LAT)
        at = first // LON_DEV + PAD
        field_ref[at : at + CHUNK // LON_DEV] = piece
        square = square + jnp.sum(piece * piece, axis=0)
    out_ref[:RT, :] = rays
    out_ref[RT : RT + 8, :] = jnp.broadcast_to(total(square), (8, LAT))
    odd = lax.axis_index("ray") % 2 == 1
    high = jnp.where(odd, edge_of(field_ref, LON_DEV - 2), edge_of(field_ref, LON_DEV - 1))
    low = jnp.where(odd, edge_of(field_ref, 1), edge_of(field_ref, 0))
    out_ref[RT + 8 :, :] = jnp.where(lax.axis_index("vox") == 0, high, low)
    left_ref[...] = jnp.broadcast_to(rows_sum(mine_ref, slots, 1) + rows_sum(other_ref, slots, 1), (8, LAT))


def second_body(slots, mine_ref, other_ref, left_ref, weight_ref, start_ref, pick_ref, tiles_ref,
                packet_ref, rays_ref, image_ref, norm_ref):
    sub = sub_iota()
    left_sq = left_ref[...]
    norm_sq = mine_ref[RT : RT + 8, :] + other_ref[RT : RT + 8, :]
    inverse = lax.rsqrt(norm_sq)
    norm = norm_sq * inverse
    weight = weight_ref[...]
    image = (mine_ref[:RT, :] + other_ref[:RT, :]) * inverse
    image_ref[...] = image
    rays = weight * image - norm / left_sq * start_ref[...]
    rays_ref[...] = rays
    norm_ref[...] = norm
    pull_lines(weight * rays, tiles_ref, pick_ref, packet_ref, slots)
    packet_ref[slots:, :] = jnp.where(sub == 0, total(rays * rays), 0.0)


def flags():
    at, count = lax.axis_index("vox"), lax.axis_size("vox")
    return (at > 0).astype(F32), (at < count - 1).astype(F32)


def smooth_body(swapped, field_ref, low_ref, low2_ref, high_ref, high2_ref, damp_ref, norm_ref,
                smooth_ref, scaled_ref, far_ref, square_ref, near_ref):
    sub, lane = sub_iota(), lane_iota()
    has_low, has_high = flags()
    inverse = 1.0 / norm_ref[...]
    col_lane, col_sub = lane_iota((PAIRS, LAT)), sub_iota((PAIRS, LAT))
    low, low2, high, high2 = low_ref[...], low2_ref[...], high_ref[...], high2_ref[...]
    if swapped:
        odd = lax.axis_index("ray") % 2 == 1
        low, low2 = jnp.where(odd, low2, low), jnp.where(odd, low, low2)
        high, high2 = low, low2
    near_ref[0] = low * has_low
    near_ref[1] = high * has_high
    scale = damp_ref[...] * damp_ref[...] * jnp.broadcast_to(inverse[:1], (PAIRS, LAT))
    far_ref[0] = scale * has_low * column_stencil(low, low2 + edge_of(field_ref, 0), col_lane, col_sub)
    far_ref[1] = scale * has_high * column_stencil(
        high, high2 + edge_of(field_ref, LON_DEV - 1), col_lane, col_sub
    )
    zeros = jnp.zeros((PAD, LON_DEV, LAT), F32)
    scaled_ref[:PAD] = zeros
    scaled_ref[PAIRS + PAD :] = zeros

    def left(pair, square):
        damped = damp_ref[pl.ds(pair, 1), :]
        value = slab_stencil(pair, field_ref, near_ref.at[0], near_ref.at[1], sub, lane) * inverse * damped
        smooth_ref[pair] = value
        scaled_ref[pair + PAD] = value * damped
        return square + value * value

    square = lax.fori_loop(0, PAIRS, left, jnp.zeros((LON_DEV, LAT), F32), unroll=UNROLL)
    square_ref[...] = jnp.broadcast_to(total(square), (8, LAT))


def onehot_body(names_ref, onehot_ref):
    pieces = [names_ref[pl.ds(j, 1), :] for j in range(onehot_ref.shape[1] // LAT)]
    for first in range(0, LINES, CHUNK):
        onehot_ref[first : first + CHUNK, :] = onehot_of(pieces, sub_iota((CHUNK, LAT)) + first)


def again_body(slots, col_ref, scaled_ref, far_ref, again_ref, lines_ref):
    sub, lane = sub_iota(), lane_iota()

    def right(pair, carry):
        again_ref[pair] = slab_stencil(pair, scaled_ref, far_ref.at[0], far_ref.at[1], sub, lane)
        return carry

    lax.fori_loop(0, PAIRS, right, 0, unroll=UNROLL)
    for k in range(slots):
        col = col_ref[k]
        lines_ref[pl.ds(k, 1), :] = again_ref[col // LON_DEV, pl.ds(col % LON_DEV, 1), :]


def third_body(slots, mine_ref, other_ref, square_ref, onehot_ref, names_ref, own_ref, lines_ref,
               again_lines_ref, again_ref, field_ref, norm_ref, pick_ref, tiles_ref,
               next_ref, out_ref, shift_ref):
    shift = jnp.broadcast_to(rows_sum(mine_ref, slots, 0) + rows_sum(other_ref, slots, 0), (8, LAT))
    shift_ref[...] = shift
    inverse = 1.0 / norm_ref[...]
    back = shift * inverse
    parts = both_parts(padded_lines(mine_ref, other_ref, slots))
    names = [names_ref[pl.ds(j, 1), :] for j in range(onehot_ref.shape[1] // LAT)]

    def take(onehot):
        found = jnp.dot(onehot, parts, preferred_element_type=F32)
        return found[:, :LAT] + found[:, LAT:]

    lines = take(onehot_of(names, own_ref[...])) + again_lines_ref[...] - lines_ref[...] * back[:1]
    rays = push_lines(lines, tiles_ref, pick_ref, slots)
    zeros = jnp.zeros((PAD, LON_DEV, LAT), F32)
    next_ref[:PAD] = zeros
    next_ref[PAIRS + PAD :] = zeros
    square = jnp.zeros((8, LAT), F32)
    cross = jnp.zeros((8, LAT), F32)
    for first in range(0, LINES, CHUNK):
        count, pair = CHUNK // LON_DEV, first // LON_DEV
        piece = take(onehot_ref[first : first + CHUNK, :]).reshape(count, LON_DEV, LAT)
        base = field_ref[pair + PAD : pair + PAD + count]
        piece = piece + again_ref[pair : pair + count] - base * back
        next_ref[pair + PAD : pair + PAD + count] = piece
        square = square + jnp.sum(piece * piece, axis=0)
        cross = cross + jnp.sum(piece * base, axis=0)
    sub = sub_iota()
    out_ref[:RT, :] = rays
    out_ref[RT : RT + 8, :] = jnp.where(
        sub == 0, total(square), jnp.where(sub == 1, total(cross) * inverse, square_ref[...])
    )
    out_ref[RT + 8 :, :] = jnp.where(
        lax.axis_index("vox") == 0, edge_of(next_ref, LON_DEV - 1), edge_of(next_ref, 0)
    )


def fourth_body(mine_ref, other_ref, shift_ref, weight_ref, rays_ref, image_ref,
                next_rays_ref, left_ref, rest_ref, norm_ref, sum_ref):
    sums = mine_ref[RT : RT + 8, :] + other_ref[RT : RT + 8, :]
    square, cross, rest = [jnp.broadcast_to(sums[j : j + 1], (8, LAT)) for j in range(3)]
    left_sq = shift_ref[...] + rest
    norm_sq = (square - 2.0 * rest * cross + rest * rest) / left_sq
    per_left = lax.rsqrt(left_sq)
    inverse = lax.rsqrt(norm_sq)
    norm = norm_sq * inverse
    rays = mine_ref[:RT, :] + other_ref[:RT, :] - rest * image_ref[...]
    rays = weight_ref[...] * rays * (per_left * inverse) - norm * per_left * rays_ref[...]
    next_rays_ref[...] = rays
    left_ref[...] = left_sq
    rest_ref[...] = rest
    norm_ref[...] = norm
    sum_ref[...] = jnp.broadcast_to(total(rays * rays), (8, LAT))


def last_smooth_body(next_ref, low_ref, high_ref, damp_ref, smooth_ref, norm_ref, left_ref, rest_ref,
                     square_ref, near_ref):
    sub, lane = sub_iota(), lane_iota()
    has_low, has_high = flags()
    near_ref[0] = low_ref[...] * has_low
    near_ref[1] = high_ref[...] * has_high
    norm, per_left = norm_ref[...], lax.rsqrt(left_ref[...])
    inverse = per_left / norm
    back = rest_ref[...] * inverse + norm * per_left

    def left(pair, square):
        damped = damp_ref[pl.ds(pair, 1), :]
        value = slab_stencil(pair, next_ref, near_ref.at[0], near_ref.at[1], sub, lane) * inverse * damped
        value = value - back * smooth_ref[pair]
        return square + value * value

    square = lax.fori_loop(0, PAIRS, left, jnp.zeros((LON_DEV, LAT), F32), unroll=UNROLL)
    square_ref[...] = jnp.broadcast_to(total(square), (8, LAT))


def end_body(share, parts, *refs):
    sums = refs[0][...]
    for ref in refs[1:parts]:
        sums = sums + ref[...]
    (left0_ref, norm0_ref, left1_ref, rest_ref, norm1_ref, rays_ref, field_ref, next_ref,
     density_ref, out_ref) = refs[parts:]
    left2_sq = sums
    out_ref[...] = rays_ref[...] * lax.rsqrt(left2_sq)
    left0_sq, norm0, left1_sq, right1 = left0_ref[...], norm0_ref[...], left1_ref[...], norm1_ref[...]
    left0, left1 = jnp.sqrt(left0_sq), jnp.sqrt(left1_sq)
    right0 = norm0 / left0
    diag1 = jnp.sqrt(right0 * right0 + left1_sq)
    cosine, sine = right0 / diag1, left1 / diag1
    coupling = sine * right1
    diag_bar = -cosine * right1
    step1, resid = cosine * left0, sine * left0
    diag2 = jnp.sqrt(diag_bar * diag_bar + left2_sq)
    step2 = diag_bar / diag2 * resid
    on_next = step2 / diag2 / (left1 * right1)
    on_first = (step1 / diag1 - step2 / diag2 * coupling / diag1 - on_next * rest_ref[...]) / norm0
    first = lax.axis_index("ray") * share + PAD
    for j in range(share):
        density_ref[j] = on_first * field_ref[first + j] + on_next * next_ref[first + j]


def on_device(
    tiles,
    tile_scale,
    tile_row,
    tile_col,
    tile_count,
    delays,
    ray_receiver,
    receiver_weight,
    smooth_scale,
):
    block = tiles[0, 0]
    slots = block.shape[0]
    rays_n = lax.axis_size("ray")
    col_index = tile_col[0, 0]
    held = (RT, RAY_TILE)
    row = ((8, LAT), F32)
    slab = ((PAIRS, LON_DEV, LAT), F32)
    padded = ((PAIRS + 2 * PAD, LON_DEV, LAT), F32)
    packet = ((slots + 8, LAT), F32)
    damp = jnp.broadcast_to(jnp.repeat(smooth_scale, EPOCHS)[:, None], (PAIRS, LAT))

    mine, weight, start, pick, own = local_call(
        functools.partial(start_body, slots), "start", [SM] * 5 + [VM] * 3,
        [packet, (held, F32), (held, F32), ((slots, RT, LAT), F32), ((slots, LAT), jnp.int32)],
    )(tile_row[0, 0], col_index, tile_scale[0, 0], tile_count[0], receiver_weight,
      ray_receiver.reshape(held), delays.reshape(held), block)
    near, far, damp = gather_rays(mine, (lambda _: damp,))
    per = LAT // slots
    names_n = 2 * -(-(near.shape[0] // (slots + 8)) // per)

    field, lines, sums, left0, names = local_call(
        functools.partial(first_body, slots), "first", [VM] * 5,
        [padded, ((slots, LAT), F32), ((RT + 8 + PAIRS, LAT), F32), row, ((names_n, LAT), jnp.int32)],
    )(near, far, own, pick, block)
    others, columns, swapped = first_halo(sums, field)
    onehot = local_call(onehot_body, "onehot", [VM], [((LINES, names_n * LAT), BF16)])(names)[0]
    others, onehot = lax.optimization_barrier((others, onehot))

    mine, rays, image, norm0 = local_call(
        functools.partial(second_body, slots), "second", [VM] * 7, [packet, (held, F32), (held, F32), row],
    )(sums, others, left0, weight, start, pick, block)
    def smooth_step(columns):
        return local_call(
            functools.partial(smooth_body, swapped), "smooth", [VM] * 7,
            [slab, padded, ((2, PAIRS, LAT), F32), row], [pltpu.VMEM((2, PAIRS, LAT), F32)],
        )(field, *columns, damp, norm0)

    def again_step(given):
        smooth, scaled, beside, square = given
        again, again_lines = local_call(
            functools.partial(again_body, slots), "again", [SM] + [VM] * 2, [slab, ((slots, LAT), F32)],
        )(col_index, scaled, beside)
        return smooth, square, again, again_lines

    near, far, given = gather_rays(mine, (lambda _: columns, smooth_step, again_step))
    smooth, square, again, again_lines = given

    following, sums, shift = local_call(
        functools.partial(third_body, slots), "third", [VM] * 13,
        [padded, ((RT + 8 + PAIRS, LAT), F32), row],
    )(near, far, square, onehot, names, own, lines, again_lines, again, field, norm0, pick, block)
    others, beside = next_halo(sums, following)
    last_rays, left1, rest, norm1, ray_square = local_call(
        fourth_body, "fourth", [VM] * 6, [(held, F32), row, row, row, row],
    )(sums, others, shift, weight, rays, image)

    def last_step(_):
        return local_call(
            last_smooth_body, "last_smooth", [VM] * 8, [row], [pltpu.VMEM((2, PAIRS, LAT), F32)],
        )(following, *beside, damp, smooth, norm1, left1, rest)[0]

    shares = last_sums(ray_square, last_step)

    share = PAIRS // rays_n
    density, rays_out = local_call(
        functools.partial(end_body, share, len(shares)), "end", [VM] * (len(shares) + 8),
        [((share, LON_DEV, LAT), F32), (held, F32)],
    )(*shares, left0, norm0, left1, rest, norm1, last_rays, field, following)
    return (density.reshape(ALT // rays_n, EPOCHS, LON_DEV, LAT), rays_out.reshape(-1))


def solution(mesh):
    in_specs = (
        P("ray", "vox", None, None, None),
        P("ray", "vox", None),
        P("ray", "vox", None),
        P("ray", "vox", None),
        P("ray", "vox"),
        P("ray"),
        P("ray"),
        P("ray"),
        P(),
    )
    out_specs = (P("ray", None, "vox", None), P("ray"))
    return jax.shard_map(
        on_device, mesh=mesh, in_specs=in_specs, out_specs=out_specs, check_vma=False
    )
```

```python
import functools

import jax
import jax.numpy as jnp
from jax import lax
from jax.experimental import pallas as pl
from jax.experimental.pallas import tpu as pltpu
from jax.sharding import PartitionSpec as P

ALT = 64
EPOCHS = 2
LAT = 128
LON_DEV = 8
RAY_TILE = 128
RT = 8
PAIRS = ALT * EPOCHS
LINES = PAIRS * LON_DEV
PAD = EPOCHS
UNROLL = 8

LATERAL = 1.0
VERTICAL = 4.0
TEMPORAL = 0.5
CENTRE = 2.0 * (2.0 * LATERAL + VERTICAL + TEMPORAL)

F32 = jnp.float32
BF16 = jnp.bfloat16
VM = pl.BlockSpec(memory_space=pltpu.VMEM)
SM = pl.BlockSpec(memory_space=pltpu.SMEM)


def local_call(body, name, in_specs, out_shapes, scratch=()):
    return pl.pallas_call(
        body,
        name=name,
        in_specs=in_specs,
        out_specs=[VM] * len(out_shapes),
        out_shape=[jax.ShapeDtypeStruct(shape, dtype) for shape, dtype in out_shapes],
        scratch_shapes=list(scratch),
        compiler_params=pltpu.CompilerParams(vmem_limit_bytes=32 << 20),
    )


def pairs_of(count, step):
    return [(i, i ^ step) for i in range(count)]


def hops(count):
    steps = []
    while count > 1:
        count //= 2
        steps.append(count)
    return steps


def gather_rays(block, during=()):
    count = lax.axis_size("ray")
    done, given = list(during), None
    if count & (count - 1) or count == 1:
        whole = lax.all_gather(block, "ray", tiled=True)
        half = whole.shape[0] // 2
        block, other = whole[:half], whole[half:]
    else:
        for step in hops(count):
            other = lax.ppermute(block, "ray", pairs_of(count, step))
            if step == 1:
                break
            joined = jnp.concatenate([block, other], axis=0)
            if done:
                given = done.pop(0)(given)
                joined, given = lax.optimization_barrier((joined, given))
            block = joined
    while done:
        given = done.pop(0)(given)
    return block, other, given


def vox_others(value):
    count = lax.axis_size("vox")
    if count == 1:
        return jnp.zeros_like(value)
    if count == 2:
        return lax.ppermute(value, "vox", [(0, 1), (1, 0)])
    return lax.psum(value, "vox") - value


def last_sums(value, given, step_of):
    count, slabs = lax.axis_size("ray"), lax.axis_size("vox")
    if slabs != 2 or count & (count - 1) or count < 16:
        mine = step_of(given)
        return lax.psum(value, "ray"), mine, vox_others(mine)
    for step in hops(count)[:-2]:
        value = value + lax.ppermute(value, "ray", pairs_of(count, step))
        if step == count // 4:
            given = step_of(given)
        value, given = lax.optimization_barrier((value, given))
    mine = given
    both = jnp.concatenate([value, mine], axis=0)
    both = lax.ppermute(both, ("ray", "vox"), [(i, i ^ 5) for i in range(2 * count)])
    value = value + both[:8]
    return value, lax.ppermute(value, "ray", pairs_of(count, 1)), mine, both[8:]


def halo_of(low_edge, high_edge):
    count = lax.axis_size("vox")
    if count == 1:
        return jnp.zeros_like(high_edge), jnp.zeros_like(low_edge)
    forward = [(i, i + 1) for i in range(count - 1)]
    backward = [(target, source) for source, target in forward]
    return lax.ppermute(high_edge, "vox", forward), lax.ppermute(low_edge, "vox", backward)


def first_halo(sums, field):
    if lax.axis_size("vox") == 2 and lax.axis_size("ray") % 2 == 0:
        other = lax.ppermute(sums, "vox", [(0, 1), (1, 0)])
        column = other[RT + 8 :]
        partner = lax.ppermute(column, "ray", pairs_of(lax.axis_size("ray"), 1))
        return other, (column, partner, column, partner), True
    low = halo_of(field[PAD:-PAD, 0], field[PAD:-PAD, -1])
    far = halo_of(field[PAD:-PAD, 1], field[PAD:-PAD, -2])
    return vox_others(sums), (low[0], far[0], low[1], far[1]), False


def next_halo(sums, field):
    if lax.axis_size("vox") == 2 and lax.axis_size("ray") % 2 == 0:
        other = lax.ppermute(sums, "vox", [(0, 1), (1, 0)])
        half = other[RT + 8 :]
        return other, (half, lax.ppermute(half, "ray", pairs_of(lax.axis_size("ray"), 1))), True
    return vox_others(sums), halo_of(field[PAD:-PAD, 0], field[PAD:-PAD, -1]), False


def total(values):
    return jnp.sum(values, axis=(0, 1), keepdims=True)


def sub_iota(shape=(8, LAT)):
    return lax.broadcasted_iota(jnp.int32, shape, 0)


def lane_iota(shape=(8, LAT)):
    return lax.broadcasted_iota(jnp.int32, shape, 1)


def pull_lines(weighted, tiles_ref, pick_ref, out_ref, slots):
    rays = weighted.astype(BF16)
    for k in range(slots):
        product = jnp.dot(rays, tiles_ref[k], preferred_element_type=F32)
        out_ref[pl.ds(k, 1), :] = jnp.sum(pick_ref[k] * product, axis=0, keepdims=True)


def push_lines(lines, tiles_ref, pick_ref, turned_ref, slots):
    lane = lane_iota((RAY_TILE, LAT))
    wide = jnp.concatenate([lines.astype(BF16), jnp.zeros((LAT - slots, LAT), BF16)], axis=0)
    turned = jnp.zeros((RAY_TILE, LAT), F32)
    for k in range(slots):
        product = lax.dot_general(
            tiles_ref[k], wide, (((1,), (1,)), ((), ())), preferred_element_type=F32
        )
        turned = jnp.where(lane == k, product, turned)
    turned_ref[...] = turned.T
    rays = jnp.zeros((RT, RAY_TILE), F32)
    for k in range(slots):
        rays = rays + pick_ref[k] * turned_ref[pl.ds(k, 1), :]
    return rays


def both_parts(lines):
    high = lines.astype(BF16)
    low = (lines - high.astype(F32)).astype(BF16)
    return jnp.concatenate([high, low], axis=1)


def across(values, sub, lane):
    up = jnp.where(lane == 0, 0.0, pltpu.roll(values, 1, 1))
    down = jnp.where(lane == LAT - 1, 0.0, pltpu.roll(values, LAT - 1, 1))
    return up + down


def column_stencil(column, beside, lane, sub):
    up = jnp.where(sub < EPOCHS, 0.0, pltpu.roll(column, EPOCHS, 0))
    down = jnp.where(sub >= PAIRS - EPOCHS, 0.0, pltpu.roll(column, PAIRS - EPOCHS, 0))
    later = pltpu.roll(column, PAIRS - 1, 0)
    earlier = pltpu.roll(column, 1, 0)
    epoch = jnp.where(sub % EPOCHS == 0, later, earlier)
    return (
        CENTRE * column
        - LATERAL * (beside + across(column, sub, lane))
        - VERTICAL * (up + down)
        - TEMPORAL * epoch
    )


def slab_stencil(pair, field_ref, low_ref, high_ref, sub, lane):
    here = field_ref[pair + PAD]
    below = jnp.where(sub == 0, low_ref[pl.ds(pair, 1), :], pltpu.roll(here, 1, 0))
    above = jnp.where(sub == LON_DEV - 1, high_ref[pl.ds(pair, 1), :], pltpu.roll(here, LON_DEV - 1, 0))
    epoch = field_ref[(pair ^ 1) + PAD]
    return (
        CENTRE * here
        - LATERAL * (below + above + across(here, sub, lane))
        - VERTICAL * (field_ref[pair] + field_ref[pair + 2 * PAD])
        - TEMPORAL * epoch
    )


PULLS = 1


def start_body(slots, count_ref, row_in, col_in, scale_in, table_in, receiver_in, delays_in, tiles_in,
               packet_ref, weight_ref, start_ref, pick_ref, own_ref, tiles_ref,
               row_ref, col_ref, scale_ref, table_ref, receiver_ref, delays_ref, sems):
    part = slots // PULLS
    copies = [
        pltpu.make_async_copy(source, target, sems.at[j])
        for j, (source, target) in enumerate([
            (receiver_in, receiver_ref), (table_in, table_ref), (delays_in, delays_ref),
            (scale_in, scale_ref), (row_in, row_ref), (col_in, col_ref),
        ])
    ]
    pulls = [
        pltpu.make_async_copy(
            tiles_in.at[pl.ds(j * part, part)], tiles_ref.at[pl.ds(j * part, part)], sems.at[6 + j]
        )
        for j in range(PULLS)
    ]
    for copy in copies + pulls:
        copy.start()
    for copy in copies:
        copy.wait()
    sub, lane = sub_iota(), lane_iota()
    receivers = receiver_ref[...]
    weight = jnp.zeros((RT, RAY_TILE), F32)
    for j in range(table_ref.shape[0]):
        weight = jnp.where(receivers == j, table_ref[j], weight)
    weight_ref[...] = weight
    start = weight * delays_ref[...]
    start_ref[...] = start
    names = jnp.zeros((8, LAT), jnp.int32)
    for k in range(slots):
        live = jnp.where(k < count_ref[0, 0], scale_ref[k], 0.0)
        pick_ref[k] = jnp.where(sub == row_ref[k], live, 0.0)
        own_ref[pl.ds(k, 1), :] = jnp.full((1, LAT), col_ref[k], jnp.int32)
        names = jnp.where(lane == k, col_ref[k], names)
    square = total(start * start)
    packet_ref[slots:, :] = jnp.where(
        sub == 0, names.astype(F32), jnp.where(sub == 1, square, 0.0)
    )
    rays = (weight * start).astype(BF16)
    for j in range(PULLS):
        pulls[j].wait()
        for k in range(j * part, (j + 1) * part):
            product = jnp.dot(rays, tiles_ref[k], preferred_element_type=F32)
            packet_ref[pl.ds(k, 1), :] = jnp.sum(pick_ref[k] * product, axis=0, keepdims=True)


def names_of(ref, slots):
    blocks = ref.shape[0] // (slots + 8)
    per = LAT // slots
    pieces = []
    for first in range(0, blocks, per):
        row = ref[pl.ds(first * (slots + 8) + slots, 1), :]
        for j in range(1, min(per, blocks - first)):
            row = row + pltpu.roll(ref[pl.ds((first + j) * (slots + 8) + slots, 1), :], j * slots, 1)
        if blocks - first < per:
            row = jnp.where(lane_iota((1, LAT)) < (blocks - first) * slots, row, -1.0)
        pieces.append(row.astype(jnp.int32))
    return pieces


def lines_in(ref, slots):
    blocks = ref.shape[0] // (slots + 8)
    return [ref[b * (slots + 8) : b * (slots + 8) + slots, :] for b in range(blocks)]


def padded_lines(ref, slots):
    per = LAT // slots
    rows = lines_in(ref, slots)
    if len(rows) % per:
        rows.append(jnp.zeros(((per - len(rows) % per) * slots, LAT), F32))
    return jnp.concatenate(rows, axis=0)


def found_lines(onehot, parts):
    found = jnp.dot(onehot, parts, preferred_element_type=F32)
    return found[:, :LAT] + found[:, LAT:]


def rows_sum(ref, slots, at):
    blocks = ref.shape[0] // (slots + 8)
    out = ref[pl.ds(slots + at, 1), :]
    for b in range(1, blocks):
        out = out + ref[pl.ds(b * (slots + 8) + slots + at, 1), :]
    return out


CHUNK = 128


def onehot_of(names, ids):
    return jnp.concatenate(
        [jnp.where(ids == piece, 1.0, 0.0).astype(BF16) for piece in names], axis=1
    )


def edge_of(field_ref, at):
    flat = field_ref.reshape((PAIRS + 2 * PAD) * LON_DEV, LAT)
    return flat[pl.ds(PAD * LON_DEV + at, PAIRS, stride=LON_DEV), :]


def first_half_body(slots, mine_ref, own_ref, field_ref, lines_ref, names_ref):
    names = names_of(mine_ref, slots)
    for j, piece in enumerate(names):
        names_ref[pl.ds(j, 1), :] = piece
    parts = both_parts(padded_lines(mine_ref, slots))
    lines_ref[...] = found_lines(onehot_of(names, own_ref[...]), parts)
    for first in range(0, LINES, CHUNK):
        onehot = onehot_of(names, sub_iota((CHUNK, LAT)) + first)
        piece = found_lines(onehot, parts).reshape(CHUNK // LON_DEV, LON_DEV, LAT)
        field_ref[first // LON_DEV : (first + CHUNK) // LON_DEV] = piece


def first_body(slots, other_ref, half_ref, half_lines_ref, mine_ref, own_ref, pick_ref, tiles_ref,
               field_ref, lines_ref, out_ref, left_ref, names_ref, turned_ref):
    names = names_of(other_ref, slots)
    for j, piece in enumerate(names):
        names_ref[pl.ds(j, 1), :] = piece
    parts = both_parts(padded_lines(other_ref, slots))
    lines = half_lines_ref[...] + found_lines(onehot_of(names, own_ref[...]), parts)
    lines_ref[...] = lines
    rays = push_lines(lines, tiles_ref, pick_ref, turned_ref, slots)
    zeros = jnp.zeros((PAD, LON_DEV, LAT), F32)
    field_ref[:PAD] = zeros
    field_ref[PAIRS + PAD :] = zeros
    square = jnp.zeros((8, LAT), F32)
    for first in range(0, LINES, CHUNK):
        onehot = onehot_of(names, sub_iota((CHUNK, LAT)) + first)
        count, pair = CHUNK // LON_DEV, first // LON_DEV
        piece = found_lines(onehot, parts).reshape(count, LON_DEV, LAT) + half_ref[pair : pair + count]
        field_ref[pair + PAD : pair + PAD + count] = piece
        square = square + jnp.sum(piece * piece, axis=0)
    out_ref[:RT, :] = rays
    out_ref[RT : RT + 8, :] = jnp.broadcast_to(total(square), (8, LAT))
    odd = lax.axis_index("ray") % 2
    at = jnp.where(lax.axis_index("vox") == 0, LON_DEV - 1 - odd, odd)
    out_ref[RT + 8 :, :] = edge_of(field_ref, at)
    left_ref[...] = jnp.broadcast_to(rows_sum(mine_ref, slots, 1) + rows_sum(other_ref, slots, 1), (8, LAT))


def second_body(slots, mine_ref, other_ref, left_ref, weight_ref, start_ref, pick_ref, tiles_ref,
                packet_ref, rays_ref, image_ref, norm_ref):
    sub = sub_iota()
    left_sq = left_ref[...]
    norm_sq = mine_ref[RT : RT + 8, :] + other_ref[RT : RT + 8, :]
    inverse = lax.rsqrt(norm_sq)
    norm = norm_sq * inverse
    weight = weight_ref[...]
    image = (mine_ref[:RT, :] + other_ref[:RT, :]) * inverse
    image_ref[...] = image
    rays = weight * image - norm / left_sq * start_ref[...]
    rays_ref[...] = rays
    norm_ref[...] = norm
    pull_lines(weight * rays, tiles_ref, pick_ref, packet_ref, slots)
    packet_ref[slots:, :] = jnp.where(sub == 0, total(rays * rays), 0.0)


def flags():
    at, count = lax.axis_index("vox"), lax.axis_size("vox")
    return (at > 0).astype(F32), (at < count - 1).astype(F32)


def smooth_body(swapped, field_ref, low_ref, low2_ref, high_ref, high2_ref, damp_ref, norm_ref,
                smooth_ref, scaled_ref, far_ref, square_ref, near_ref):
    sub, lane = sub_iota(), lane_iota()
    has_low, has_high = flags()
    inverse = 1.0 / norm_ref[...]
    col_lane, col_sub = lane_iota((PAIRS, LAT)), sub_iota((PAIRS, LAT))
    low, low2, high, high2 = low_ref[...], low2_ref[...], high_ref[...], high2_ref[...]
    if swapped:
        odd = lax.axis_index("ray") % 2 == 1
        low, low2 = jnp.where(odd, low2, low), jnp.where(odd, low, low2)
        high, high2 = low, low2
    near_ref[0] = low * has_low
    near_ref[1] = high * has_high
    scale = damp_ref[...] * damp_ref[...] * jnp.broadcast_to(inverse[:1], (PAIRS, LAT))
    far_ref[0] = scale * has_low * column_stencil(low, low2 + edge_of(field_ref, 0), col_lane, col_sub)
    far_ref[1] = scale * has_high * column_stencil(
        high, high2 + edge_of(field_ref, LON_DEV - 1), col_lane, col_sub
    )
    zeros = jnp.zeros((PAD, LON_DEV, LAT), F32)
    scaled_ref[:PAD] = zeros
    scaled_ref[PAIRS + PAD :] = zeros

    def left(pair, square):
        damped = damp_ref[pl.ds(pair, 1), :]
        value = slab_stencil(pair, field_ref, near_ref.at[0], near_ref.at[1], sub, lane) * inverse * damped
        smooth_ref[pair] = value
        scaled_ref[pair + PAD] = value * damped
        return square + value * value

    square = lax.fori_loop(0, PAIRS, left, jnp.zeros((LON_DEV, LAT), F32), unroll=UNROLL)
    square_ref[...] = jnp.broadcast_to(total(square), (8, LAT))


def onehot_body(*refs):
    names_refs, onehot_refs = refs[: len(refs) // 2], refs[len(refs) // 2 :]
    for names_ref, onehot_ref in zip(names_refs, onehot_refs):
        pieces = [names_ref[pl.ds(j, 1), :] for j in range(onehot_ref.shape[1] // LAT)]
        for first in range(0, LINES, CHUNK):
            onehot_ref[first : first + CHUNK, :] = onehot_of(pieces, sub_iota((CHUNK, LAT)) + first)


def again_body(slots, col_ref, scaled_ref, far_ref, again_ref, lines_ref):
    sub, lane = sub_iota(), lane_iota()

    def right(pair, carry):
        again_ref[pair] = slab_stencil(pair, scaled_ref, far_ref.at[0], far_ref.at[1], sub, lane)
        return carry

    lax.fori_loop(0, PAIRS, right, 0, unroll=UNROLL)
    for k in range(slots):
        col = col_ref[k]
        lines_ref[pl.ds(k, 1), :] = again_ref[col // LON_DEV, pl.ds(col % LON_DEV, 1), :]


def third_half_body(slots, mine_ref, onehot_ref, names_ref, own_ref, again_lines_ref, again_ref,
                    half_ref, lines_ref):
    parts = both_parts(padded_lines(mine_ref, slots))
    names = [names_ref[pl.ds(j, 1), :] for j in range(onehot_ref.shape[1] // LAT)]
    lines_ref[...] = found_lines(onehot_of(names, own_ref[...]), parts) + again_lines_ref[...]
    for first in range(0, LINES, CHUNK):
        count, pair = CHUNK // LON_DEV, first // LON_DEV
        piece = found_lines(onehot_ref[first : first + CHUNK, :], parts).reshape(count, LON_DEV, LAT)
        half_ref[pair : pair + count] = piece + again_ref[pair : pair + count]


def third_body(slots, other_ref, half_ref, half_lines_ref, mine_ref, square_ref, onehot_ref, names_ref, own_ref,
               lines_ref, field_ref, norm_ref, pick_ref, tiles_ref,
               next_ref, out_ref, shift_ref, turned_ref):
    shift = jnp.broadcast_to(rows_sum(mine_ref, slots, 0) + rows_sum(other_ref, slots, 0), (8, LAT))
    shift_ref[...] = shift
    inverse = 1.0 / norm_ref[...]
    back = shift * inverse
    parts = both_parts(padded_lines(other_ref, slots))
    names = [names_ref[pl.ds(j, 1), :] for j in range(onehot_ref.shape[1] // LAT)]
    lines = found_lines(onehot_of(names, own_ref[...]), parts) + half_lines_ref[...] - lines_ref[...] * back[:1]
    rays = push_lines(lines, tiles_ref, pick_ref, turned_ref, slots)
    zeros = jnp.zeros((PAD, LON_DEV, LAT), F32)
    next_ref[:PAD] = zeros
    next_ref[PAIRS + PAD :] = zeros
    square = jnp.zeros((8, LAT), F32)
    cross = jnp.zeros((8, LAT), F32)
    for first in range(0, LINES, CHUNK):
        count, pair = CHUNK // LON_DEV, first // LON_DEV
        piece = found_lines(onehot_ref[first : first + CHUNK, :], parts).reshape(count, LON_DEV, LAT)
        base = field_ref[pair + PAD : pair + PAD + count]
        piece = piece + half_ref[pair : pair + count] - base * back
        next_ref[pair + PAD : pair + PAD + count] = piece
        square = square + jnp.sum(piece * piece, axis=0)
        cross = cross + jnp.sum(piece * base, axis=0)
    sub = sub_iota()
    out_ref[:RT, :] = rays
    out_ref[RT : RT + 8, :] = jnp.where(
        sub == 0, total(square), jnp.where(sub == 1, total(cross) * inverse, square_ref[...])
    )
    edge = edge_of(next_ref, jnp.where(lax.axis_index("vox") == 0, LON_DEV - 1, 0))
    half = PAIRS // 2
    out_ref[RT + 8 :, :] = jnp.where(lax.axis_index("ray") % 2 == 0, edge[:half], edge[half:])


def fourth_body(mine_ref, other_ref, shift_ref, weight_ref, rays_ref, image_ref,
                next_rays_ref, left_ref, rest_ref, norm_ref, sum_ref):
    sums = mine_ref[RT : RT + 8, :] + other_ref[RT : RT + 8, :]
    square, cross, rest = [jnp.broadcast_to(sums[j : j + 1], (8, LAT)) for j in range(3)]
    left_sq = shift_ref[...] + rest
    norm_sq = (square - 2.0 * rest * cross + rest * rest) / left_sq
    per_left = lax.rsqrt(left_sq)
    inverse = lax.rsqrt(norm_sq)
    norm = norm_sq * inverse
    rays = mine_ref[:RT, :] + other_ref[:RT, :] - rest * image_ref[...]
    rays = weight_ref[...] * rays * (per_left * inverse) - norm * per_left * rays_ref[...]
    next_rays_ref[...] = rays
    left_ref[...] = left_sq
    rest_ref[...] = rest
    norm_ref[...] = norm
    sum_ref[...] = jnp.broadcast_to(total(rays * rays), (8, LAT))


def last_smooth_body(halves, next_ref, low_ref, high_ref, damp_ref, smooth_ref, norm_ref, left_ref, rest_ref,
                     square_ref, near_ref):
    sub, lane = sub_iota(), lane_iota()
    has_low, has_high = flags()
    if halves:
        odd, half = lax.axis_index("ray") % 2, PAIRS // 2
        for ref, at in ((low_ref, odd), (high_ref, 1 - odd)):
            near_ref[0, pl.ds(at * half, half), :] = ref[...] * has_low
            near_ref[1, pl.ds(at * half, half), :] = ref[...] * has_high
    else:
        near_ref[0] = low_ref[...] * has_low
        near_ref[1] = high_ref[...] * has_high
    norm, per_left = norm_ref[...], lax.rsqrt(left_ref[...])
    inverse = per_left / norm
    back = rest_ref[...] * inverse + norm * per_left

    def left(pair, square):
        damped = damp_ref[pl.ds(pair, 1), :]
        value = slab_stencil(pair, next_ref, near_ref.at[0], near_ref.at[1], sub, lane) * inverse * damped
        value = value - back * smooth_ref[pair]
        return square + value * value

    square = lax.fori_loop(0, PAIRS, left, jnp.zeros((LON_DEV, LAT), F32), unroll=UNROLL)
    square_ref[...] = jnp.broadcast_to(total(square), (8, LAT))


def end_body(share, parts, *refs):
    sums = refs[0][...]
    for ref in refs[1:parts]:
        sums = sums + ref[...]
    (left0_ref, norm0_ref, left1_ref, rest_ref, norm1_ref, rays_ref, field_ref, next_ref,
     density_ref, out_ref) = refs[parts:]
    left2_sq = sums
    out_ref[...] = rays_ref[...] * lax.rsqrt(left2_sq)
    left0_sq, norm0, left1_sq, right1 = left0_ref[...], norm0_ref[...], left1_ref[...], norm1_ref[...]
    left0, left1 = jnp.sqrt(left0_sq), jnp.sqrt(left1_sq)
    right0 = norm0 / left0
    diag1 = jnp.sqrt(right0 * right0 + left1_sq)
    cosine, sine = right0 / diag1, left1 / diag1
    coupling = sine * right1
    diag_bar = -cosine * right1
    step1, resid = cosine * left0, sine * left0
    diag2 = jnp.sqrt(diag_bar * diag_bar + left2_sq)
    step2 = diag_bar / diag2 * resid
    on_next = step2 / diag2 / (left1 * right1)
    on_first = (step1 / diag1 - step2 / diag2 * coupling / diag1 - on_next * rest_ref[...]) / norm0
    first = lax.axis_index("ray") * share + PAD
    for j in range(share):
        density_ref[j] = on_first * field_ref[first + j] + on_next * next_ref[first + j]


def on_device(
    tiles,
    tile_scale,
    tile_row,
    tile_col,
    tile_count,
    delays,
    ray_receiver,
    receiver_weight,
    smooth_scale,
):
    block = tiles[0, 0]
    slots = block.shape[0]
    rays_n = lax.axis_size("ray")
    col_index = tile_col[0, 0]
    held = (RT, RAY_TILE)
    row = ((8, LAT), F32)
    slab = ((PAIRS, LON_DEV, LAT), F32)
    padded = ((PAIRS + 2 * PAD, LON_DEV, LAT), F32)
    packet = ((slots + 8, LAT), F32)
    damp = jnp.broadcast_to(jnp.repeat(smooth_scale, EPOCHS)[:, None], (PAIRS, LAT))

    hbm = pl.BlockSpec(memory_space=pl.ANY)
    table = receiver_weight.shape[0]
    mine, weight, start, pick, own, block = local_call(
        functools.partial(start_body, slots), "start", [SM] + [hbm] * 7,
        [packet, (held, F32), (held, F32), ((slots, RT, LAT), F32), ((slots, LAT), jnp.int32),
         (block.shape, BF16)],
        [pltpu.SMEM((slots,), jnp.int32), pltpu.SMEM((slots,), jnp.int32), pltpu.SMEM((slots,), F32),
         pltpu.SMEM((table,), F32), pltpu.VMEM(held, jnp.int32),
         pltpu.VMEM(held, F32), pltpu.SemaphoreType.DMA((6 + PULLS,))],
    )(tile_count, *(pltpu.with_memory_space_constraint(x, pltpu.MemorySpace.HBM) for x in (
        tile_row[0, 0], col_index, tile_scale[0, 0], receiver_weight,
        ray_receiver.reshape(held), delays.reshape(held), block)))
    near, far, damp = gather_rays(mine, (lambda _: damp,))
    per = LAT // slots
    names_n = -(-(near.shape[0] // (slots + 8)) // per)
    named = ((names_n, LAT), jnp.int32)
    turned = pltpu.VMEM((RAY_TILE, LAT), F32)

    half, half_lines, names_a = local_call(
        functools.partial(first_half_body, slots), "first_half", [VM] * 2,
        [slab, ((slots, LAT), F32), named],
    )(near, own)
    field, lines, sums, left0, names_b = local_call(
        functools.partial(first_body, slots), "first", [VM] * 7,
        [padded, ((slots, LAT), F32), ((RT + 8 + PAIRS, LAT), F32), row, named], [turned],
    )(far, half, half_lines, near, own, pick, block)
    others, columns, swapped = first_halo(sums, field)
    onehots = local_call(
        onehot_body, "onehot", [VM] * 2, [((LINES, names_n * LAT), BF16)] * 2,
    )(names_a, names_b)
    others, (onehot_a, onehot_b) = lax.optimization_barrier((others, onehots))

    mine, rays, image, norm0 = local_call(
        functools.partial(second_body, slots), "second", [VM] * 7, [packet, (held, F32), (held, F32), row],
    )(sums, others, left0, weight, start, pick, block)
    def smooth_step(columns):
        return local_call(
            functools.partial(smooth_body, swapped), "smooth", [VM] * 7,
            [slab, padded, ((2, PAIRS, LAT), F32), row], [pltpu.VMEM((2, PAIRS, LAT), F32)],
        )(field, *columns, damp, norm0)

    def again_step(given):
        smooth, scaled, beside, square = given
        again, again_lines = local_call(
            functools.partial(again_body, slots), "again", [SM] + [VM] * 2, [slab, ((slots, LAT), F32)],
        )(col_index, scaled, beside)
        return smooth, square, again, again_lines

    near, far, given = gather_rays(mine, (lambda _: columns, smooth_step, again_step))
    smooth, square, again, again_lines = given

    half, half_lines = local_call(
        functools.partial(third_half_body, slots), "third_half", [VM] * 6, [slab, ((slots, LAT), F32)],
    )(near, onehot_a, names_a, own, again_lines, again)
    following, sums, shift = local_call(
        functools.partial(third_body, slots), "third", [VM] * 13,
        [padded, ((RT + 8 + PAIRS // 2, LAT), F32), row], [turned],
    )(far, half, half_lines, near, square, onehot_b, names_b, own, lines, field, norm0, pick, block)
    others, beside, halves = next_halo(sums, following)
    last_rays, left1, rest, norm1, ray_square = local_call(
        fourth_body, "fourth", [VM] * 6, [(held, F32), row, row, row, row],
    )(sums, others, shift, weight, rays, image)

    def last_step(beside):
        return local_call(
            functools.partial(last_smooth_body, halves), "last_smooth", [VM] * 8, [row], [pltpu.VMEM((2, PAIRS, LAT), F32)],
        )(following, *beside, damp, smooth, norm1, left1, rest)[0]

    shares = last_sums(ray_square, beside, last_step)

    share = PAIRS // rays_n
    density, rays_out = local_call(
        functools.partial(end_body, share, len(shares)), "end", [VM] * (len(shares) + 8),
        [((share, LON_DEV, LAT), F32), (held, F32)],
    )(*shares, left0, norm0, left1, rest, norm1, last_rays, field, following)
    return (density.reshape(ALT // rays_n, EPOCHS, LON_DEV, LAT), rays_out.reshape(-1))


def solution(mesh):
    in_specs = (
        P("ray", "vox", None, None, None),
        P("ray", "vox", None),
        P("ray", "vox", None),
        P("ray", "vox", None),
        P("ray", "vox"),
        P("ray"),
        P("ray"),
        P("ray"),
        P(),
    )
    out_specs = (P("ray", None, "vox", None), P("ray"))
    return jax.shard_map(
        on_device, mesh=mesh, in_specs=in_specs, out_specs=out_specs, check_vma=False
    )
```

```python
import functools

import jax
import jax.numpy as jnp
from jax import lax
from jax.experimental import pallas as pl
from jax.experimental.pallas import tpu as pltpu
from jax.sharding import PartitionSpec as P

ALT = 64
EPOCHS = 2
LAT = 128
LON_DEV = 8
RAY_TILE = 128
RT = 8
PAIRS = ALT * EPOCHS
LINES = PAIRS * LON_DEV
PAD = EPOCHS
UNROLL = 8

LATERAL = 1.0
VERTICAL = 4.0
TEMPORAL = 0.5
CENTRE = 2.0 * (2.0 * LATERAL + VERTICAL + TEMPORAL)

F32 = jnp.float32
BF16 = jnp.bfloat16
VM = pl.BlockSpec(memory_space=pltpu.VMEM)
SM = pl.BlockSpec(memory_space=pltpu.SMEM)


def local_call(body, name, in_specs, out_shapes, scratch=()):
    return pl.pallas_call(
        body,
        name=name,
        in_specs=in_specs,
        out_specs=[VM] * len(out_shapes),
        out_shape=[jax.ShapeDtypeStruct(shape, dtype) for shape, dtype in out_shapes],
        scratch_shapes=list(scratch),
        compiler_params=pltpu.CompilerParams(vmem_limit_bytes=32 << 20),
    )


def pairs_of(count, step):
    return [(i, i ^ step) for i in range(count)]


def hops(count):
    steps = []
    while count > 1:
        count //= 2
        steps.append(count | 1)
    return steps


def gather_rays(block, during=()):
    count = lax.axis_size("ray")
    done, given = list(during), None
    if count & (count - 1) or count == 1:
        whole = lax.all_gather(block, "ray", tiled=True)
        half = whole.shape[0] // 2
        block, other = whole[:half], whole[half:]
    else:
        for step in hops(count):
            other = lax.ppermute(block, "ray", pairs_of(count, step))
            if step == 1:
                break
            joined = jnp.concatenate([block, other], axis=0)
            if done:
                given = done.pop(0)(given)
                joined, given = lax.optimization_barrier((joined, given))
            block = joined
    while done:
        given = done.pop(0)(given)
    return block, other, given


def vox_others(value):
    count = lax.axis_size("vox")
    if count == 1:
        return jnp.zeros_like(value)
    if count == 2:
        return lax.ppermute(value, "vox", [(0, 1), (1, 0)])
    return lax.psum(value, "vox") - value


def last_sums(value, given, step_of):
    count, slabs = lax.axis_size("ray"), lax.axis_size("vox")
    if slabs != 2 or count & (count - 1) or count < 16:
        mine = step_of(given)
        return lax.psum(value, "ray"), mine, vox_others(mine)
    for step in hops(count)[:-2]:
        value = value + lax.ppermute(value, "ray", pairs_of(count, step))
        if step == count // 4 | 1:
            given = step_of(given)
        value, given = lax.optimization_barrier((value, given))
    mine = given
    both = jnp.concatenate([value, mine], axis=0)
    both = lax.ppermute(both, ("ray", "vox"), [(i, i ^ 7) for i in range(2 * count)])
    value = value + both[:8]
    return value, lax.ppermute(value, "ray", pairs_of(count, 1)), mine, both[8:]


def halo_of(low_edge, high_edge):
    count = lax.axis_size("vox")
    if count == 1:
        return jnp.zeros_like(high_edge), jnp.zeros_like(low_edge)
    forward = [(i, i + 1) for i in range(count - 1)]
    backward = [(target, source) for source, target in forward]
    return lax.ppermute(high_edge, "vox", forward), lax.ppermute(low_edge, "vox", backward)


def first_halo(sums, field):
    if lax.axis_size("vox") == 2 and lax.axis_size("ray") % 2 == 0:
        other = lax.ppermute(sums, "vox", [(0, 1), (1, 0)])
        column = other[RT + 8 :]
        partner = lax.ppermute(column, "ray", pairs_of(lax.axis_size("ray"), 1))
        return other, (column, partner, column, partner), True
    low = halo_of(field[PAD:-PAD, 0], field[PAD:-PAD, -1])
    far = halo_of(field[PAD:-PAD, 1], field[PAD:-PAD, -2])
    return vox_others(sums), (low[0], far[0], low[1], far[1]), False


def next_halo(sums, field):
    if lax.axis_size("vox") == 2 and lax.axis_size("ray") % 2 == 0:
        other = lax.ppermute(sums, "vox", [(0, 1), (1, 0)])
        half = other[RT + 8 :]
        return other, (half, lax.ppermute(half, "ray", pairs_of(lax.axis_size("ray"), 1))), True
    return vox_others(sums), halo_of(field[PAD:-PAD, 0], field[PAD:-PAD, -1]), False


def total(values):
    return jnp.sum(values, axis=(0, 1), keepdims=True)


def sub_iota(shape=(8, LAT)):
    return lax.broadcasted_iota(jnp.int32, shape, 0)


def lane_iota(shape=(8, LAT)):
    return lax.broadcasted_iota(jnp.int32, shape, 1)


def pull_lines(weighted, tiles_ref, pick_ref, out_ref, slots):
    rays = weighted.astype(BF16)
    for k in range(0, slots, 2):
        pair = jnp.concatenate([tiles_ref[k], tiles_ref[k + 1]], axis=1)
        product = jnp.dot(rays, pair, preferred_element_type=F32)
        out_ref[pl.ds(k, 1), :] = jnp.sum(pick_ref[k] * product[:, :LAT], axis=0, keepdims=True)
        out_ref[pl.ds(k + 1, 1), :] = jnp.sum(pick_ref[k + 1] * product[:, LAT:], axis=0, keepdims=True)


def push_lines(rays, lines, tiles_ref, pick_ref, first, last):
    for k in range(first, last, 2):
        both = [jnp.broadcast_to(lines[j : j + 1], (RT, LAT)) for j in (k, k + 1)]
        product = lax.dot_general(
            jnp.concatenate(both, axis=0).astype(BF16),
            tiles_ref[pl.ds(k, 2)].reshape(2 * RAY_TILE, LAT),
            (((1,), (1,)), ((), ())),
            preferred_element_type=F32,
        )
        rays = rays + pick_ref[k] * product[:RT, :RAY_TILE]
        rays = rays + pick_ref[k + 1] * product[RT:, RAY_TILE:]
    return rays


def both_parts(lines):
    high = lines.astype(BF16)
    low = (lines - high.astype(F32)).astype(BF16)
    return jnp.concatenate([high, low], axis=1)


def across(values, sub, lane):
    up = jnp.where(lane == 0, 0.0, pltpu.roll(values, 1, 1))
    down = jnp.where(lane == LAT - 1, 0.0, pltpu.roll(values, LAT - 1, 1))
    return up + down


def column_stencil(column, beside, lane, sub):
    up = jnp.where(sub < EPOCHS, 0.0, pltpu.roll(column, EPOCHS, 0))
    down = jnp.where(sub >= PAIRS - EPOCHS, 0.0, pltpu.roll(column, PAIRS - EPOCHS, 0))
    later = pltpu.roll(column, PAIRS - 1, 0)
    earlier = pltpu.roll(column, 1, 0)
    epoch = jnp.where(sub % EPOCHS == 0, later, earlier)
    return (
        CENTRE * column
        - LATERAL * (beside + across(column, sub, lane))
        - VERTICAL * (up + down)
        - TEMPORAL * epoch
    )


def slab_stencil(pair, field_ref, low_ref, high_ref, sub, lane):
    here = field_ref[pair + PAD]
    below = jnp.where(sub == 0, low_ref[pl.ds(pair, 1), :], pltpu.roll(here, 1, 0))
    above = jnp.where(sub == LON_DEV - 1, high_ref[pl.ds(pair, 1), :], pltpu.roll(here, LON_DEV - 1, 0))
    epoch = field_ref[(pair ^ 1) + PAD]
    return (
        CENTRE * here
        - LATERAL * (below + above + across(here, sub, lane))
        - VERTICAL * (field_ref[pair] + field_ref[pair + 2 * PAD])
        - TEMPORAL * epoch
    )


def start_body(slots, count_ref, row_in, col_in, scale_in, table_in, receiver_in, delays_in, tiles_in,
               packet_ref, weight_ref, start_ref, pick_ref, own_ref, tiles_ref,
               row_ref, col_ref, scale_ref, table_ref, receiver_ref, delays_ref, sems):
    copies = [
        pltpu.make_async_copy(source, target, sems.at[j])
        for j, (source, target) in enumerate([
            (receiver_in, receiver_ref), (table_in, table_ref), (delays_in, delays_ref),
            (scale_in, scale_ref), (row_in, row_ref), (col_in, col_ref),
        ])
    ]
    pull = pltpu.make_async_copy(tiles_in, tiles_ref, sems.at[6])
    pull.start()
    for copy in copies:
        copy.start()
    for copy in copies:
        copy.wait()
    sub, lane = sub_iota(), lane_iota()
    receivers = receiver_ref[...]
    weight = jnp.zeros((RT, RAY_TILE), F32)
    for j in range(table_ref.shape[0]):
        weight = jnp.where(receivers == j, table_ref[j], weight)
    weight_ref[...] = weight
    start = weight * delays_ref[...]
    start_ref[...] = start
    names = jnp.zeros((8, LAT), jnp.int32)
    for k in range(slots):
        live = jnp.where(k < count_ref[0, 0], scale_ref[k], 0.0)
        pick_ref[k] = jnp.where(sub == row_ref[k], live, 0.0)
        own_ref[pl.ds(k, 1), :] = jnp.full((1, LAT), col_ref[k], jnp.int32)
        names = jnp.where(lane == k, col_ref[k], names)
    square = total(start * start)
    packet_ref[slots:, :] = jnp.where(
        sub == 0, names.astype(F32), jnp.where(sub == 1, square, 0.0)
    )
    pull.wait()
    pull_lines(weight * start, tiles_ref, pick_ref, packet_ref, slots)


def names_of(ref, slots):
    blocks = ref.shape[0] // (slots + 8)
    per = LAT // slots
    pieces = []
    for first in range(0, blocks, per):
        row = ref[pl.ds(first * (slots + 8) + slots, 1), :]
        for j in range(1, min(per, blocks - first)):
            row = row + pltpu.roll(ref[pl.ds((first + j) * (slots + 8) + slots, 1), :], j * slots, 1)
        if blocks - first < per:
            row = jnp.where(lane_iota((1, LAT)) < (blocks - first) * slots, row, -1.0)
        pieces.append(row.astype(jnp.int32))
    return pieces


def lines_in(ref, slots):
    blocks = ref.shape[0] // (slots + 8)
    return [ref[b * (slots + 8) : b * (slots + 8) + slots, :] for b in range(blocks)]


def padded_lines(ref, slots):
    per = LAT // slots
    rows = lines_in(ref, slots)
    if len(rows) % per:
        rows.append(jnp.zeros(((per - len(rows) % per) * slots, LAT), F32))
    return jnp.concatenate(rows, axis=0)


def found_lines(onehot, parts):
    found = jnp.dot(onehot, parts, preferred_element_type=F32)
    return found[:, :LAT] + found[:, LAT:]


def rows_sum(ref, slots, at):
    blocks = ref.shape[0] // (slots + 8)
    out = ref[pl.ds(slots + at, 1), :]
    for b in range(1, blocks):
        out = out + ref[pl.ds(b * (slots + 8) + slots + at, 1), :]
    return out


CHUNK = 128


def onehot_of(names, ids):
    return jnp.concatenate(
        [jnp.where(ids == piece, 1.0, 0.0).astype(BF16) for piece in names], axis=1
    )


def edge_of(field_ref, at):
    flat = field_ref.reshape((PAIRS + 2 * PAD) * LON_DEV, LAT)
    return flat[pl.ds(PAD * LON_DEV + at, PAIRS, stride=LON_DEV), :]


def first_half_body(slots, mine_ref, own_ref, field_ref, lines_ref, names_ref):
    names = names_of(mine_ref, slots)
    for j, piece in enumerate(names):
        names_ref[pl.ds(j, 1), :] = piece
    parts = both_parts(padded_lines(mine_ref, slots))
    lines_ref[...] = found_lines(onehot_of(names, own_ref[...]), parts)
    for first in range(0, LINES, CHUNK):
        onehot = onehot_of(names, sub_iota((CHUNK, LAT)) + first)
        piece = found_lines(onehot, parts).reshape(CHUNK // LON_DEV, LON_DEV, LAT)
        field_ref[first // LON_DEV : (first + CHUNK) // LON_DEV] = piece


def first_body(slots, other_ref, half_ref, half_lines_ref, mine_ref, own_ref, pick_ref, tiles_ref,
               field_ref, lines_ref, out_ref, left_ref, names_ref):
    names = names_of(other_ref, slots)
    for j, piece in enumerate(names):
        names_ref[pl.ds(j, 1), :] = piece
    parts = both_parts(padded_lines(other_ref, slots))
    lines = half_lines_ref[...] + found_lines(onehot_of(names, own_ref[...]), parts)
    lines_ref[...] = lines
    rays, part = jnp.zeros((RT, RAY_TILE), F32), slots * CHUNK // LINES
    zeros = jnp.zeros((PAD, LON_DEV, LAT), F32)
    field_ref[:PAD] = zeros
    field_ref[PAIRS + PAD :] = zeros
    square = jnp.zeros((8, LAT), F32)
    for first in range(0, LINES, CHUNK):
        onehot = onehot_of(names, sub_iota((CHUNK, LAT)) + first)
        count, pair = CHUNK // LON_DEV, first // LON_DEV
        piece = found_lines(onehot, parts).reshape(count, LON_DEV, LAT) + half_ref[pair : pair + count]
        field_ref[pair + PAD : pair + PAD + count] = piece
        square = square + jnp.sum(piece * piece, axis=0)
        rays = push_lines(rays, lines, tiles_ref, pick_ref, first // CHUNK * part, (first // CHUNK + 1) * part)
    out_ref[:RT, :] = rays
    out_ref[RT : RT + 8, :] = jnp.broadcast_to(total(square), (8, LAT))
    odd = lax.axis_index("ray") % 2
    at = jnp.where(lax.axis_index("vox") == 0, LON_DEV - 1 - odd, odd)
    out_ref[RT + 8 :, :] = edge_of(field_ref, at)
    left_ref[...] = jnp.broadcast_to(rows_sum(mine_ref, slots, 1) + rows_sum(other_ref, slots, 1), (8, LAT))


def second_body(slots, mine_ref, other_ref, left_ref, weight_ref, start_ref, pick_ref, tiles_ref,
                packet_ref, rays_ref, image_ref, norm_ref):
    sub = sub_iota()
    left_sq = left_ref[...]
    norm_sq = mine_ref[RT : RT + 8, :] + other_ref[RT : RT + 8, :]
    inverse = lax.rsqrt(norm_sq)
    norm = norm_sq * inverse
    weight = weight_ref[...]
    image = (mine_ref[:RT, :] + other_ref[:RT, :]) * inverse
    image_ref[...] = image
    rays = weight * image - norm / left_sq * start_ref[...]
    rays_ref[...] = rays
    norm_ref[...] = norm
    pull_lines(weight * rays, tiles_ref, pick_ref, packet_ref, slots)
    packet_ref[slots:, :] = jnp.where(sub == 0, total(rays * rays), 0.0)


def flags():
    at, count = lax.axis_index("vox"), lax.axis_size("vox")
    return (at > 0).astype(F32), (at < count - 1).astype(F32)


def smooth_body(swapped, field_ref, low_ref, low2_ref, high_ref, high2_ref, damp_ref, norm_ref,
                smooth_ref, scaled_ref, far_ref, square_ref, near_ref):
    sub, lane = sub_iota(), lane_iota()
    has_low, has_high = flags()
    inverse = 1.0 / norm_ref[...]
    col_lane, col_sub = lane_iota((PAIRS, LAT)), sub_iota((PAIRS, LAT))
    low, low2, high, high2 = low_ref[...], low2_ref[...], high_ref[...], high2_ref[...]
    if swapped:
        odd = lax.axis_index("ray") % 2 == 1
        low, low2 = jnp.where(odd, low2, low), jnp.where(odd, low, low2)
        high, high2 = low, low2
    near_ref[0] = low * has_low
    near_ref[1] = high * has_high
    scale = damp_ref[...] * damp_ref[...] * jnp.broadcast_to(inverse[:1], (PAIRS, LAT))
    far_ref[0] = scale * has_low * column_stencil(low, low2 + edge_of(field_ref, 0), col_lane, col_sub)
    far_ref[1] = scale * has_high * column_stencil(
        high, high2 + edge_of(field_ref, LON_DEV - 1), col_lane, col_sub
    )
    zeros = jnp.zeros((PAD, LON_DEV, LAT), F32)
    scaled_ref[:PAD] = zeros
    scaled_ref[PAIRS + PAD :] = zeros

    def left(pair, square):
        damped = damp_ref[pl.ds(pair, 1), :]
        value = slab_stencil(pair, field_ref, near_ref.at[0], near_ref.at[1], sub, lane) * inverse * damped
        smooth_ref[pair] = value
        scaled_ref[pair + PAD] = value * damped
        return square + value * value

    square = lax.fori_loop(0, PAIRS, left, jnp.zeros((LON_DEV, LAT), F32), unroll=UNROLL)
    square_ref[...] = jnp.broadcast_to(total(square), (8, LAT))


def onehot_body(*refs):
    names_refs, onehot_refs = refs[: len(refs) // 2], refs[len(refs) // 2 :]
    for names_ref, onehot_ref in zip(names_refs, onehot_refs):
        pieces = [names_ref[pl.ds(j, 1), :] for j in range(onehot_ref.shape[1] // LAT)]
        for first in range(0, LINES, CHUNK):
            onehot_ref[first : first + CHUNK, :] = onehot_of(pieces, sub_iota((CHUNK, LAT)) + first)


def again_body(slots, col_ref, scaled_ref, far_ref, again_ref, lines_ref):
    sub, lane = sub_iota(), lane_iota()

    def right(pair, carry):
        again_ref[pair] = slab_stencil(pair, scaled_ref, far_ref.at[0], far_ref.at[1], sub, lane)
        return carry

    lax.fori_loop(0, PAIRS, right, 0, unroll=UNROLL)
    for k in range(slots):
        col = col_ref[k]
        lines_ref[pl.ds(k, 1), :] = again_ref[col // LON_DEV, pl.ds(col % LON_DEV, 1), :]


def third_half_body(slots, mine_ref, onehot_ref, names_ref, own_ref, again_lines_ref, again_ref,
                    half_ref, lines_ref):
    parts = both_parts(padded_lines(mine_ref, slots))
    names = [names_ref[pl.ds(j, 1), :] for j in range(onehot_ref.shape[1] // LAT)]
    lines_ref[...] = found_lines(onehot_of(names, own_ref[...]), parts) + again_lines_ref[...]
    for first in range(0, LINES, CHUNK):
        count, pair = CHUNK // LON_DEV, first // LON_DEV
        piece = found_lines(onehot_ref[first : first + CHUNK, :], parts).reshape(count, LON_DEV, LAT)
        half_ref[pair : pair + count] = piece + again_ref[pair : pair + count]


def third_body(slots, other_ref, half_ref, half_lines_ref, mine_ref, square_ref, onehot_ref, names_ref, own_ref,
               lines_ref, field_ref, norm_ref, pick_ref, tiles_ref,
               next_ref, out_ref, shift_ref):
    shift = jnp.broadcast_to(rows_sum(mine_ref, slots, 0) + rows_sum(other_ref, slots, 0), (8, LAT))
    shift_ref[...] = shift
    inverse = 1.0 / norm_ref[...]
    back = shift * inverse
    parts = both_parts(padded_lines(other_ref, slots))
    names = [names_ref[pl.ds(j, 1), :] for j in range(onehot_ref.shape[1] // LAT)]
    lines = found_lines(onehot_of(names, own_ref[...]), parts) + half_lines_ref[...] - lines_ref[...] * back[:1]
    rays, part = jnp.zeros((RT, RAY_TILE), F32), slots * CHUNK // LINES
    zeros = jnp.zeros((PAD, LON_DEV, LAT), F32)
    next_ref[:PAD] = zeros
    next_ref[PAIRS + PAD :] = zeros
    square = jnp.zeros((8, LAT), F32)
    cross = jnp.zeros((8, LAT), F32)
    for first in range(0, LINES, CHUNK):
        count, pair = CHUNK // LON_DEV, first // LON_DEV
        piece = found_lines(onehot_ref[first : first + CHUNK, :], parts).reshape(count, LON_DEV, LAT)
        base = field_ref[pair + PAD : pair + PAD + count]
        piece = piece + half_ref[pair : pair + count] - base * back
        next_ref[pair + PAD : pair + PAD + count] = piece
        square = square + jnp.sum(piece * piece, axis=0)
        cross = cross + jnp.sum(piece * base, axis=0)
        rays = push_lines(rays, lines, tiles_ref, pick_ref, first // CHUNK * part, (first // CHUNK + 1) * part)
    sub = sub_iota()
    out_ref[:RT, :] = rays
    out_ref[RT : RT + 8, :] = jnp.where(
        sub == 0, total(square), jnp.where(sub == 1, total(cross) * inverse, square_ref[...])
    )
    edge = edge_of(next_ref, jnp.where(lax.axis_index("vox") == 0, LON_DEV - 1, 0))
    half = PAIRS // 2
    out_ref[RT + 8 :, :] = jnp.where(lax.axis_index("ray") % 2 == 0, edge[:half], edge[half:])


def fourth_body(mine_ref, other_ref, shift_ref, weight_ref, rays_ref, image_ref,
                next_rays_ref, left_ref, rest_ref, norm_ref, sum_ref):
    sums = mine_ref[RT : RT + 8, :] + other_ref[RT : RT + 8, :]
    square, cross, rest = [jnp.broadcast_to(sums[j : j + 1], (8, LAT)) for j in range(3)]
    left_sq = shift_ref[...] + rest
    norm_sq = (square - 2.0 * rest * cross + rest * rest) / left_sq
    per_left = lax.rsqrt(left_sq)
    inverse = lax.rsqrt(norm_sq)
    norm = norm_sq * inverse
    rays = mine_ref[:RT, :] + other_ref[:RT, :] - rest * image_ref[...]
    rays = weight_ref[...] * rays * (per_left * inverse) - norm * per_left * rays_ref[...]
    next_rays_ref[...] = rays
    left_ref[...] = left_sq
    rest_ref[...] = rest
    norm_ref[...] = norm
    sum_ref[...] = jnp.broadcast_to(total(rays * rays), (8, LAT))


def last_smooth_body(halves, next_ref, low_ref, high_ref, damp_ref, smooth_ref, norm_ref, left_ref, rest_ref,
                     square_ref, near_ref):
    sub, lane = sub_iota(), lane_iota()
    has_low, has_high = flags()
    if halves:
        odd, half = lax.axis_index("ray") % 2, PAIRS // 2
        for ref, at in ((low_ref, odd), (high_ref, 1 - odd)):
            near_ref[0, pl.ds(at * half, half), :] = ref[...] * has_low
            near_ref[1, pl.ds(at * half, half), :] = ref[...] * has_high
    else:
        near_ref[0] = low_ref[...] * has_low
        near_ref[1] = high_ref[...] * has_high
    norm, per_left = norm_ref[...], lax.rsqrt(left_ref[...])
    inverse = per_left / norm
    back = rest_ref[...] * inverse + norm * per_left

    def left(pair, square):
        damped = damp_ref[pl.ds(pair, 1), :]
        value = slab_stencil(pair, next_ref, near_ref.at[0], near_ref.at[1], sub, lane) * inverse * damped
        value = value - back * smooth_ref[pair]
        return square + value * value

    square = lax.fori_loop(0, PAIRS, left, jnp.zeros((LON_DEV, LAT), F32), unroll=UNROLL)
    square_ref[...] = jnp.broadcast_to(total(square), (8, LAT))


def end_body(share, parts, *refs):
    sums = refs[0][...]
    for ref in refs[1:parts]:
        sums = sums + ref[...]
    (left0_ref, norm0_ref, left1_ref, rest_ref, norm1_ref, rays_ref, field_ref, next_ref,
     density_ref, out_ref) = refs[parts:]
    left2_sq = sums
    out_ref[...] = rays_ref[...] * lax.rsqrt(left2_sq)
    left0_sq, norm0, left1_sq, right1 = left0_ref[...], norm0_ref[...], left1_ref[...], norm1_ref[...]
    left0, left1 = jnp.sqrt(left0_sq), jnp.sqrt(left1_sq)
    right0 = norm0 / left0
    diag1 = jnp.sqrt(right0 * right0 + left1_sq)
    cosine, sine = right0 / diag1, left1 / diag1
    coupling = sine * right1
    diag_bar = -cosine * right1
    step1, resid = cosine * left0, sine * left0
    diag2 = jnp.sqrt(diag_bar * diag_bar + left2_sq)
    step2 = diag_bar / diag2 * resid
    on_next = step2 / diag2 / (left1 * right1)
    on_first = (step1 / diag1 - step2 / diag2 * coupling / diag1 - on_next * rest_ref[...]) / norm0
    first = lax.axis_index("ray") * share + PAD
    for j in range(share):
        density_ref[j] = on_first * field_ref[first + j] + on_next * next_ref[first + j]


def on_device(
    tiles,
    tile_scale,
    tile_row,
    tile_col,
    tile_count,
    delays,
    ray_receiver,
    receiver_weight,
    smooth_scale,
):
    block = tiles[0, 0]
    slots = block.shape[0]
    rays_n = lax.axis_size("ray")
    col_index = tile_col[0, 0]
    held = (RT, RAY_TILE)
    row = ((8, LAT), F32)
    slab = ((PAIRS, LON_DEV, LAT), F32)
    padded = ((PAIRS + 2 * PAD, LON_DEV, LAT), F32)
    packet = ((slots + 8, LAT), F32)
    damp = jnp.broadcast_to(jnp.repeat(smooth_scale, EPOCHS)[:, None], (PAIRS, LAT))

    hbm = pl.BlockSpec(memory_space=pl.ANY)
    table = receiver_weight.shape[0]
    mine, weight, start, pick, own, block = local_call(
        functools.partial(start_body, slots), "start", [SM] + [hbm] * 7,
        [packet, (held, F32), (held, F32), ((slots, RT, LAT), F32), ((slots, LAT), jnp.int32),
         (block.shape, BF16)],
        [pltpu.SMEM((slots,), jnp.int32), pltpu.SMEM((slots,), jnp.int32), pltpu.SMEM((slots,), F32),
         pltpu.SMEM((table,), F32), pltpu.VMEM(held, jnp.int32),
         pltpu.VMEM(held, F32), pltpu.SemaphoreType.DMA((7,))],
    )(tile_count, *(pltpu.with_memory_space_constraint(x, pltpu.MemorySpace.HBM) for x in (
        tile_row[0, 0], col_index, tile_scale[0, 0], receiver_weight,
        ray_receiver.reshape(held), delays.reshape(held), block)))
    near, far, damp = gather_rays(mine, (lambda _: damp,))
    per = LAT // slots
    names_n = -(-(near.shape[0] // (slots + 8)) // per)
    named = ((names_n, LAT), jnp.int32)

    half, half_lines, names_a = local_call(
        functools.partial(first_half_body, slots), "first_half", [VM] * 2,
        [slab, ((slots, LAT), F32), named],
    )(near, own)
    field, lines, sums, left0, names_b = local_call(
        functools.partial(first_body, slots), "first", [VM] * 7,
        [padded, ((slots, LAT), F32), ((RT + 8 + PAIRS, LAT), F32), row, named],
    )(far, half, half_lines, near, own, pick, block)
    others, columns, swapped = first_halo(sums, field)
    onehots = local_call(
        onehot_body, "onehot", [VM] * 2, [((LINES, names_n * LAT), BF16)] * 2,
    )(names_a, names_b)
    others, (onehot_a, onehot_b) = lax.optimization_barrier((others, onehots))

    mine, rays, image, norm0 = local_call(
        functools.partial(second_body, slots), "second", [VM] * 7, [packet, (held, F32), (held, F32), row],
    )(sums, others, left0, weight, start, pick, block)
    def smooth_step(columns):
        return local_call(
            functools.partial(smooth_body, swapped), "smooth", [VM] * 7,
            [slab, padded, ((2, PAIRS, LAT), F32), row], [pltpu.VMEM((2, PAIRS, LAT), F32)],
        )(field, *columns, damp, norm0)

    def again_step(given):
        smooth, scaled, beside, square = given
        again, again_lines = local_call(
            functools.partial(again_body, slots), "again", [SM] + [VM] * 2, [slab, ((slots, LAT), F32)],
        )(col_index, scaled, beside)
        return smooth, square, again, again_lines

    near, far, given = gather_rays(mine, (lambda _: columns, smooth_step, again_step))
    smooth, square, again, again_lines = given

    half, half_lines = local_call(
        functools.partial(third_half_body, slots), "third_half", [VM] * 6, [slab, ((slots, LAT), F32)],
    )(near, onehot_a, names_a, own, again_lines, again)
    following, sums, shift = local_call(
        functools.partial(third_body, slots), "third", [VM] * 13,
        [padded, ((RT + 8 + PAIRS // 2, LAT), F32), row],
    )(far, half, half_lines, near, square, onehot_b, names_b, own, lines, field, norm0, pick, block)
    others, beside, halves = next_halo(sums, following)
    last_rays, left1, rest, norm1, ray_square = local_call(
        fourth_body, "fourth", [VM] * 6, [(held, F32), row, row, row, row],
    )(sums, others, shift, weight, rays, image)

    def last_step(beside):
        return local_call(
            functools.partial(last_smooth_body, halves), "last_smooth", [VM] * 8, [row], [pltpu.VMEM((2, PAIRS, LAT), F32)],
        )(following, *beside, damp, smooth, norm1, left1, rest)[0]

    shares = last_sums(ray_square, beside, last_step)

    share = PAIRS // rays_n
    density, rays_out = local_call(
        functools.partial(end_body, share, len(shares)), "end", [VM] * (len(shares) + 8),
        [((share, LON_DEV, LAT), F32), (held, F32)],
    )(*shares, left0, norm0, left1, rest, norm1, last_rays, field, following)
    return (density.reshape(ALT // rays_n, EPOCHS, LON_DEV, LAT), rays_out.reshape(-1))


def solution(mesh):
    in_specs = (
        P("ray", "vox", None, None, None),
        P("ray", "vox", None),
        P("ray", "vox", None),
        P("ray", "vox", None),
        P("ray", "vox"),
        P("ray"),
        P("ray"),
        P("ray"),
        P(),
    )
    out_specs = (P("ray", None, "vox", None), P("ray"))
    return jax.shard_map(
        on_device, mesh=mesh, in_specs=in_specs, out_specs=out_specs, check_vma=False
    )
```

```python
import functools

import jax
import jax.numpy as jnp
from jax import lax
from jax.experimental import pallas as pl
from jax.experimental.pallas import tpu as pltpu
from jax.sharding import PartitionSpec as P

ALT = 64
EPOCHS = 2
LAT = 128
LON_DEV = 8
RAY_TILE = 128
RT = 8
CORES = 2
PAIRS = ALT * EPOCHS
LINES = PAIRS * LON_DEV
PAD = EPOCHS
UNROLL = 32

LATERAL = 1.0
VERTICAL = 4.0
TEMPORAL = 0.5
CENTRE = 2.0 * (2.0 * LATERAL + VERTICAL + TEMPORAL)

F32 = jnp.float32
BF16 = jnp.bfloat16
VM = pl.BlockSpec(memory_space=pltpu.VMEM)
SM = pl.BlockSpec(memory_space=pltpu.SMEM)


def local_call(body, name, in_specs, out_shapes, scratch=()):
    return pl.pallas_call(
        body,
        name=name,
        in_specs=in_specs,
        out_specs=[VM] * len(out_shapes),
        out_shape=[jax.ShapeDtypeStruct(shape, dtype) for shape, dtype in out_shapes],
        scratch_shapes=list(scratch),
        compiler_params=pltpu.CompilerParams(vmem_limit_bytes=32 << 20),
    )


def pairs_of(count, step):
    return [(i, i ^ step) for i in range(count)]


def hops(count):
    steps = []
    while count > 1:
        count //= 2
        steps.append(count | 1)
    return steps


def gather_rays(packet, extra, during=()):
    count = lax.axis_size("ray")
    if count < 2 or count & (count - 1):
        raise ValueError("ray size")
    done, given = list(during), None
    for step in hops(count):
        other = lax.ppermute(packet, "ray", pairs_of(count, step))
        if step == 1:
            break
        joined = jnp.concatenate(
            [packet[:-extra], other[:-extra], packet[-extra:] + other[-extra:]], axis=0
        )
        if done:
            given = done.pop(0)(given)
            joined, given = lax.optimization_barrier((joined, given))
        packet = joined
    while done:
        given = done.pop(0)(given)
    return packet, other, given


def vox_others(value):
    count = lax.axis_size("vox")
    if count == 1:
        return jnp.zeros_like(value)
    if count == 2:
        return lax.ppermute(value, "vox", [(0, 1), (1, 0)])
    return lax.psum(value, "vox") - value


def last_sums(value, given, step_of):
    count, slabs = lax.axis_size("ray"), lax.axis_size("vox")
    if slabs != 2 or count & (count - 1) or count < 16:
        mine = step_of(given)
        return lax.psum(value, "ray"), mine, vox_others(mine)
    for step in hops(count)[:-2]:
        value = value + lax.ppermute(value, "ray", pairs_of(count, step))
        if step == count // 4 | 1:
            given = step_of(given)
        value, given = lax.optimization_barrier((value, given))
    mine = given
    both = jnp.concatenate([value, mine], axis=0)
    both = lax.ppermute(both, ("ray", "vox"), [(i, i ^ 7) for i in range(2 * count)])
    value = value + both[:8]
    return value, lax.ppermute(value, "ray", pairs_of(count, 1)), mine, both[8:]


def halo_of(low_edge, high_edge):
    count = lax.axis_size("vox")
    if count == 1:
        return jnp.zeros_like(high_edge), jnp.zeros_like(low_edge)
    forward = [(i, i + 1) for i in range(count - 1)]
    backward = [(target, source) for source, target in forward]
    return lax.ppermute(high_edge, "vox", forward), lax.ppermute(low_edge, "vox", backward)


def first_halo(sums, field):
    if lax.axis_size("vox") == 2 and lax.axis_size("ray") % 2 == 0:
        other = lax.ppermute(sums, "vox", [(0, 1), (1, 0)])
        column = other[RT + 8 :]
        partner = lax.ppermute(column, "ray", pairs_of(lax.axis_size("ray"), 1))
        return other, (column, partner, column, partner), True
    low = halo_of(field[PAD:-PAD, 0], field[PAD:-PAD, -1])
    far = halo_of(field[PAD:-PAD, 1], field[PAD:-PAD, -2])
    return vox_others(sums), (low[0], far[0], low[1], far[1]), False


def next_halo(sums, field):
    if lax.axis_size("vox") == 2 and lax.axis_size("ray") % 2 == 0:
        other = lax.ppermute(sums, "vox", [(0, 1), (1, 0)])
        half = other[RT + 8 :]
        return other, (half, lax.ppermute(half, "ray", pairs_of(lax.axis_size("ray"), 1))), True
    return vox_others(sums), halo_of(field[PAD:-PAD, 0], field[PAD:-PAD, -1]), False


def total(values):
    return jnp.sum(values, axis=(0, 1), keepdims=True)


def sub_iota(shape=(8, LAT)):
    return lax.broadcasted_iota(jnp.int32, shape, 0)


def lane_iota(shape=(8, LAT)):
    return lax.broadcasted_iota(jnp.int32, shape, 1)


def pull_lines(weighted, tiles_ref, pick_ref, out_ref, slots):
    rays = weighted.astype(BF16)
    for k in range(0, slots, 2):
        pair = jnp.concatenate([tiles_ref[k], tiles_ref[k + 1]], axis=1)
        product = jnp.dot(rays, pair, preferred_element_type=F32)
        out_ref[pl.ds(k, 1), :] = jnp.sum(pick_ref[k] * product[:, :LAT], axis=0, keepdims=True)
        out_ref[pl.ds(k + 1, 1), :] = jnp.sum(pick_ref[k + 1] * product[:, LAT:], axis=0, keepdims=True)


def push_lines(rays, lines, tiles_ref, pick_ref, first, last):
    for k in range(first, last, 2):
        both = [jnp.broadcast_to(lines[j : j + 1], (RT, LAT)) for j in (k, k + 1)]
        product = lax.dot_general(
            jnp.concatenate(both, axis=0).astype(BF16),
            tiles_ref[pl.ds(k, 2)].reshape(2 * RAY_TILE, LAT),
            (((1,), (1,)), ((), ())),
            preferred_element_type=F32,
        )
        rays = rays + pick_ref[k] * product[:RT, :RAY_TILE]
        rays = rays + pick_ref[k + 1] * product[RT:, RAY_TILE:]
    return rays


def both_parts(lines):
    high = lines.astype(BF16)
    low = (lines - high.astype(F32)).astype(BF16)
    return jnp.concatenate([high, low], axis=1)


def across(values, sub, lane):
    up = jnp.where(lane == 0, 0.0, pltpu.roll(values, 1, 1))
    down = jnp.where(lane == LAT - 1, 0.0, pltpu.roll(values, LAT - 1, 1))
    return up + down


def column_stencil(column, beside, lane, sub):
    up = jnp.where(sub < EPOCHS, 0.0, pltpu.roll(column, EPOCHS, 0))
    down = jnp.where(sub >= PAIRS - EPOCHS, 0.0, pltpu.roll(column, PAIRS - EPOCHS, 0))
    later = pltpu.roll(column, PAIRS - 1, 0)
    earlier = pltpu.roll(column, 1, 0)
    epoch = jnp.where(sub % EPOCHS == 0, later, earlier)
    return (
        CENTRE * column
        - LATERAL * (beside + across(column, sub, lane))
        - VERTICAL * (up + down)
        - TEMPORAL * epoch
    )


def slab_stencil(pair, field_ref, low_ref, high_ref, sub, lane):
    here = field_ref[pair + PAD]
    below = jnp.where(sub == 0, low_ref[pl.ds(pair, 1), :], pltpu.roll(here, 1, 0))
    above = jnp.where(sub == LON_DEV - 1, high_ref[pl.ds(pair, 1), :], pltpu.roll(here, LON_DEV - 1, 0))
    epoch = field_ref[(pair ^ 1) + PAD]
    return (
        CENTRE * here
        - LATERAL * (below + above + across(here, sub, lane))
        - VERTICAL * (field_ref[pair] + field_ref[pair + 2 * PAD])
        - TEMPORAL * epoch
    )


def start_body(slots, count_ref, row_in, col_in, scale_in, table_in, receiver_in, delays_in, tiles_in,
               packet_ref, weight_ref, start_ref, pick_ref, own_ref, tiles_ref,
               row_ref, col_ref, scale_ref, table_ref, receiver_ref, delays_ref, sems):
    copies = [
        pltpu.make_async_copy(source, target, sems.at[j])
        for j, (source, target) in enumerate([
            (receiver_in, receiver_ref), (table_in, table_ref), (delays_in, delays_ref),
            (scale_in, scale_ref), (row_in, row_ref), (col_in, col_ref),
        ])
    ]
    pull = pltpu.make_async_copy(tiles_in, tiles_ref, sems.at[6])
    pull.start()
    for copy in copies:
        copy.start()
    for copy in copies:
        copy.wait()
    sub, lane = sub_iota(), lane_iota()
    receivers = receiver_ref[...]
    weight = jnp.zeros((RT, RAY_TILE), F32)
    for j in range(table_ref.shape[0]):
        weight = jnp.where(receivers == j, table_ref[j], weight)
    weight_ref[...] = weight
    start = weight * delays_ref[...]
    start_ref[...] = start
    extra = packet_ref.shape[0] - slots
    sub_x, lane_x = sub_iota((extra, LAT)), lane_iota((extra, LAT))
    side, place = own_place()
    rows, per = names_rows(slots), LAT // slots
    first = place % per * slots
    names = jnp.zeros((1, LAT), jnp.int32)
    for k in range(slots):
        live = jnp.where(k < count_ref[0, 0], scale_ref[k], 0.0)
        pick_ref[k] = jnp.where(sub == row_ref[k], live, 0.0)
        own_ref[pl.ds(k, 1), :] = jnp.full((1, LAT), col_ref[k], jnp.int32)
        names = jnp.where(lane[:1] == first + k, col_ref[k], names)
    square = total(start * start)
    packet_ref[slots:, :] = jnp.where(
        sub_x == side * rows + place // per,
        jnp.broadcast_to(names.astype(F32), (extra, LAT)),
        jnp.where(sub_x == CORES * rows, square, 0.0),
    )
    pull.wait()
    pull_lines(weight * start, tiles_ref, pick_ref, packet_ref, slots)


def own_place():
    count, at = lax.axis_size("ray"), lax.axis_index("ray")
    side, place, bit = at % 2, 0, 1
    for step in hops(count)[:-1]:
        digit = at // (step - 1) % 2
        side = (side + digit) % 2
        place = place + bit * digit
        bit *= 2
    return side, place


def names_rows(slots):
    return lax.axis_size("ray") // CORES * slots // LAT


def names_of(ref, side, slots):
    rows = names_rows(slots)
    first = lax.axis_size("ray") // CORES * slots + side * rows
    return [ref[pl.ds(first + j, 1), :].astype(jnp.int32) for j in range(rows)]


def placed_lines(ref, slots):
    place = own_place()[1]
    return jnp.concatenate(
        [
            ref[pl.ds(pl.multiple_of((j ^ place) * slots, slots), slots), :]
            for j in range(lax.axis_size("ray") // CORES)
        ],
        axis=0,
    )


def extra_row(ref, slots, at):
    first = lax.axis_size("ray") // CORES * slots
    return ref[first + at : first + at + 1, :]


def found_lines(onehot, parts):
    found = jnp.dot(onehot, parts, preferred_element_type=F32)
    return found[:, :LAT] + found[:, LAT:]


CHUNK = 128


def onehot_of(names, ids):
    return jnp.concatenate(
        [jnp.where(ids == piece, 1.0, 0.0).astype(BF16) for piece in names], axis=1
    )


def edge_of(field_ref, at):
    flat = field_ref.reshape((PAIRS + 2 * PAD) * LON_DEV, LAT)
    return flat[pl.ds(PAD * LON_DEV + at, PAIRS, stride=LON_DEV), :]


def first_half_body(slots, mine_ref, own_ref, field_ref, lines_ref, names_ref):
    names = names_of(mine_ref, own_place()[0], slots)
    for j, piece in enumerate(names):
        names_ref[pl.ds(j, 1), :] = piece
    parts = both_parts(placed_lines(mine_ref, slots))
    lines_ref[...] = found_lines(onehot_of(names, own_ref[...]), parts)
    for first in range(0, LINES, CHUNK):
        onehot = onehot_of(names, sub_iota((CHUNK, LAT)) + first)
        piece = found_lines(onehot, parts).reshape(CHUNK // LON_DEV, LON_DEV, LAT)
        field_ref[first // LON_DEV : (first + CHUNK) // LON_DEV] = piece


def first_body(slots, other_ref, half_ref, half_lines_ref, mine_ref, own_ref, pick_ref, tiles_ref,
               field_ref, lines_ref, out_ref, left_ref, names_ref):
    names = names_of(other_ref, 1 - own_place()[0], slots)
    for j, piece in enumerate(names):
        names_ref[pl.ds(j, 1), :] = piece
    parts = both_parts(placed_lines(other_ref, slots))
    lines = half_lines_ref[...] + found_lines(onehot_of(names, own_ref[...]), parts)
    lines_ref[...] = lines
    rays, part = jnp.zeros((RT, RAY_TILE), F32), slots * CHUNK // LINES
    zeros = jnp.zeros((PAD, LON_DEV, LAT), F32)
    field_ref[:PAD] = zeros
    field_ref[PAIRS + PAD :] = zeros
    square = jnp.zeros((8, LAT), F32)
    for first in range(0, LINES, CHUNK):
        onehot = onehot_of(names, sub_iota((CHUNK, LAT)) + first)
        count, pair = CHUNK // LON_DEV, first // LON_DEV
        piece = found_lines(onehot, parts).reshape(count, LON_DEV, LAT) + half_ref[pair : pair + count]
        field_ref[pair + PAD : pair + PAD + count] = piece
        square = square + jnp.sum(piece * piece, axis=0)
        rays = push_lines(rays, lines, tiles_ref, pick_ref, first // CHUNK * part, (first // CHUNK + 1) * part)
    out_ref[:RT, :] = rays
    out_ref[RT : RT + 8, :] = jnp.broadcast_to(total(square), (8, LAT))
    odd = lax.axis_index("ray") % 2
    at = jnp.where(lax.axis_index("vox") == 0, LON_DEV - 1 - odd, odd)
    out_ref[RT + 8 :, :] = edge_of(field_ref, at)
    at = CORES * names_rows(slots)
    left = extra_row(mine_ref, slots, at) + extra_row(other_ref, slots, at)
    left_ref[...] = jnp.broadcast_to(left, (8, LAT))


def second_body(slots, mine_ref, other_ref, left_ref, weight_ref, start_ref, pick_ref, tiles_ref,
                packet_ref, rays_ref, image_ref, norm_ref):
    sub = sub_iota()
    left_sq = left_ref[...]
    norm_sq = mine_ref[RT : RT + 8, :] + other_ref[RT : RT + 8, :]
    inverse = lax.rsqrt(norm_sq)
    norm = norm_sq * inverse
    weight = weight_ref[...]
    image = (mine_ref[:RT, :] + other_ref[:RT, :]) * inverse
    image_ref[...] = image
    rays = weight * image - norm / left_sq * start_ref[...]
    rays_ref[...] = rays
    norm_ref[...] = norm
    pull_lines(weight * rays, tiles_ref, pick_ref, packet_ref, slots)
    packet_ref[slots:, :] = jnp.where(sub == 0, total(rays * rays), 0.0)


def flags():
    at, count = lax.axis_index("vox"), lax.axis_size("vox")
    return (at > 0).astype(F32), (at < count - 1).astype(F32)


def smooth_body(swapped, field_ref, low_ref, low2_ref, high_ref, high2_ref, damp_ref, norm_ref,
                smooth_ref, scaled_ref, far_ref, square_ref, near_ref):
    sub, lane = sub_iota(), lane_iota()
    has_low, has_high = flags()
    inverse = 1.0 / norm_ref[...]
    col_lane, col_sub = lane_iota((PAIRS, LAT)), sub_iota((PAIRS, LAT))
    low, low2, high, high2 = low_ref[...], low2_ref[...], high_ref[...], high2_ref[...]
    if swapped:
        odd = lax.axis_index("ray") % 2 == 1
        low, low2 = jnp.where(odd, low2, low), jnp.where(odd, low, low2)
        high, high2 = low, low2
    near_ref[0] = low * has_low
    near_ref[1] = high * has_high
    scale = damp_ref[...] * damp_ref[...] * jnp.broadcast_to(inverse[:1], (PAIRS, LAT))
    far_ref[0] = scale * has_low * column_stencil(low, low2 + edge_of(field_ref, 0), col_lane, col_sub)
    far_ref[1] = scale * has_high * column_stencil(
        high, high2 + edge_of(field_ref, LON_DEV - 1), col_lane, col_sub
    )
    zeros = jnp.zeros((PAD, LON_DEV, LAT), F32)
    scaled_ref[:PAD] = zeros
    scaled_ref[PAIRS + PAD :] = zeros

    def left(pair, square):
        damped = damp_ref[pl.ds(pair, 1), :]
        value = slab_stencil(pair, field_ref, near_ref.at[0], near_ref.at[1], sub, lane) * inverse * damped
        smooth_ref[pair] = value
        scaled_ref[pair + PAD] = value * damped
        return square + value * value

    square = lax.fori_loop(0, PAIRS, left, jnp.zeros((LON_DEV, LAT), F32), unroll=UNROLL)
    square_ref[...] = jnp.broadcast_to(total(square), (8, LAT))


def onehot_body(*refs):
    names_refs, onehot_refs = refs[: len(refs) // 2], refs[len(refs) // 2 :]
    for names_ref, onehot_ref in zip(names_refs, onehot_refs):
        pieces = [names_ref[pl.ds(j, 1), :] for j in range(onehot_ref.shape[1] // LAT)]
        for first in range(0, LINES, CHUNK):
            onehot_ref[first : first + CHUNK, :] = onehot_of(pieces, sub_iota((CHUNK, LAT)) + first)


def again_body(slots, col_ref, scaled_ref, far_ref, again_ref, lines_ref):
    sub, lane = sub_iota(), lane_iota()

    def right(pair, carry):
        again_ref[pair] = slab_stencil(pair, scaled_ref, far_ref.at[0], far_ref.at[1], sub, lane)
        return carry

    lax.fori_loop(0, PAIRS, right, 0, unroll=UNROLL)
    for k in range(slots):
        col = col_ref[k]
        lines_ref[pl.ds(k, 1), :] = again_ref[col // LON_DEV, pl.ds(col % LON_DEV, 1), :]


def third_half_body(slots, mine_ref, onehot_ref, names_ref, own_ref, again_lines_ref, again_ref,
                    half_ref, lines_ref):
    parts = both_parts(placed_lines(mine_ref, slots))
    names = [names_ref[pl.ds(j, 1), :] for j in range(onehot_ref.shape[1] // LAT)]
    lines_ref[...] = found_lines(onehot_of(names, own_ref[...]), parts) + again_lines_ref[...]
    for first in range(0, LINES, CHUNK):
        count, pair = CHUNK // LON_DEV, first // LON_DEV
        piece = found_lines(onehot_ref[first : first + CHUNK, :], parts).reshape(count, LON_DEV, LAT)
        half_ref[pair : pair + count] = piece + again_ref[pair : pair + count]


def third_body(slots, other_ref, half_ref, half_lines_ref, mine_ref, square_ref, onehot_ref, names_ref, own_ref,
               lines_ref, field_ref, norm_ref, pick_ref, tiles_ref,
               next_ref, out_ref, shift_ref):
    shift = jnp.broadcast_to(extra_row(mine_ref, slots, 0) + extra_row(other_ref, slots, 0), (8, LAT))
    shift_ref[...] = shift
    inverse = 1.0 / norm_ref[...]
    back = shift * inverse
    parts = both_parts(placed_lines(other_ref, slots))
    names = [names_ref[pl.ds(j, 1), :] for j in range(onehot_ref.shape[1] // LAT)]
    lines = found_lines(onehot_of(names, own_ref[...]), parts) + half_lines_ref[...] - lines_ref[...] * back[:1]
    rays, part = jnp.zeros((RT, RAY_TILE), F32), slots * CHUNK // LINES
    zeros = jnp.zeros((PAD, LON_DEV, LAT), F32)
    next_ref[:PAD] = zeros
    next_ref[PAIRS + PAD :] = zeros
    square = jnp.zeros((8, LAT), F32)
    cross = jnp.zeros((8, LAT), F32)
    for first in range(0, LINES, CHUNK):
        count, pair = CHUNK // LON_DEV, first // LON_DEV
        piece = found_lines(onehot_ref[first : first + CHUNK, :], parts).reshape(count, LON_DEV, LAT)
        base = field_ref[pair + PAD : pair + PAD + count]
        piece = piece + half_ref[pair : pair + count] - base * back
        next_ref[pair + PAD : pair + PAD + count] = piece
        square = square + jnp.sum(piece * piece, axis=0)
        cross = cross + jnp.sum(piece * base, axis=0)
        rays = push_lines(rays, lines, tiles_ref, pick_ref, first // CHUNK * part, (first // CHUNK + 1) * part)
    sub = sub_iota()
    out_ref[:RT, :] = rays
    out_ref[RT : RT + 8, :] = jnp.where(
        sub == 0, total(square), jnp.where(sub == 1, total(cross) * inverse, square_ref[...])
    )
    edge = edge_of(next_ref, jnp.where(lax.axis_index("vox") == 0, LON_DEV - 1, 0))
    half = PAIRS // 2
    out_ref[RT + 8 :, :] = jnp.where(lax.axis_index("ray") % 2 == 0, edge[:half], edge[half:])


def fourth_body(mine_ref, other_ref, shift_ref, weight_ref, rays_ref, image_ref,
                next_rays_ref, left_ref, rest_ref, norm_ref, sum_ref):
    sums = mine_ref[RT : RT + 8, :] + other_ref[RT : RT + 8, :]
    square, cross, rest = [jnp.broadcast_to(sums[j : j + 1], (8, LAT)) for j in range(3)]
    left_sq = shift_ref[...] + rest
    norm_sq = (square - 2.0 * rest * cross + rest * rest) / left_sq
    per_left = lax.rsqrt(left_sq)
    inverse = lax.rsqrt(norm_sq)
    norm = norm_sq * inverse
    rays = mine_ref[:RT, :] + other_ref[:RT, :] - rest * image_ref[...]
    rays = weight_ref[...] * rays * (per_left * inverse) - norm * per_left * rays_ref[...]
    next_rays_ref[...] = rays
    left_ref[...] = left_sq
    rest_ref[...] = rest
    norm_ref[...] = norm
    sum_ref[...] = jnp.broadcast_to(total(rays * rays), (8, LAT))


def last_smooth_body(halves, next_ref, low_ref, high_ref, damp_ref, smooth_ref, norm_ref, left_ref, rest_ref,
                     square_ref, near_ref):
    sub, lane = sub_iota(), lane_iota()
    has_low, has_high = flags()
    if halves:
        odd, half = lax.axis_index("ray") % 2, PAIRS // 2
        for ref, at in ((low_ref, odd), (high_ref, 1 - odd)):
            near_ref[0, pl.ds(at * half, half), :] = ref[...] * has_low
            near_ref[1, pl.ds(at * half, half), :] = ref[...] * has_high
    else:
        near_ref[0] = low_ref[...] * has_low
        near_ref[1] = high_ref[...] * has_high
    norm, per_left = norm_ref[...], lax.rsqrt(left_ref[...])
    inverse = per_left / norm
    back = rest_ref[...] * inverse + norm * per_left

    def left(pair, square):
        damped = damp_ref[pl.ds(pair, 1), :]
        value = slab_stencil(pair, next_ref, near_ref.at[0], near_ref.at[1], sub, lane) * inverse * damped
        value = value - back * smooth_ref[pair]
        return square + value * value

    square = lax.fori_loop(0, PAIRS, left, jnp.zeros((LON_DEV, LAT), F32), unroll=UNROLL)
    square_ref[...] = jnp.broadcast_to(total(square), (8, LAT))


def end_body(share, parts, *refs):
    sums = refs[0][...]
    for ref in refs[1:parts]:
        sums = sums + ref[...]
    (left0_ref, norm0_ref, left1_ref, rest_ref, norm1_ref, rays_ref, field_ref, next_ref,
     density_ref, out_ref) = refs[parts:]
    left2_sq = sums
    out_ref[...] = rays_ref[...] * lax.rsqrt(left2_sq)
    left0_sq, norm0, left1_sq, right1 = left0_ref[...], norm0_ref[...], left1_ref[...], norm1_ref[...]
    left0, left1 = jnp.sqrt(left0_sq), jnp.sqrt(left1_sq)
    right0 = norm0 / left0
    diag1 = jnp.sqrt(right0 * right0 + left1_sq)
    cosine, sine = right0 / diag1, left1 / diag1
    coupling = sine * right1
    diag_bar = -cosine * right1
    step1, resid = cosine * left0, sine * left0
    diag2 = jnp.sqrt(diag_bar * diag_bar + left2_sq)
    step2 = diag_bar / diag2 * resid
    on_next = step2 / diag2 / (left1 * right1)
    on_first = (step1 / diag1 - step2 / diag2 * coupling / diag1 - on_next * rest_ref[...]) / norm0
    first = lax.axis_index("ray") * share + PAD
    for j in range(share):
        density_ref[j] = on_first * field_ref[first + j] + on_next * next_ref[first + j]


def on_device(
    tiles,
    tile_scale,
    tile_row,
    tile_col,
    tile_count,
    delays,
    ray_receiver,
    receiver_weight,
    smooth_scale,
):
    block = tiles[0, 0]
    slots = block.shape[0]
    rays_n = lax.axis_size("ray")
    col_index = tile_col[0, 0]
    held = (RT, RAY_TILE)
    row = ((8, LAT), F32)
    slab = ((PAIRS, LON_DEV, LAT), F32)
    padded = ((PAIRS + 2 * PAD, LON_DEV, LAT), F32)
    packet = ((slots + 8, LAT), F32)
    names_n = rays_n // CORES * slots // LAT
    extra = -(-(CORES * names_n + 1) // 8) * 8
    damp = jnp.broadcast_to(jnp.repeat(smooth_scale, EPOCHS)[:, None], (PAIRS, LAT))

    hbm = pl.BlockSpec(memory_space=pl.ANY)
    table = receiver_weight.shape[0]
    mine, weight, start, pick, own, block = local_call(
        functools.partial(start_body, slots), "start", [SM] + [hbm] * 7,
        [((slots + extra, LAT), F32), (held, F32), (held, F32), ((slots, RT, LAT), F32), ((slots, LAT), jnp.int32),
         (block.shape, BF16)],
        [pltpu.SMEM((slots,), jnp.int32), pltpu.SMEM((slots,), jnp.int32), pltpu.SMEM((slots,), F32),
         pltpu.SMEM((table,), F32), pltpu.VMEM(held, jnp.int32),
         pltpu.VMEM(held, F32), pltpu.SemaphoreType.DMA((7,))],
    )(tile_count, *(pltpu.with_memory_space_constraint(x, pltpu.MemorySpace.HBM) for x in (
        tile_row[0, 0], col_index, tile_scale[0, 0], receiver_weight,
        ray_receiver.reshape(held), delays.reshape(held), block)))
    near, far, damp = gather_rays(mine, extra, (lambda _: damp,))
    named = ((names_n, LAT), jnp.int32)

    half, half_lines, names_a = local_call(
        functools.partial(first_half_body, slots), "first_half", [VM] * 2,
        [slab, ((slots, LAT), F32), named],
    )(near, own)
    field, lines, sums, left0, names_b = local_call(
        functools.partial(first_body, slots), "first", [VM] * 7,
        [padded, ((slots, LAT), F32), ((RT + 8 + PAIRS, LAT), F32), row, named],
    )(far, half, half_lines, near, own, pick, block)
    others, columns, swapped = first_halo(sums, field)
    onehots = local_call(
        onehot_body, "onehot", [VM] * 2, [((LINES, names_n * LAT), BF16)] * 2,
    )(names_a, names_b)
    others, (onehot_a, onehot_b) = lax.optimization_barrier((others, onehots))

    mine, rays, image, norm0 = local_call(
        functools.partial(second_body, slots), "second", [VM] * 7, [packet, (held, F32), (held, F32), row],
    )(sums, others, left0, weight, start, pick, block)
    def smooth_step(columns):
        return local_call(
            functools.partial(smooth_body, swapped), "smooth", [VM] * 7,
            [slab, padded, ((2, PAIRS, LAT), F32), row], [pltpu.VMEM((2, PAIRS, LAT), F32)],
        )(field, *columns, damp, norm0)

    def again_step(given):
        smooth, scaled, beside, square = given
        again, again_lines = local_call(
            functools.partial(again_body, slots), "again", [SM] + [VM] * 2, [slab, ((slots, LAT), F32)],
        )(col_index, scaled, beside)
        return smooth, square, again, again_lines

    near, far, given = gather_rays(mine, 8, (lambda _: columns, smooth_step, again_step))
    smooth, square, again, again_lines = given

    half, half_lines = local_call(
        functools.partial(third_half_body, slots), "third_half", [VM] * 6, [slab, ((slots, LAT), F32)],
    )(near, onehot_a, names_a, own, again_lines, again)
    following, sums, shift = local_call(
        functools.partial(third_body, slots), "third", [VM] * 13,
        [padded, ((RT + 8 + PAIRS // 2, LAT), F32), row],
    )(far, half, half_lines, near, square, onehot_b, names_b, own, lines, field, norm0, pick, block)
    others, beside, halves = next_halo(sums, following)
    last_rays, left1, rest, norm1, ray_square = local_call(
        fourth_body, "fourth", [VM] * 6, [(held, F32), row, row, row, row],
    )(sums, others, shift, weight, rays, image)

    def last_step(beside):
        return local_call(
            functools.partial(last_smooth_body, halves), "last_smooth", [VM] * 8, [row], [pltpu.VMEM((2, PAIRS, LAT), F32)],
        )(following, *beside, damp, smooth, norm1, left1, rest)[0]

    shares = last_sums(ray_square, beside, last_step)

    share = PAIRS // rays_n
    density, rays_out = local_call(
        functools.partial(end_body, share, len(shares)), "end", [VM] * (len(shares) + 8),
        [((share, LON_DEV, LAT), F32), (held, F32)],
    )(*shares, left0, norm0, left1, rest, norm1, last_rays, field, following)
    return (density.reshape(ALT // rays_n, EPOCHS, LON_DEV, LAT), rays_out.reshape(-1))


def solution(mesh):
    in_specs = (
        P("ray", "vox", None, None, None),
        P("ray", "vox", None),
        P("ray", "vox", None),
        P("ray", "vox", None),
        P("ray", "vox"),
        P("ray"),
        P("ray"),
        P("ray"),
        P(),
    )
    out_specs = (P("ray", None, "vox", None), P("ray"))
    return jax.shard_map(
        on_device, mesh=mesh, in_specs=in_specs, out_specs=out_specs, check_vma=False
    )
```

```python
import functools

import jax
import jax.numpy as jnp
from jax import lax
from jax.experimental import pallas as pl
from jax.experimental.pallas import tpu as pltpu
from jax.sharding import PartitionSpec as P

ALT = 64
EPOCHS = 2
LAT = 128
LON_DEV = 8
RAY_TILE = 128
RT = 8
CORES = 2
PAIRS = ALT * EPOCHS
LINES = PAIRS * LON_DEV
PAD = EPOCHS
UNROLL = 32

LATERAL = 1.0
VERTICAL = 4.0
TEMPORAL = 0.5
CENTRE = 2.0 * (2.0 * LATERAL + VERTICAL + TEMPORAL)

F32 = jnp.float32
BF16 = jnp.bfloat16
VM = pl.BlockSpec(memory_space=pltpu.VMEM)
SM = pl.BlockSpec(memory_space=pltpu.SMEM)


def local_call(body, name, in_specs, out_shapes, scratch=()):
    return pl.pallas_call(
        body,
        name=name,
        in_specs=in_specs,
        out_specs=[VM] * len(out_shapes),
        out_shape=[jax.ShapeDtypeStruct(shape, dtype) for shape, dtype in out_shapes],
        scratch_shapes=list(scratch),
        compiler_params=pltpu.CompilerParams(vmem_limit_bytes=32 << 20),
    )


def pairs_of(count, step):
    return [(i, i ^ step) for i in range(count)]


def hops(count):
    steps = []
    while count > 1:
        count //= 2
        steps.append(count | 1)
    return steps


def gather_rays(packet, extra, during=()):
    count = lax.axis_size("ray")
    if count < 2 or count & (count - 1):
        raise ValueError("ray size")
    done, given = list(during), None
    for step in hops(count):
        other = lax.ppermute(packet, "ray", pairs_of(count, step))
        if step == 1:
            break
        joined = jnp.concatenate(
            [packet[:-extra], other[:-extra], packet[-extra:] + other[-extra:]], axis=0
        )
        if done:
            given = done.pop(0)(given)
            joined, given = lax.optimization_barrier((joined, given))
        packet = joined
    while done:
        given = done.pop(0)(given)
    return packet, other, given


def vox_others(value):
    count = lax.axis_size("vox")
    if count == 1:
        return jnp.zeros_like(value)
    if count == 2:
        return lax.ppermute(value, "vox", [(0, 1), (1, 0)])
    return lax.psum(value, "vox") - value


def last_sums(value, given, step_of):
    count, slabs = lax.axis_size("ray"), lax.axis_size("vox")
    if slabs != 2 or count & (count - 1) or count < 16:
        mine = step_of(given)
        return lax.psum(value, "ray"), mine, vox_others(mine)
    for step in hops(count)[:-2]:
        value = value + lax.ppermute(value, "ray", pairs_of(count, step))
        if step == count // 4 | 1:
            given = step_of(given)
        value, given = lax.optimization_barrier((value, given))
    mine = given
    both = jnp.concatenate([value, mine], axis=0)
    both = lax.ppermute(both, ("ray", "vox"), [(i, i ^ 7) for i in range(2 * count)])
    value = value + both[:8]
    return value, lax.ppermute(value, "ray", pairs_of(count, 1)), mine, both[8:]


def halo_of(low_edge, high_edge):
    count = lax.axis_size("vox")
    if count == 1:
        return jnp.zeros_like(high_edge), jnp.zeros_like(low_edge)
    forward = [(i, i + 1) for i in range(count - 1)]
    backward = [(target, source) for source, target in forward]
    return lax.ppermute(high_edge, "vox", forward), lax.ppermute(low_edge, "vox", backward)


def first_halo(sums, field):
    if lax.axis_size("vox") == 2 and lax.axis_size("ray") % 2 == 0:
        other = lax.ppermute(sums, "vox", [(0, 1), (1, 0)])
        column = other[RT + 8 :]
        partner = lax.ppermute(column, "ray", pairs_of(lax.axis_size("ray"), 1))
        return other, (column, partner, column, partner), True
    low = halo_of(field[PAD:-PAD, 0], field[PAD:-PAD, -1])
    far = halo_of(field[PAD:-PAD, 1], field[PAD:-PAD, -2])
    return vox_others(sums), (low[0], far[0], low[1], far[1]), False


def next_halo(sums, field):
    if lax.axis_size("vox") == 2 and lax.axis_size("ray") % 2 == 0:
        other = lax.ppermute(sums, "vox", [(0, 1), (1, 0)])
        half = other[RT + 8 :]
        return other, (half, lax.ppermute(half, "ray", pairs_of(lax.axis_size("ray"), 1))), True
    return vox_others(sums), halo_of(field[PAD:-PAD, 0], field[PAD:-PAD, -1]), False


def total(values):
    return jnp.sum(values, axis=(0, 1), keepdims=True)


def sub_iota(shape=(8, LAT)):
    return lax.broadcasted_iota(jnp.int32, shape, 0)


def lane_iota(shape=(8, LAT)):
    return lax.broadcasted_iota(jnp.int32, shape, 1)


def pull_lines(weighted, tiles_ref, pick_ref, out_ref, slots):
    rays = weighted.astype(BF16)
    for k in range(0, slots, 2):
        pair = jnp.concatenate([tiles_ref[k], tiles_ref[k + 1]], axis=1)
        product = jnp.dot(rays, pair, preferred_element_type=F32)
        out_ref[pl.ds(k, 1), :] = jnp.sum(pick_ref[k] * product[:, :LAT], axis=0, keepdims=True)
        out_ref[pl.ds(k + 1, 1), :] = jnp.sum(pick_ref[k + 1] * product[:, LAT:], axis=0, keepdims=True)


def push_lines(rays, lines, turned_ref, pick_ref, first, last):
    for k in range(first, last, 2):
        both = [jnp.broadcast_to(lines[j : j + 1], (RT, LAT)) for j in (k, k + 1)]
        pair = jnp.concatenate([turned_ref[k], turned_ref[k + 1]], axis=1)
        product = jnp.dot(
            jnp.concatenate(both, axis=0).astype(BF16), pair, preferred_element_type=F32
        )
        rays = rays + pick_ref[k] * product[:RT, :RAY_TILE]
        rays = rays + pick_ref[k + 1] * product[RT:, RAY_TILE:]
    return rays


def both_parts(lines):
    high = lines.astype(BF16)
    low = (lines - high.astype(F32)).astype(BF16)
    return jnp.concatenate([high, low], axis=1)


def across(values, sub, lane):
    up = jnp.where(lane == 0, 0.0, pltpu.roll(values, 1, 1))
    down = jnp.where(lane == LAT - 1, 0.0, pltpu.roll(values, LAT - 1, 1))
    return up + down


def column_stencil(column, beside, lane, sub):
    up = jnp.where(sub < EPOCHS, 0.0, pltpu.roll(column, EPOCHS, 0))
    down = jnp.where(sub >= PAIRS - EPOCHS, 0.0, pltpu.roll(column, PAIRS - EPOCHS, 0))
    later = pltpu.roll(column, PAIRS - 1, 0)
    earlier = pltpu.roll(column, 1, 0)
    epoch = jnp.where(sub % EPOCHS == 0, later, earlier)
    return (
        CENTRE * column
        - LATERAL * (beside + across(column, sub, lane))
        - VERTICAL * (up + down)
        - TEMPORAL * epoch
    )


def slab_stencil(pair, field_ref, low_ref, high_ref, sub, lane):
    here = field_ref[pair + PAD]
    below = jnp.where(sub == 0, low_ref[pl.ds(pair, 1), :], pltpu.roll(here, 1, 0))
    above = jnp.where(sub == LON_DEV - 1, high_ref[pl.ds(pair, 1), :], pltpu.roll(here, LON_DEV - 1, 0))
    epoch = field_ref[(pair ^ 1) + PAD]
    return (
        CENTRE * here
        - LATERAL * (below + above + across(here, sub, lane))
        - VERTICAL * (field_ref[pair] + field_ref[pair + 2 * PAD])
        - TEMPORAL * epoch
    )


def start_body(slots, count_ref, row_in, col_in, scale_in, table_in, receiver_in, delays_in, tiles_in,
               packet_ref, weight_ref, start_ref, pick_ref, own_ref, tiles_ref,
               row_ref, col_ref, scale_ref, table_ref, receiver_ref, delays_ref, sems):
    copies = [
        pltpu.make_async_copy(source, target, sems.at[j])
        for j, (source, target) in enumerate([
            (receiver_in, receiver_ref), (table_in, table_ref), (delays_in, delays_ref),
            (scale_in, scale_ref), (row_in, row_ref), (col_in, col_ref),
        ])
    ]
    pull = pltpu.make_async_copy(tiles_in, tiles_ref, sems.at[6])
    pull.start()
    for copy in copies:
        copy.start()
    for copy in copies:
        copy.wait()
    sub, lane = sub_iota(), lane_iota()
    receivers = receiver_ref[...]
    weight = jnp.zeros((RT, RAY_TILE), F32)
    for j in range(table_ref.shape[0]):
        weight = jnp.where(receivers == j, table_ref[j], weight)
    weight_ref[...] = weight
    start = weight * delays_ref[...]
    start_ref[...] = start
    extra = packet_ref.shape[0] - slots
    sub_x, lane_x = sub_iota((extra, LAT)), lane_iota((extra, LAT))
    side, place = own_place()
    rows, per = names_rows(slots), LAT // slots
    first = place % per * slots
    names = jnp.zeros((1, LAT), jnp.int32)
    for k in range(slots):
        live = jnp.where(k < count_ref[0, 0], scale_ref[k], 0.0)
        pick_ref[k] = jnp.where(sub == row_ref[k], live, 0.0)
        own_ref[pl.ds(k, 1), :] = jnp.full((1, LAT), col_ref[k], jnp.int32)
        names = jnp.where(lane[:1] == first + k, col_ref[k], names)
    square = total(start * start)
    packet_ref[slots:, :] = jnp.where(
        sub_x == side * rows + place // per,
        jnp.broadcast_to(names.astype(F32), (extra, LAT)),
        jnp.where(sub_x == CORES * rows, square, 0.0),
    )
    pull.wait()
    pull_lines(weight * start, tiles_ref, pick_ref, packet_ref, slots)


def turn_body(tiles_ref, turned_ref):
    for k in range(tiles_ref.shape[0]):
        turned_ref[k] = tiles_ref[k].T


def own_place():
    count, at = lax.axis_size("ray"), lax.axis_index("ray")
    side, place, bit = at % 2, 0, 1
    for step in hops(count)[:-1]:
        digit = at // (step - 1) % 2
        side = (side + digit) % 2
        place = place + bit * digit
        bit *= 2
    return side, place


def names_rows(slots):
    return lax.axis_size("ray") // CORES * slots // LAT


def names_of(ref, side, slots):
    rows = names_rows(slots)
    first = lax.axis_size("ray") // CORES * slots + side * rows
    return [ref[pl.ds(first + j, 1), :].astype(jnp.int32) for j in range(rows)]


def placed_lines(ref, slots):
    place = own_place()[1]
    return jnp.concatenate(
        [
            ref[pl.ds(pl.multiple_of((j ^ place) * slots, slots), slots), :]
            for j in range(lax.axis_size("ray") // CORES)
        ],
        axis=0,
    )


def extra_row(ref, slots, at):
    first = lax.axis_size("ray") // CORES * slots
    return ref[first + at : first + at + 1, :]


def found_lines(onehot, parts):
    found = jnp.dot(onehot, parts, preferred_element_type=F32)
    return found[:, :LAT] + found[:, LAT:]


CHUNK = 256


def onehot_of(names, ids):
    return jnp.concatenate(
        [jnp.where(ids == piece, 1.0, 0.0).astype(BF16) for piece in names], axis=1
    )


def edge_of(field_ref, at):
    flat = field_ref.reshape((PAIRS + 2 * PAD) * LON_DEV, LAT)
    return flat[pl.ds(PAD * LON_DEV + at, PAIRS, stride=LON_DEV), :]


def first_half_body(slots, mine_ref, own_ref, field_ref, lines_ref, names_ref):
    names = names_of(mine_ref, own_place()[0], slots)
    for j, piece in enumerate(names):
        names_ref[pl.ds(j, 1), :] = piece
    parts = both_parts(placed_lines(mine_ref, slots))
    lines_ref[...] = found_lines(onehot_of(names, own_ref[...]), parts)
    for first in range(0, LINES, CHUNK):
        onehot = onehot_of(names, sub_iota((CHUNK, LAT)) + first)
        piece = found_lines(onehot, parts).reshape(CHUNK // LON_DEV, LON_DEV, LAT)
        field_ref[first // LON_DEV : (first + CHUNK) // LON_DEV] = piece


def first_body(slots, other_ref, half_ref, half_lines_ref, mine_ref, own_ref, pick_ref, turned_ref,
               field_ref, lines_ref, out_ref, left_ref, names_ref):
    names = names_of(other_ref, 1 - own_place()[0], slots)
    for j, piece in enumerate(names):
        names_ref[pl.ds(j, 1), :] = piece
    parts = both_parts(placed_lines(other_ref, slots))
    lines = half_lines_ref[...] + found_lines(onehot_of(names, own_ref[...]), parts)
    lines_ref[...] = lines
    rays, part = jnp.zeros((RT, RAY_TILE), F32), slots * CHUNK // LINES
    zeros = jnp.zeros((PAD, LON_DEV, LAT), F32)
    field_ref[:PAD] = zeros
    field_ref[PAIRS + PAD :] = zeros
    square = jnp.zeros((8, LAT), F32)
    for first in range(0, LINES, CHUNK):
        onehot = onehot_of(names, sub_iota((CHUNK, LAT)) + first)
        count, pair = CHUNK // LON_DEV, first // LON_DEV
        piece = found_lines(onehot, parts).reshape(count, LON_DEV, LAT) + half_ref[pair : pair + count]
        field_ref[pair + PAD : pair + PAD + count] = piece
        square = square + jnp.sum(piece * piece, axis=0)
        rays = push_lines(rays, lines, turned_ref, pick_ref, first // CHUNK * part, (first // CHUNK + 1) * part)
    out_ref[:RT, :] = rays
    out_ref[RT : RT + 8, :] = jnp.broadcast_to(total(square), (8, LAT))
    odd = lax.axis_index("ray") % 2
    at = jnp.where(lax.axis_index("vox") == 0, LON_DEV - 1 - odd, odd)
    out_ref[RT + 8 :, :] = edge_of(field_ref, at)
    at = CORES * names_rows(slots)
    left = extra_row(mine_ref, slots, at) + extra_row(other_ref, slots, at)
    left_ref[...] = jnp.broadcast_to(left, (8, LAT))


def second_body(slots, mine_ref, other_ref, left_ref, weight_ref, start_ref, pick_ref, tiles_ref,
                packet_ref, rays_ref, image_ref, norm_ref):
    sub = sub_iota()
    left_sq = left_ref[...]
    norm_sq = mine_ref[RT : RT + 8, :] + other_ref[RT : RT + 8, :]
    inverse = lax.rsqrt(norm_sq)
    norm = norm_sq * inverse
    weight = weight_ref[...]
    image = (mine_ref[:RT, :] + other_ref[:RT, :]) * inverse
    image_ref[...] = image
    rays = weight * image - norm / left_sq * start_ref[...]
    rays_ref[...] = rays
    norm_ref[...] = norm
    pull_lines(weight * rays, tiles_ref, pick_ref, packet_ref, slots)
    packet_ref[slots:, :] = jnp.where(sub == 0, total(rays * rays), 0.0)


def flags():
    at, count = lax.axis_index("vox"), lax.axis_size("vox")
    return (at > 0).astype(F32), (at < count - 1).astype(F32)


def smooth_body(swapped, field_ref, low_ref, low2_ref, high_ref, high2_ref, damp_ref, norm_ref,
                smooth_ref, scaled_ref, far_ref, square_ref, near_ref):
    sub, lane = sub_iota(), lane_iota()
    has_low, has_high = flags()
    inverse = 1.0 / norm_ref[...]
    col_lane, col_sub = lane_iota((PAIRS, LAT)), sub_iota((PAIRS, LAT))
    low, low2, high, high2 = low_ref[...], low2_ref[...], high_ref[...], high2_ref[...]
    if swapped:
        odd = lax.axis_index("ray") % 2 == 1
        low, low2 = jnp.where(odd, low2, low), jnp.where(odd, low, low2)
        high, high2 = low, low2
    near_ref[0] = low * has_low
    near_ref[1] = high * has_high
    scale = damp_ref[...] * damp_ref[...] * jnp.broadcast_to(inverse[:1], (PAIRS, LAT))
    far_ref[0] = scale * has_low * column_stencil(low, low2 + edge_of(field_ref, 0), col_lane, col_sub)
    far_ref[1] = scale * has_high * column_stencil(
        high, high2 + edge_of(field_ref, LON_DEV - 1), col_lane, col_sub
    )
    zeros = jnp.zeros((PAD, LON_DEV, LAT), F32)
    scaled_ref[:PAD] = zeros
    scaled_ref[PAIRS + PAD :] = zeros

    def left(pair, square):
        damped = damp_ref[pl.ds(pair, 1), :]
        value = slab_stencil(pair, field_ref, near_ref.at[0], near_ref.at[1], sub, lane) * inverse * damped
        smooth_ref[pair] = value
        scaled_ref[pair + PAD] = value * damped
        return square + value * value

    square = lax.fori_loop(0, PAIRS, left, jnp.zeros((LON_DEV, LAT), F32), unroll=UNROLL)
    square_ref[...] = jnp.broadcast_to(total(square), (8, LAT))


def onehot_body(*refs):
    names_refs, onehot_refs = refs[: len(refs) // 2], refs[len(refs) // 2 :]
    for names_ref, onehot_ref in zip(names_refs, onehot_refs):
        pieces = [names_ref[pl.ds(j, 1), :] for j in range(onehot_ref.shape[1] // LAT)]
        for first in range(0, LINES, CHUNK):
            onehot_ref[first : first + CHUNK, :] = onehot_of(pieces, sub_iota((CHUNK, LAT)) + first)


def again_body(slots, col_ref, scaled_ref, far_ref, again_ref, lines_ref):
    sub, lane = sub_iota(), lane_iota()

    def right(pair, carry):
        again_ref[pair] = slab_stencil(pair, scaled_ref, far_ref.at[0], far_ref.at[1], sub, lane)
        return carry

    lax.fori_loop(0, PAIRS, right, 0, unroll=UNROLL)
    for k in range(slots):
        col = col_ref[k]
        lines_ref[pl.ds(k, 1), :] = again_ref[col // LON_DEV, pl.ds(col % LON_DEV, 1), :]


def third_half_body(slots, mine_ref, onehot_ref, names_ref, own_ref, again_lines_ref, again_ref,
                    half_ref, lines_ref):
    parts = both_parts(placed_lines(mine_ref, slots))
    names = [names_ref[pl.ds(j, 1), :] for j in range(onehot_ref.shape[1] // LAT)]
    lines_ref[...] = found_lines(onehot_of(names, own_ref[...]), parts) + again_lines_ref[...]
    for first in range(0, LINES, CHUNK):
        count, pair = CHUNK // LON_DEV, first // LON_DEV
        piece = found_lines(onehot_ref[first : first + CHUNK, :], parts).reshape(count, LON_DEV, LAT)
        half_ref[pair : pair + count] = piece + again_ref[pair : pair + count]


def third_body(slots, other_ref, half_ref, half_lines_ref, mine_ref, square_ref, onehot_ref, names_ref, own_ref,
               lines_ref, field_ref, norm_ref, pick_ref, turned_ref,
               next_ref, out_ref, shift_ref):
    shift = jnp.broadcast_to(extra_row(mine_ref, slots, 0) + extra_row(other_ref, slots, 0), (8, LAT))
    shift_ref[...] = shift
    inverse = 1.0 / norm_ref[...]
    back = shift * inverse
    parts = both_parts(placed_lines(other_ref, slots))
    names = [names_ref[pl.ds(j, 1), :] for j in range(onehot_ref.shape[1] // LAT)]
    lines = found_lines(onehot_of(names, own_ref[...]), parts) + half_lines_ref[...] - lines_ref[...] * back[:1]
    rays, part = jnp.zeros((RT, RAY_TILE), F32), slots * CHUNK // LINES
    zeros = jnp.zeros((PAD, LON_DEV, LAT), F32)
    next_ref[:PAD] = zeros
    next_ref[PAIRS + PAD :] = zeros
    square = jnp.zeros((8, LAT), F32)
    cross = jnp.zeros((8, LAT), F32)
    for first in range(0, LINES, CHUNK):
        count, pair = CHUNK // LON_DEV, first // LON_DEV
        piece = found_lines(onehot_ref[first : first + CHUNK, :], parts).reshape(count, LON_DEV, LAT)
        base = field_ref[pair + PAD : pair + PAD + count]
        piece = piece + half_ref[pair : pair + count] - base * back
        next_ref[pair + PAD : pair + PAD + count] = piece
        square = square + jnp.sum(piece * piece, axis=0)
        cross = cross + jnp.sum(piece * base, axis=0)
        rays = push_lines(rays, lines, turned_ref, pick_ref, first // CHUNK * part, (first // CHUNK + 1) * part)
    sub = sub_iota()
    out_ref[:RT, :] = rays
    out_ref[RT : RT + 8, :] = jnp.where(
        sub == 0, total(square), jnp.where(sub == 1, total(cross) * inverse, square_ref[...])
    )
    edge = edge_of(next_ref, jnp.where(lax.axis_index("vox") == 0, LON_DEV - 1, 0))
    half = PAIRS // 2
    out_ref[RT + 8 :, :] = jnp.where(lax.axis_index("ray") % 2 == 0, edge[:half], edge[half:])


def fourth_body(mine_ref, other_ref, shift_ref, weight_ref, rays_ref, image_ref,
                next_rays_ref, left_ref, rest_ref, norm_ref, sum_ref):
    sums = mine_ref[RT : RT + 8, :] + other_ref[RT : RT + 8, :]
    square, cross, rest = [jnp.broadcast_to(sums[j : j + 1], (8, LAT)) for j in range(3)]
    left_sq = shift_ref[...] + rest
    norm_sq = (square - 2.0 * rest * cross + rest * rest) / left_sq
    per_left = lax.rsqrt(left_sq)
    inverse = lax.rsqrt(norm_sq)
    norm = norm_sq * inverse
    rays = mine_ref[:RT, :] + other_ref[:RT, :] - rest * image_ref[...]
    rays = weight_ref[...] * rays * (per_left * inverse) - norm * per_left * rays_ref[...]
    next_rays_ref[...] = rays
    left_ref[...] = left_sq
    rest_ref[...] = rest
    norm_ref[...] = norm
    sum_ref[...] = jnp.broadcast_to(total(rays * rays), (8, LAT))


def last_smooth_body(halves, next_ref, low_ref, high_ref, damp_ref, smooth_ref, norm_ref, left_ref, rest_ref,
                     square_ref, near_ref):
    sub, lane = sub_iota(), lane_iota()
    has_low, has_high = flags()
    if halves:
        odd, half = lax.axis_index("ray") % 2, PAIRS // 2
        for ref, at in ((low_ref, odd), (high_ref, 1 - odd)):
            near_ref[0, pl.ds(at * half, half), :] = ref[...] * has_low
            near_ref[1, pl.ds(at * half, half), :] = ref[...] * has_high
    else:
        near_ref[0] = low_ref[...] * has_low
        near_ref[1] = high_ref[...] * has_high
    norm, per_left = norm_ref[...], lax.rsqrt(left_ref[...])
    inverse = per_left / norm
    back = rest_ref[...] * inverse + norm * per_left

    def left(pair, square):
        damped = damp_ref[pl.ds(pair, 1), :]
        value = slab_stencil(pair, next_ref, near_ref.at[0], near_ref.at[1], sub, lane) * inverse * damped
        value = value - back * smooth_ref[pair]
        return square + value * value

    square = lax.fori_loop(0, PAIRS, left, jnp.zeros((LON_DEV, LAT), F32), unroll=UNROLL)
    square_ref[...] = jnp.broadcast_to(total(square), (8, LAT))


def end_body(share, parts, *refs):
    sums = refs[0][...]
    for ref in refs[1:parts]:
        sums = sums + ref[...]
    (left0_ref, norm0_ref, left1_ref, rest_ref, norm1_ref, rays_ref, field_ref, next_ref,
     density_ref, out_ref) = refs[parts:]
    left2_sq = sums
    out_ref[...] = rays_ref[...] * lax.rsqrt(left2_sq)
    left0_sq, norm0, left1_sq, right1 = left0_ref[...], norm0_ref[...], left1_ref[...], norm1_ref[...]
    left0, left1 = jnp.sqrt(left0_sq), jnp.sqrt(left1_sq)
    right0 = norm0 / left0
    diag1 = jnp.sqrt(right0 * right0 + left1_sq)
    cosine, sine = right0 / diag1, left1 / diag1
    coupling = sine * right1
    diag_bar = -cosine * right1
    step1, resid = cosine * left0, sine * left0
    diag2 = jnp.sqrt(diag_bar * diag_bar + left2_sq)
    step2 = diag_bar / diag2 * resid
    on_next = step2 / diag2 / (left1 * right1)
    on_first = (step1 / diag1 - step2 / diag2 * coupling / diag1 - on_next * rest_ref[...]) / norm0
    first = lax.axis_index("ray") * share + PAD
    for j in range(share):
        density_ref[j] = on_first * field_ref[first + j] + on_next * next_ref[first + j]


def on_device(
    tiles,
    tile_scale,
    tile_row,
    tile_col,
    tile_count,
    delays,
    ray_receiver,
    receiver_weight,
    smooth_scale,
):
    block = tiles[0, 0]
    slots = block.shape[0]
    rays_n = lax.axis_size("ray")
    col_index = tile_col[0, 0]
    held = (RT, RAY_TILE)
    row = ((8, LAT), F32)
    slab = ((PAIRS, LON_DEV, LAT), F32)
    padded = ((PAIRS + 2 * PAD, LON_DEV, LAT), F32)
    packet = ((slots + 8, LAT), F32)
    names_n = rays_n // CORES * slots // LAT
    extra = -(-(CORES * names_n + 1) // 8) * 8
    damp = jnp.broadcast_to(jnp.repeat(smooth_scale, EPOCHS)[:, None], (PAIRS, LAT))

    hbm = pl.BlockSpec(memory_space=pl.ANY)
    table = receiver_weight.shape[0]
    mine, weight, start, pick, own, block = local_call(
        functools.partial(start_body, slots), "start", [SM] + [hbm] * 7,
        [((slots + extra, LAT), F32), (held, F32), (held, F32), ((slots, RT, LAT), F32), ((slots, LAT), jnp.int32),
         (block.shape, BF16)],
        [pltpu.SMEM((slots,), jnp.int32), pltpu.SMEM((slots,), jnp.int32), pltpu.SMEM((slots,), F32),
         pltpu.SMEM((table,), F32), pltpu.VMEM(held, jnp.int32),
         pltpu.VMEM(held, F32), pltpu.SemaphoreType.DMA((7,))],
    )(tile_count, *(pltpu.with_memory_space_constraint(x, pltpu.MemorySpace.HBM) for x in (
        tile_row[0, 0], col_index, tile_scale[0, 0], receiver_weight,
        ray_receiver.reshape(held), delays.reshape(held), block)))
    turn = lambda given: (given, *local_call(turn_body, "turn", [VM], [(block.shape, BF16)])(block))
    near, far, (damp, turned) = gather_rays(mine, extra, (lambda _: damp, turn))
    named = ((names_n, LAT), jnp.int32)

    half, half_lines, names_a = local_call(
        functools.partial(first_half_body, slots), "first_half", [VM] * 2,
        [slab, ((slots, LAT), F32), named],
    )(near, own)
    field, lines, sums, left0, names_b = local_call(
        functools.partial(first_body, slots), "first", [VM] * 7,
        [padded, ((slots, LAT), F32), ((RT + 8 + PAIRS, LAT), F32), row, named],
    )(far, half, half_lines, near, own, pick, turned)
    others, columns, swapped = first_halo(sums, field)
    onehots = local_call(
        onehot_body, "onehot", [VM] * 2, [((LINES, names_n * LAT), BF16)] * 2,
    )(names_a, names_b)
    others, (onehot_a, onehot_b) = lax.optimization_barrier((others, onehots))

    mine, rays, image, norm0 = local_call(
        functools.partial(second_body, slots), "second", [VM] * 7, [packet, (held, F32), (held, F32), row],
    )(sums, others, left0, weight, start, pick, block)
    def smooth_step(columns):
        return local_call(
            functools.partial(smooth_body, swapped), "smooth", [VM] * 7,
            [slab, padded, ((2, PAIRS, LAT), F32), row], [pltpu.VMEM((2, PAIRS, LAT), F32)],
        )(field, *columns, damp, norm0)

    def again_step(given):
        smooth, scaled, beside, square = given
        again, again_lines = local_call(
            functools.partial(again_body, slots), "again", [SM] + [VM] * 2, [slab, ((slots, LAT), F32)],
        )(col_index, scaled, beside)
        return smooth, square, again, again_lines

    near, far, given = gather_rays(mine, 8, (lambda _: columns, smooth_step, again_step))
    smooth, square, again, again_lines = given

    half, half_lines = local_call(
        functools.partial(third_half_body, slots), "third_half", [VM] * 6, [slab, ((slots, LAT), F32)],
    )(near, onehot_a, names_a, own, again_lines, again)
    following, sums, shift = local_call(
        functools.partial(third_body, slots), "third", [VM] * 13,
        [padded, ((RT + 8 + PAIRS // 2, LAT), F32), row],
    )(far, half, half_lines, near, square, onehot_b, names_b, own, lines, field, norm0, pick, turned)
    others, beside, halves = next_halo(sums, following)
    last_rays, left1, rest, norm1, ray_square = local_call(
        fourth_body, "fourth", [VM] * 6, [(held, F32), row, row, row, row],
    )(sums, others, shift, weight, rays, image)

    def last_step(beside):
        return local_call(
            functools.partial(last_smooth_body, halves), "last_smooth", [VM] * 8, [row], [pltpu.VMEM((2, PAIRS, LAT), F32)],
        )(following, *beside, damp, smooth, norm1, left1, rest)[0]

    shares = last_sums(ray_square, beside, last_step)

    share = PAIRS // rays_n
    density, rays_out = local_call(
        functools.partial(end_body, share, len(shares)), "end", [VM] * (len(shares) + 8),
        [((share, LON_DEV, LAT), F32), (held, F32)],
    )(*shares, left0, norm0, left1, rest, norm1, last_rays, field, following)
    return (density.reshape(ALT // rays_n, EPOCHS, LON_DEV, LAT), rays_out.reshape(-1))


def solution(mesh):
    in_specs = (
        P("ray", "vox", None, None, None),
        P("ray", "vox", None),
        P("ray", "vox", None),
        P("ray", "vox", None),
        P("ray", "vox"),
        P("ray"),
        P("ray"),
        P("ray"),
        P(),
    )
    out_specs = (P("ray", None, "vox", None), P("ray"))
    return jax.shard_map(
        on_device, mesh=mesh, in_specs=in_specs, out_specs=out_specs, check_vma=False
    )
```

```python
import functools

import jax
import jax.numpy as jnp
from jax import lax
from jax.experimental import pallas as pl
from jax.experimental.pallas import tpu as pltpu
from jax.sharding import PartitionSpec as P

ALT = 64
EPOCHS = 2
LAT = 128
LON_DEV = 8
RAY_TILE = 128
RT = 8
CORES = 2
PAIRS = ALT * EPOCHS
LINES = PAIRS * LON_DEV
PAD = EPOCHS
UNROLL = 32

LATERAL = 1.0
VERTICAL = 4.0
TEMPORAL = 0.5
CENTRE = 2.0 * (2.0 * LATERAL + VERTICAL + TEMPORAL)

F32 = jnp.float32
BF16 = jnp.bfloat16
VM = pl.BlockSpec(memory_space=pltpu.VMEM)
SM = pl.BlockSpec(memory_space=pltpu.SMEM)


def local_call(body, name, in_specs, out_shapes, scratch=()):
    return pl.pallas_call(
        body,
        name=name,
        in_specs=in_specs,
        out_specs=[VM] * len(out_shapes),
        out_shape=[jax.ShapeDtypeStruct(shape, dtype) for shape, dtype in out_shapes],
        scratch_shapes=list(scratch),
        compiler_params=pltpu.CompilerParams(vmem_limit_bytes=32 << 20),
    )


def pairs_of(count, step):
    return [(i, i ^ step) for i in range(count)]


def hops(count):
    steps = []
    while count > 1:
        count //= 2
        steps.append(count | 1)
    return steps


def gather_rays(packet, extra, during=()):
    count = lax.axis_size("ray")
    if count < 2 or count & (count - 1):
        raise ValueError("ray size")
    done, given = list(during), None
    for step in hops(count):
        other = lax.ppermute(packet, "ray", pairs_of(count, step))
        if step == 1:
            break
        joined = jnp.concatenate(
            [packet[:-extra], other[:-extra], packet[-extra:] + other[-extra:]], axis=0
        )
        if done:
            given = done.pop(0)(given)
            joined, given = lax.optimization_barrier((joined, given))
        packet = joined
    while done:
        given = done.pop(0)(given)
    return packet, other, given


def vox_others(value):
    count = lax.axis_size("vox")
    if count == 1:
        return jnp.zeros_like(value)
    if count == 2:
        return lax.ppermute(value, "vox", [(0, 1), (1, 0)])
    return lax.psum(value, "vox") - value


def last_sums(value, given, step_of):
    count, slabs = lax.axis_size("ray"), lax.axis_size("vox")
    if slabs != 2 or count & (count - 1) or count < 16:
        mine, rest = step_of(given)
        return (lax.psum(value, "ray"), mine, vox_others(mine)), rest
    for step in hops(count)[:-2]:
        value = value + lax.ppermute(value, "ray", pairs_of(count, step))
        if step == count // 4 | 1:
            given = step_of(given)
        value, given = lax.optimization_barrier((value, given))
    mine, rest = given
    both = jnp.concatenate([value, mine], axis=0)
    both = lax.ppermute(both, ("ray", "vox"), [(i, i ^ 7) for i in range(2 * count)])
    value = value + both[:8]
    return (value, lax.ppermute(value, "ray", pairs_of(count, 1)), mine, both[8:]), rest


def halo_of(low_edge, high_edge):
    count = lax.axis_size("vox")
    if count == 1:
        return jnp.zeros_like(high_edge), jnp.zeros_like(low_edge)
    forward = [(i, i + 1) for i in range(count - 1)]
    backward = [(target, source) for source, target in forward]
    return lax.ppermute(high_edge, "vox", forward), lax.ppermute(low_edge, "vox", backward)


def first_halo(sums, field):
    if lax.axis_size("vox") == 2 and lax.axis_size("ray") % 2 == 0:
        other = lax.ppermute(sums, "vox", [(0, 1), (1, 0)])
        column = other[RT + 8 :]
        partner = lax.ppermute(column, "ray", pairs_of(lax.axis_size("ray"), 1))
        return other, (column, partner, column, partner), True
    low = halo_of(field[PAD:-PAD, 0], field[PAD:-PAD, -1])
    far = halo_of(field[PAD:-PAD, 1], field[PAD:-PAD, -2])
    return vox_others(sums), (low[0], far[0], low[1], far[1]), False


def next_halo(sums, field):
    if lax.axis_size("vox") == 2 and lax.axis_size("ray") % 2 == 0:
        other = lax.ppermute(sums, "vox", [(0, 1), (1, 0)])
        half = other[RT + 8 :]
        return other, (half, lax.ppermute(half, "ray", pairs_of(lax.axis_size("ray"), 1))), True
    return vox_others(sums), halo_of(field[PAD:-PAD, 0], field[PAD:-PAD, -1]), False


def total(values):
    return jnp.sum(values, axis=(0, 1), keepdims=True)


def sub_iota(shape=(8, LAT)):
    return lax.broadcasted_iota(jnp.int32, shape, 0)


def lane_iota(shape=(8, LAT)):
    return lax.broadcasted_iota(jnp.int32, shape, 1)


def pull_lines(weighted, tiles_ref, pick_ref, out_ref, slots):
    rays = weighted.astype(BF16)
    for k in range(0, slots, 2):
        pair = jnp.concatenate([tiles_ref[k], tiles_ref[k + 1]], axis=1)
        product = jnp.dot(rays, pair, preferred_element_type=F32)
        out_ref[pl.ds(k, 1), :] = jnp.sum(pick_ref[k] * product[:, :LAT], axis=0, keepdims=True)
        out_ref[pl.ds(k + 1, 1), :] = jnp.sum(pick_ref[k + 1] * product[:, LAT:], axis=0, keepdims=True)


def push_lines(rays, lines, turned_ref, pick_ref, first, last):
    for k in range(first, last, 2):
        both = [jnp.broadcast_to(lines[j : j + 1], (RT, LAT)) for j in (k, k + 1)]
        pair = jnp.concatenate([turned_ref[k], turned_ref[k + 1]], axis=1)
        product = jnp.dot(
            jnp.concatenate(both, axis=0).astype(BF16), pair, preferred_element_type=F32
        )
        rays = rays + pick_ref[k] * product[:RT, :RAY_TILE]
        rays = rays + pick_ref[k + 1] * product[RT:, RAY_TILE:]
    return rays


def both_parts(lines):
    high = lines.astype(BF16)
    low = (lines - high.astype(F32)).astype(BF16)
    return jnp.concatenate([high, low], axis=1)


def across(values, sub, lane):
    up = jnp.where(lane == 0, 0.0, pltpu.roll(values, 1, 1))
    down = jnp.where(lane == LAT - 1, 0.0, pltpu.roll(values, LAT - 1, 1))
    return up + down


def column_stencil(column, beside, lane, sub):
    up = jnp.where(sub < EPOCHS, 0.0, pltpu.roll(column, EPOCHS, 0))
    down = jnp.where(sub >= PAIRS - EPOCHS, 0.0, pltpu.roll(column, PAIRS - EPOCHS, 0))
    later = pltpu.roll(column, PAIRS - 1, 0)
    earlier = pltpu.roll(column, 1, 0)
    epoch = jnp.where(sub % EPOCHS == 0, later, earlier)
    return (
        CENTRE * column
        - LATERAL * (beside + across(column, sub, lane))
        - VERTICAL * (up + down)
        - TEMPORAL * epoch
    )


def slab_stencil(pair, field_ref, low_ref, high_ref, sub, lane):
    here = field_ref[pair + PAD]
    below = jnp.where(sub == 0, low_ref[pl.ds(pair, 1), :], pltpu.roll(here, 1, 0))
    above = jnp.where(sub == LON_DEV - 1, high_ref[pl.ds(pair, 1), :], pltpu.roll(here, LON_DEV - 1, 0))
    epoch = field_ref[(pair ^ 1) + PAD]
    return (
        CENTRE * here
        - LATERAL * (below + above + across(here, sub, lane))
        - VERTICAL * (field_ref[pair] + field_ref[pair + 2 * PAD])
        - TEMPORAL * epoch
    )


def start_body(slots, count_ref, row_in, col_in, scale_in, table_in, receiver_in, delays_in, tiles_in,
               packet_ref, weight_ref, start_ref, pick_ref, own_ref, tiles_ref,
               row_ref, col_ref, scale_ref, table_ref, receiver_ref, delays_ref, sems):
    copies = [
        pltpu.make_async_copy(source, target, sems.at[j])
        for j, (source, target) in enumerate([
            (receiver_in, receiver_ref), (table_in, table_ref), (delays_in, delays_ref),
            (scale_in, scale_ref), (row_in, row_ref), (col_in, col_ref),
        ])
    ]
    pull = pltpu.make_async_copy(tiles_in, tiles_ref, sems.at[6])
    pull.start()
    for copy in copies:
        copy.start()
    for copy in copies:
        copy.wait()
    sub, lane = sub_iota(), lane_iota()
    receivers = receiver_ref[...]
    weight = jnp.zeros((RT, RAY_TILE), F32)
    for j in range(table_ref.shape[0]):
        weight = jnp.where(receivers == j, table_ref[j], weight)
    weight_ref[...] = weight
    start = weight * delays_ref[...]
    start_ref[...] = start
    extra = packet_ref.shape[0] - slots
    sub_x, lane_x = sub_iota((extra, LAT)), lane_iota((extra, LAT))
    side, place = own_place()
    rows, per = names_rows(slots), LAT // slots
    first = place % per * slots
    names = jnp.zeros((1, LAT), jnp.int32)
    for k in range(slots):
        live = jnp.where(k < count_ref[0, 0], scale_ref[k], 0.0)
        pick_ref[k] = jnp.where(sub == row_ref[k], live, 0.0)
        own_ref[pl.ds(k, 1), :] = jnp.full((1, LAT), col_ref[k], jnp.int32)
        names = jnp.where(lane[:1] == first + k, col_ref[k], names)
    square = total(start * start)
    packet_ref[slots:, :] = jnp.where(
        sub_x == side * rows + place // per,
        jnp.broadcast_to(names.astype(F32), (extra, LAT)),
        jnp.where(sub_x == CORES * rows, square, 0.0),
    )
    pull.wait()
    pull_lines(weight * start, tiles_ref, pick_ref, packet_ref, slots)


def turn_body(tiles_ref, turned_ref):
    for k in range(tiles_ref.shape[0]):
        turned_ref[k] = tiles_ref[k].T


def own_place():
    count, at = lax.axis_size("ray"), lax.axis_index("ray")
    side, place, bit = at % 2, 0, 1
    for step in hops(count)[:-1]:
        digit = at // (step - 1) % 2
        side = (side + digit) % 2
        place = place + bit * digit
        bit *= 2
    return side, place


def names_rows(slots):
    return lax.axis_size("ray") // CORES * slots // LAT


def names_of(ref, side, slots):
    rows = names_rows(slots)
    first = lax.axis_size("ray") // CORES * slots + side * rows
    return [ref[pl.ds(first + j, 1), :].astype(jnp.int32) for j in range(rows)]


def placed_lines(ref, slots):
    place = own_place()[1]
    return jnp.concatenate(
        [
            ref[pl.ds(pl.multiple_of((j ^ place) * slots, slots), slots), :]
            for j in range(lax.axis_size("ray") // CORES)
        ],
        axis=0,
    )


def extra_row(ref, slots, at):
    first = lax.axis_size("ray") // CORES * slots
    return ref[first + at : first + at + 1, :]


def found_lines(onehot, parts):
    found = jnp.dot(onehot, parts, preferred_element_type=F32)
    return found[:, :LAT] + found[:, LAT:]


CHUNK = 256


def onehot_of(names, ids):
    return jnp.concatenate(
        [jnp.where(ids == piece, 1.0, 0.0).astype(BF16) for piece in names], axis=1
    )


def edge_of(field_ref, at):
    flat = field_ref.reshape((PAIRS + 2 * PAD) * LON_DEV, LAT)
    return flat[pl.ds(PAD * LON_DEV + at, PAIRS, stride=LON_DEV), :]


def first_half_body(slots, mine_ref, own_ref, field_ref, lines_ref, names_ref):
    names = names_of(mine_ref, own_place()[0], slots)
    for j, piece in enumerate(names):
        names_ref[pl.ds(j, 1), :] = piece
    parts = both_parts(placed_lines(mine_ref, slots))
    lines_ref[...] = found_lines(onehot_of(names, own_ref[...]), parts)
    for first in range(0, LINES, CHUNK):
        onehot = onehot_of(names, sub_iota((CHUNK, LAT)) + first)
        piece = found_lines(onehot, parts).reshape(CHUNK // LON_DEV, LON_DEV, LAT)
        field_ref[first // LON_DEV : (first + CHUNK) // LON_DEV] = piece


def first_body(slots, other_ref, half_ref, half_lines_ref, mine_ref, own_ref, pick_ref, turned_ref,
               field_ref, lines_ref, out_ref, left_ref, names_ref):
    names = names_of(other_ref, 1 - own_place()[0], slots)
    for j, piece in enumerate(names):
        names_ref[pl.ds(j, 1), :] = piece
    parts = both_parts(placed_lines(other_ref, slots))
    lines = half_lines_ref[...] + found_lines(onehot_of(names, own_ref[...]), parts)
    lines_ref[...] = lines
    rays, part = jnp.zeros((RT, RAY_TILE), F32), slots * CHUNK // LINES
    zeros = jnp.zeros((PAD, LON_DEV, LAT), F32)
    field_ref[:PAD] = zeros
    field_ref[PAIRS + PAD :] = zeros
    square = jnp.zeros((8, LAT), F32)
    for first in range(0, LINES, CHUNK):
        onehot = onehot_of(names, sub_iota((CHUNK, LAT)) + first)
        count, pair = CHUNK // LON_DEV, first // LON_DEV
        piece = found_lines(onehot, parts).reshape(count, LON_DEV, LAT) + half_ref[pair : pair + count]
        field_ref[pair + PAD : pair + PAD + count] = piece
        square = square + jnp.sum(piece * piece, axis=0)
        rays = push_lines(rays, lines, turned_ref, pick_ref, first // CHUNK * part, (first // CHUNK + 1) * part)
    out_ref[:RT, :] = rays
    out_ref[RT : RT + 8, :] = jnp.broadcast_to(total(square), (8, LAT))
    odd = lax.axis_index("ray") % 2
    at = jnp.where(lax.axis_index("vox") == 0, LON_DEV - 1 - odd, odd)
    out_ref[RT + 8 :, :] = edge_of(field_ref, at)
    at = CORES * names_rows(slots)
    left = extra_row(mine_ref, slots, at) + extra_row(other_ref, slots, at)
    left_ref[...] = jnp.broadcast_to(left, (8, LAT))


def second_body(slots, mine_ref, other_ref, left_ref, weight_ref, start_ref, pick_ref, tiles_ref,
                packet_ref, rays_ref, image_ref, norm_ref):
    sub = sub_iota()
    left_sq = left_ref[...]
    norm_sq = mine_ref[RT : RT + 8, :] + other_ref[RT : RT + 8, :]
    inverse = lax.rsqrt(norm_sq)
    norm = norm_sq * inverse
    weight = weight_ref[...]
    image = (mine_ref[:RT, :] + other_ref[:RT, :]) * inverse
    image_ref[...] = image
    rays = weight * image - norm / left_sq * start_ref[...]
    rays_ref[...] = rays
    norm_ref[...] = norm
    pull_lines(weight * rays, tiles_ref, pick_ref, packet_ref, slots)
    packet_ref[slots:, :] = jnp.where(sub == 0, total(rays * rays), 0.0)


def flags():
    at, count = lax.axis_index("vox"), lax.axis_size("vox")
    return (at > 0).astype(F32), (at < count - 1).astype(F32)


def smooth_body(swapped, field_ref, low_ref, low2_ref, high_ref, high2_ref, damp_ref, norm_ref,
                smooth_ref, scaled_ref, far_ref, square_ref, near_ref):
    sub, lane = sub_iota(), lane_iota()
    has_low, has_high = flags()
    inverse = 1.0 / norm_ref[...]
    col_lane, col_sub = lane_iota((PAIRS, LAT)), sub_iota((PAIRS, LAT))
    low, low2, high, high2 = low_ref[...], low2_ref[...], high_ref[...], high2_ref[...]
    if swapped:
        odd = lax.axis_index("ray") % 2 == 1
        low, low2 = jnp.where(odd, low2, low), jnp.where(odd, low, low2)
        high, high2 = low, low2
    near_ref[0] = low * has_low
    near_ref[1] = high * has_high
    scale = damp_ref[...] * damp_ref[...] * jnp.broadcast_to(inverse[:1], (PAIRS, LAT))
    far_ref[0] = scale * has_low * column_stencil(low, low2 + edge_of(field_ref, 0), col_lane, col_sub)
    far_ref[1] = scale * has_high * column_stencil(
        high, high2 + edge_of(field_ref, LON_DEV - 1), col_lane, col_sub
    )
    zeros = jnp.zeros((PAD, LON_DEV, LAT), F32)
    scaled_ref[:PAD] = zeros
    scaled_ref[PAIRS + PAD :] = zeros

    def left(pair, square):
        damped = damp_ref[pl.ds(pair, 1), :]
        value = slab_stencil(pair, field_ref, near_ref.at[0], near_ref.at[1], sub, lane) * inverse * damped
        smooth_ref[pair] = value
        scaled_ref[pair + PAD] = value * damped
        return square + value * value

    square = lax.fori_loop(0, PAIRS, left, jnp.zeros((LON_DEV, LAT), F32), unroll=UNROLL)
    square_ref[...] = jnp.broadcast_to(total(square), (8, LAT))


def onehot_body(*refs):
    names_refs, onehot_refs = refs[: len(refs) // 2], refs[len(refs) // 2 :]
    for names_ref, onehot_ref in zip(names_refs, onehot_refs):
        pieces = [names_ref[pl.ds(j, 1), :] for j in range(onehot_ref.shape[1] // LAT)]
        for first in range(0, LINES, CHUNK):
            onehot_ref[first : first + CHUNK, :] = onehot_of(pieces, sub_iota((CHUNK, LAT)) + first)


def again_body(slots, col_ref, scaled_ref, far_ref, again_ref, lines_ref):
    sub, lane = sub_iota(), lane_iota()

    def right(pair, carry):
        again_ref[pair] = slab_stencil(pair, scaled_ref, far_ref.at[0], far_ref.at[1], sub, lane)
        return carry

    lax.fori_loop(0, PAIRS, right, 0, unroll=UNROLL)
    for k in range(slots):
        col = col_ref[k]
        lines_ref[pl.ds(k, 1), :] = again_ref[col // LON_DEV, pl.ds(col % LON_DEV, 1), :]


def third_half_body(slots, mine_ref, onehot_ref, names_ref, own_ref, again_lines_ref, again_ref,
                    half_ref, lines_ref):
    parts = both_parts(placed_lines(mine_ref, slots))
    names = [names_ref[pl.ds(j, 1), :] for j in range(onehot_ref.shape[1] // LAT)]
    lines_ref[...] = found_lines(onehot_of(names, own_ref[...]), parts) + again_lines_ref[...]
    for first in range(0, LINES, CHUNK):
        count, pair = CHUNK // LON_DEV, first // LON_DEV
        piece = found_lines(onehot_ref[first : first + CHUNK, :], parts).reshape(count, LON_DEV, LAT)
        half_ref[pair : pair + count] = piece + again_ref[pair : pair + count]


def third_body(slots, other_ref, half_ref, half_lines_ref, mine_ref, square_ref, onehot_ref, names_ref, own_ref,
               lines_ref, field_ref, norm_ref, pick_ref, turned_ref,
               next_ref, out_ref, shift_ref):
    shift = jnp.broadcast_to(extra_row(mine_ref, slots, 0) + extra_row(other_ref, slots, 0), (8, LAT))
    shift_ref[...] = shift
    inverse = 1.0 / norm_ref[...]
    back = shift * inverse
    parts = both_parts(placed_lines(other_ref, slots))
    names = [names_ref[pl.ds(j, 1), :] for j in range(onehot_ref.shape[1] // LAT)]
    lines = found_lines(onehot_of(names, own_ref[...]), parts) + half_lines_ref[...] - lines_ref[...] * back[:1]
    rays, part = jnp.zeros((RT, RAY_TILE), F32), slots * CHUNK // LINES
    zeros = jnp.zeros((PAD, LON_DEV, LAT), F32)
    next_ref[:PAD] = zeros
    next_ref[PAIRS + PAD :] = zeros
    square = jnp.zeros((8, LAT), F32)
    cross = jnp.zeros((8, LAT), F32)
    for first in range(0, LINES, CHUNK):
        count, pair = CHUNK // LON_DEV, first // LON_DEV
        piece = found_lines(onehot_ref[first : first + CHUNK, :], parts).reshape(count, LON_DEV, LAT)
        base = field_ref[pair + PAD : pair + PAD + count]
        piece = piece + half_ref[pair : pair + count] - base * back
        next_ref[pair + PAD : pair + PAD + count] = piece
        square = square + jnp.sum(piece * piece, axis=0)
        cross = cross + jnp.sum(piece * base, axis=0)
        rays = push_lines(rays, lines, turned_ref, pick_ref, first // CHUNK * part, (first // CHUNK + 1) * part)
    sub = sub_iota()
    out_ref[:RT, :] = rays
    out_ref[RT : RT + 8, :] = jnp.where(
        sub == 0, total(square), jnp.where(sub == 1, total(cross) * inverse, square_ref[...])
    )
    edge = edge_of(next_ref, jnp.where(lax.axis_index("vox") == 0, LON_DEV - 1, 0))
    half = PAIRS // 2
    out_ref[RT + 8 :, :] = jnp.where(lax.axis_index("ray") % 2 == 0, edge[:half], edge[half:])


def fourth_body(mine_ref, other_ref, shift_ref, weight_ref, rays_ref, image_ref,
                next_rays_ref, left_ref, rest_ref, norm_ref, sum_ref):
    sums = mine_ref[RT : RT + 8, :] + other_ref[RT : RT + 8, :]
    square, cross, rest = [jnp.broadcast_to(sums[j : j + 1], (8, LAT)) for j in range(3)]
    left_sq = shift_ref[...] + rest
    norm_sq = (square - 2.0 * rest * cross + rest * rest) / left_sq
    per_left = lax.rsqrt(left_sq)
    inverse = lax.rsqrt(norm_sq)
    norm = norm_sq * inverse
    rays = mine_ref[:RT, :] + other_ref[:RT, :] - rest * image_ref[...]
    rays = weight_ref[...] * rays * (per_left * inverse) - norm * per_left * rays_ref[...]
    next_rays_ref[...] = rays
    left_ref[...] = left_sq
    rest_ref[...] = rest
    norm_ref[...] = norm
    sum_ref[...] = jnp.broadcast_to(total(rays * rays), (8, LAT))


def last_smooth_body(halves, next_ref, low_ref, high_ref, damp_ref, smooth_ref, norm_ref, left_ref, rest_ref,
                     left0_ref, norm0_ref, square_ref, weights_ref, near_ref):
    sub, lane = sub_iota(), lane_iota()
    has_low, has_high = flags()
    if halves:
        odd, half = lax.axis_index("ray") % 2, PAIRS // 2
        for ref, at in ((low_ref, odd), (high_ref, 1 - odd)):
            near_ref[0, pl.ds(at * half, half), :] = ref[...] * has_low
            near_ref[1, pl.ds(at * half, half), :] = ref[...] * has_high
    else:
        near_ref[0] = low_ref[...] * has_low
        near_ref[1] = high_ref[...] * has_high
    norm, per_left = norm_ref[...], lax.rsqrt(left_ref[...])
    inverse = per_left / norm
    back = rest_ref[...] * inverse + norm * per_left

    def left(pair, square):
        damped = damp_ref[pl.ds(pair, 1), :]
        value = slab_stencil(pair, next_ref, near_ref.at[0], near_ref.at[1], sub, lane) * inverse * damped
        value = value - back * smooth_ref[pair]
        return square + value * value

    square = lax.fori_loop(0, PAIRS, left, jnp.zeros((LON_DEV, LAT), F32), unroll=UNROLL)
    square_ref[...] = jnp.broadcast_to(total(square), (8, LAT))
    left0_sq, norm0, left1_sq = left0_ref[...], norm0_ref[...], left_ref[...]
    left0, left1 = jnp.sqrt(left0_sq), jnp.sqrt(left1_sq)
    right0 = norm0 / left0
    diag1 = jnp.sqrt(right0 * right0 + left1_sq)
    cosine, sine = right0 / diag1, left1 / diag1
    coupling = sine * norm
    diag_bar = -cosine * norm
    step1, resid = cosine * left0, sine * left0
    weights_ref[0] = diag_bar * resid / (left1 * norm)
    weights_ref[1] = diag_bar * diag_bar
    weights_ref[2] = step1 / diag1 / norm0
    weights_ref[3] = (left1 * norm * coupling / diag1 + rest_ref[...]) / norm0


def end_body(share, parts, *refs):
    left2_sq = refs[0][...]
    for ref in refs[1:parts]:
        left2_sq = left2_sq + ref[...]
    weights_ref, rays_ref, field_ref, next_ref, density_ref, out_ref = refs[parts:]
    out_ref[...] = rays_ref[...] * lax.rsqrt(left2_sq)
    on_next = weights_ref[0] / (weights_ref[1] + left2_sq)
    on_first = weights_ref[2] - weights_ref[3] * on_next
    first = lax.axis_index("ray") * share + PAD
    for j in range(share):
        density_ref[j] = on_first * field_ref[first + j] + on_next * next_ref[first + j]


def on_device(
    tiles,
    tile_scale,
    tile_row,
    tile_col,
    tile_count,
    delays,
    ray_receiver,
    receiver_weight,
    smooth_scale,
):
    block = tiles[0, 0]
    slots = block.shape[0]
    rays_n = lax.axis_size("ray")
    col_index = tile_col[0, 0]
    held = (RT, RAY_TILE)
    row = ((8, LAT), F32)
    slab = ((PAIRS, LON_DEV, LAT), F32)
    padded = ((PAIRS + 2 * PAD, LON_DEV, LAT), F32)
    packet = ((slots + 8, LAT), F32)
    names_n = rays_n // CORES * slots // LAT
    extra = -(-(CORES * names_n + 1) // 8) * 8
    damp = jnp.broadcast_to(jnp.repeat(smooth_scale, EPOCHS)[:, None], (PAIRS, LAT))

    hbm = pl.BlockSpec(memory_space=pl.ANY)
    table = receiver_weight.shape[0]
    mine, weight, start, pick, own, block = local_call(
        functools.partial(start_body, slots), "start", [SM] + [hbm] * 7,
        [((slots + extra, LAT), F32), (held, F32), (held, F32), ((slots, RT, LAT), F32), ((slots, LAT), jnp.int32),
         (block.shape, BF16)],
        [pltpu.SMEM((slots,), jnp.int32), pltpu.SMEM((slots,), jnp.int32), pltpu.SMEM((slots,), F32),
         pltpu.SMEM((table,), F32), pltpu.VMEM(held, jnp.int32),
         pltpu.VMEM(held, F32), pltpu.SemaphoreType.DMA((7,))],
    )(tile_count, *(pltpu.with_memory_space_constraint(x, pltpu.MemorySpace.HBM) for x in (
        tile_row[0, 0], col_index, tile_scale[0, 0], receiver_weight,
        ray_receiver.reshape(held), delays.reshape(held), block)))
    turn = lambda given: (given, *local_call(turn_body, "turn", [VM], [(block.shape, BF16)])(block))
    near, far, (damp, turned) = gather_rays(mine, extra, (lambda _: damp, turn))
    named = ((names_n, LAT), jnp.int32)

    half, half_lines, names_a = local_call(
        functools.partial(first_half_body, slots), "first_half", [VM] * 2,
        [slab, ((slots, LAT), F32), named],
    )(near, own)
    field, lines, sums, left0, names_b = local_call(
        functools.partial(first_body, slots), "first", [VM] * 7,
        [padded, ((slots, LAT), F32), ((RT + 8 + PAIRS, LAT), F32), row, named],
    )(far, half, half_lines, near, own, pick, turned)
    others, columns, swapped = first_halo(sums, field)
    onehots = local_call(
        onehot_body, "onehot", [VM] * 2, [((LINES, names_n * LAT), BF16)] * 2,
    )(names_a, names_b)
    others, (onehot_a, onehot_b) = lax.optimization_barrier((others, onehots))

    mine, rays, image, norm0 = local_call(
        functools.partial(second_body, slots), "second", [VM] * 7, [packet, (held, F32), (held, F32), row],
    )(sums, others, left0, weight, start, pick, block)
    def smooth_step(columns):
        return local_call(
            functools.partial(smooth_body, swapped), "smooth", [VM] * 7,
            [slab, padded, ((2, PAIRS, LAT), F32), row], [pltpu.VMEM((2, PAIRS, LAT), F32)],
        )(field, *columns, damp, norm0)

    def again_step(given):
        smooth, scaled, beside, square = given
        again, again_lines = local_call(
            functools.partial(again_body, slots), "again", [SM] + [VM] * 2, [slab, ((slots, LAT), F32)],
        )(col_index, scaled, beside)
        return smooth, square, again, again_lines

    near, far, given = gather_rays(mine, 8, (lambda _: columns, smooth_step, again_step))
    smooth, square, again, again_lines = given

    half, half_lines = local_call(
        functools.partial(third_half_body, slots), "third_half", [VM] * 6, [slab, ((slots, LAT), F32)],
    )(near, onehot_a, names_a, own, again_lines, again)
    following, sums, shift = local_call(
        functools.partial(third_body, slots), "third", [VM] * 13,
        [padded, ((RT + 8 + PAIRS // 2, LAT), F32), row],
    )(far, half, half_lines, near, square, onehot_b, names_b, own, lines, field, norm0, pick, turned)
    others, beside, halves = next_halo(sums, following)
    last_rays, left1, rest, norm1, ray_square = local_call(
        fourth_body, "fourth", [VM] * 6, [(held, F32), row, row, row, row],
    )(sums, others, shift, weight, rays, image)

    def last_step(beside):
        return local_call(
            functools.partial(last_smooth_body, halves), "last_smooth", [VM] * 10, [row, ((4, 8, LAT), F32)],
            [pltpu.VMEM((2, PAIRS, LAT), F32)],
        )(following, *beside, damp, smooth, norm1, left1, rest, left0, norm0)

    shares, weights = last_sums(ray_square, beside, last_step)

    share = PAIRS // rays_n
    density, rays_out = local_call(
        functools.partial(end_body, share, len(shares)), "end", [VM] * (len(shares) + 4),
        [((share, LON_DEV, LAT), F32), (held, F32)],
    )(*shares, weights, last_rays, field, following)
    return (density.reshape(ALT // rays_n, EPOCHS, LON_DEV, LAT), rays_out.reshape(-1))


def solution(mesh):
    in_specs = (
        P("ray", "vox", None, None, None),
        P("ray", "vox", None),
        P("ray", "vox", None),
        P("ray", "vox", None),
        P("ray", "vox"),
        P("ray"),
        P("ray"),
        P("ray"),
        P(),
    )
    out_specs = (P("ray", None, "vox", None), P("ray"))
    return jax.shard_map(
        on_device, mesh=mesh, in_specs=in_specs, out_specs=out_specs, check_vma=False
    )
```

```python
import functools

import jax
import jax.numpy as jnp
from jax import lax
from jax.experimental import pallas as pl
from jax.experimental.pallas import tpu as pltpu
from jax.sharding import PartitionSpec as P

ALT = 64
EPOCHS = 2
LAT = 128
LON_DEV = 8
RAY_TILE = 128
RT = 8
CORES = 2
PAIRS = ALT * EPOCHS
LINES = PAIRS * LON_DEV
PAD = EPOCHS
UNROLL = 32

LATERAL = 1.0
VERTICAL = 4.0
TEMPORAL = 0.5
CENTRE = 2.0 * (2.0 * LATERAL + VERTICAL + TEMPORAL)

F32 = jnp.float32
BF16 = jnp.bfloat16
VM = pl.BlockSpec(memory_space=pltpu.VMEM)
SM = pl.BlockSpec(memory_space=pltpu.SMEM)


def local_call(body, name, in_specs, out_shapes, scratch=()):
    return pl.pallas_call(
        body,
        name=name,
        in_specs=in_specs,
        out_specs=[VM] * len(out_shapes),
        out_shape=[jax.ShapeDtypeStruct(shape, dtype) for shape, dtype in out_shapes],
        scratch_shapes=list(scratch),
        compiler_params=pltpu.CompilerParams(vmem_limit_bytes=32 << 20),
    )


def pairs_of(count, step):
    return [(i, i ^ step) for i in range(count)]


def hops(count):
    steps = []
    while count > 1:
        count //= 2
        steps.append(count | 1)
    return steps


def gather_rays(packet, extra, during=()):
    count = lax.axis_size("ray")
    if count < 2 or count & (count - 1):
        raise ValueError("ray size")
    done, given = list(during), None
    for step in hops(count):
        other = lax.ppermute(packet, "ray", pairs_of(count, step))
        if step == 1:
            break
        joined = jnp.concatenate(
            [packet[:-extra], other[:-extra], packet[-extra:] + other[-extra:]], axis=0
        )
        if done:
            given = done.pop(0)(given)
            joined, given = lax.optimization_barrier((joined, given))
        packet = joined
    while done:
        given = done.pop(0)(given)
    return packet, other, given


def vox_others(value):
    count = lax.axis_size("vox")
    if count == 1:
        return jnp.zeros_like(value)
    if count == 2:
        return lax.ppermute(value, "vox", [(0, 1), (1, 0)])
    return lax.psum(value, "vox") - value


def last_sums(value, given, step_of):
    count, slabs = lax.axis_size("ray"), lax.axis_size("vox")
    if slabs != 2 or count & (count - 1) or count < 16:
        mine, rest = step_of(given)
        return (lax.psum(value, "ray"), mine, vox_others(mine)), rest
    for step in hops(count)[:-2]:
        value = value + lax.ppermute(value, "ray", pairs_of(count, step))
        if step == count // 4 | 1:
            given = step_of(given)
        value, given = lax.optimization_barrier((value, given))
    mine, rest = given
    both = jnp.concatenate([value, mine], axis=0)
    both = lax.ppermute(both, ("ray", "vox"), [(i, i ^ 7) for i in range(2 * count)])
    value = value + both[:8]
    return (value, lax.ppermute(value, "ray", pairs_of(count, 1)), mine, both[8:]), rest


def halo_of(low_edge, high_edge):
    count = lax.axis_size("vox")
    if count == 1:
        return jnp.zeros_like(high_edge), jnp.zeros_like(low_edge)
    forward = [(i, i + 1) for i in range(count - 1)]
    backward = [(target, source) for source, target in forward]
    return lax.ppermute(high_edge, "vox", forward), lax.ppermute(low_edge, "vox", backward)


def first_halo(sums, field):
    if lax.axis_size("vox") == 2 and lax.axis_size("ray") % 2 == 0:
        other = lax.ppermute(sums, "vox", [(0, 1), (1, 0)])
        column = other[RT + 8 :]
        partner = lax.ppermute(column, "ray", pairs_of(lax.axis_size("ray"), 1))
        return other, (column, partner, column, partner), True
    low = halo_of(field[PAD:-PAD, 0], field[PAD:-PAD, -1])
    far = halo_of(field[PAD:-PAD, 1], field[PAD:-PAD, -2])
    return vox_others(sums), (low[0], far[0], low[1], far[1]), False


def next_halo(sums, field):
    if lax.axis_size("vox") == 2 and lax.axis_size("ray") % 2 == 0:
        other = lax.ppermute(sums, "vox", [(0, 1), (1, 0)])
        half = other[RT + 8 :]
        return other, (half, lax.ppermute(half, "ray", pairs_of(lax.axis_size("ray"), 1))), True
    return vox_others(sums), halo_of(field[PAD:-PAD, 0], field[PAD:-PAD, -1]), False


def total(values):
    return jnp.sum(values, axis=(0, 1), keepdims=True)


def sub_iota(shape=(8, LAT)):
    return lax.broadcasted_iota(jnp.int32, shape, 0)


def lane_iota(shape=(8, LAT)):
    return lax.broadcasted_iota(jnp.int32, shape, 1)


def pull_lines(weighted, tiles_ref, pick_ref, out_ref, slots):
    rays = weighted.astype(BF16)
    for k in range(0, slots, 2):
        pair = jnp.concatenate([tiles_ref[k], tiles_ref[k + 1]], axis=1)
        product = jnp.dot(rays, pair, preferred_element_type=F32)
        out_ref[pl.ds(k, 1), :] = jnp.sum(pick_ref[k] * product[:, :LAT], axis=0, keepdims=True)
        out_ref[pl.ds(k + 1, 1), :] = jnp.sum(pick_ref[k + 1] * product[:, LAT:], axis=0, keepdims=True)


def push_lines(rays, lines, turned_ref, pick_ref, first, last):
    for k in range(first, last, 2):
        both = [jnp.broadcast_to(lines[j : j + 1], (RT, LAT)) for j in (k, k + 1)]
        pair = jnp.concatenate([turned_ref[k], turned_ref[k + 1]], axis=1)
        product = jnp.dot(
            jnp.concatenate(both, axis=0).astype(BF16), pair, preferred_element_type=F32
        )
        rays = rays + pick_ref[k] * product[:RT, :RAY_TILE]
        rays = rays + pick_ref[k + 1] * product[RT:, RAY_TILE:]
    return rays


def both_parts(lines):
    high = lines.astype(BF16)
    low = (lines - high.astype(F32)).astype(BF16)
    return jnp.concatenate([high, low], axis=1)


def across(values, sub, lane):
    up = jnp.where(lane == 0, 0.0, pltpu.roll(values, 1, 1))
    down = jnp.where(lane == LAT - 1, 0.0, pltpu.roll(values, LAT - 1, 1))
    return up + down


def column_stencil(column, beside, lane, sub):
    up = jnp.where(sub < EPOCHS, 0.0, pltpu.roll(column, EPOCHS, 0))
    down = jnp.where(sub >= PAIRS - EPOCHS, 0.0, pltpu.roll(column, PAIRS - EPOCHS, 0))
    later = pltpu.roll(column, PAIRS - 1, 0)
    earlier = pltpu.roll(column, 1, 0)
    epoch = jnp.where(sub % EPOCHS == 0, later, earlier)
    return (
        CENTRE * column
        - LATERAL * (beside + across(column, sub, lane))
        - VERTICAL * (up + down)
        - TEMPORAL * epoch
    )


def slab_stencil(pair, field_ref, low_ref, high_ref, sub, lane):
    here = field_ref[pair + PAD]
    below = jnp.where(sub == 0, low_ref[pl.ds(pair, 1), :], pltpu.roll(here, 1, 0))
    above = jnp.where(sub == LON_DEV - 1, high_ref[pl.ds(pair, 1), :], pltpu.roll(here, LON_DEV - 1, 0))
    epoch = field_ref[(pair ^ 1) + PAD]
    return (
        CENTRE * here
        - LATERAL * (below + above + across(here, sub, lane))
        - VERTICAL * (field_ref[pair] + field_ref[pair + 2 * PAD])
        - TEMPORAL * epoch
    )


def start_body(slots, count_ref, row_in, col_in, scale_in, table_in, receiver_in, delays_in, tiles_in,
               packet_ref, weight_ref, start_ref, pick_ref, own_ref, tiles_ref,
               row_ref, col_ref, scale_ref, table_ref, receiver_ref, delays_ref, sems):
    copies = [
        pltpu.make_async_copy(source, target, sems.at[j])
        for j, (source, target) in enumerate([
            (receiver_in, receiver_ref), (table_in, table_ref), (delays_in, delays_ref),
            (scale_in, scale_ref), (row_in, row_ref), (col_in, col_ref),
        ])
    ]
    pull = pltpu.make_async_copy(tiles_in, tiles_ref, sems.at[6])
    pull.start()
    for copy in copies:
        copy.start()
    for copy in copies:
        copy.wait()
    sub, lane = sub_iota(), lane_iota()
    receivers = receiver_ref[...]
    weight = jnp.zeros((RT, RAY_TILE), F32)
    for j in range(table_ref.shape[0]):
        weight = jnp.where(receivers == j, table_ref[j], weight)
    weight_ref[...] = weight
    start = weight * delays_ref[...]
    start_ref[...] = start
    extra = packet_ref.shape[0] - slots
    sub_x, lane_x = sub_iota((extra, LAT)), lane_iota((extra, LAT))
    side, place = own_place()
    rows, per = names_rows(slots), LAT // slots
    first = place % per * slots
    names = jnp.zeros((1, LAT), jnp.int32)
    for k in range(slots):
        live = jnp.where(k < count_ref[0, 0], scale_ref[k], 0.0)
        pick_ref[k] = jnp.where(sub == row_ref[k], live, 0.0)
        own_ref[pl.ds(k, 1), :] = jnp.full((1, LAT), col_ref[k], jnp.int32)
        names = jnp.where(lane[:1] == first + k, col_ref[k], names)
    square = total(start * start)
    packet_ref[slots:, :] = jnp.where(
        sub_x == side * rows + place // per,
        jnp.broadcast_to(names.astype(F32), (extra, LAT)),
        jnp.where(sub_x == CORES * rows, square, 0.0),
    )
    pull.wait()
    pull_lines(weight * start, tiles_ref, pick_ref, packet_ref, slots)


def turn_body(tiles_ref, turned_ref):
    for k in range(tiles_ref.shape[0]):
        turned_ref[k] = tiles_ref[k].T


def own_place():
    count, at = lax.axis_size("ray"), lax.axis_index("ray")
    side, place, bit = at % 2, 0, 1
    for step in hops(count)[:-1]:
        digit = at // (step - 1) % 2
        side = (side + digit) % 2
        place = place + bit * digit
        bit *= 2
    return side, place


def names_rows(slots):
    return lax.axis_size("ray") // CORES * slots // LAT


def names_of(ref, side, slots):
    rows = names_rows(slots)
    first = lax.axis_size("ray") // CORES * slots + side * rows
    return [ref[pl.ds(first + j, 1), :].astype(jnp.int32) for j in range(rows)]


def placed_lines(ref, slots):
    place = own_place()[1]
    return jnp.concatenate(
        [
            ref[pl.ds(pl.multiple_of((j ^ place) * slots, slots), slots), :]
            for j in range(lax.axis_size("ray") // CORES)
        ],
        axis=0,
    )


def extra_row(ref, slots, at):
    first = lax.axis_size("ray") // CORES * slots
    return ref[first + at : first + at + 1, :]


def found_lines(onehot, parts):
    found = jnp.dot(onehot, parts, preferred_element_type=F32)
    return found[:, :LAT] + found[:, LAT:]


CHUNK = 256


def onehot_of(names, ids):
    return jnp.concatenate(
        [jnp.where(ids == piece, 1.0, 0.0).astype(BF16) for piece in names], axis=1
    )


def edge_of(field_ref, at):
    flat = field_ref.reshape((PAIRS + 2 * PAD) * LON_DEV, LAT)
    return flat[pl.ds(PAD * LON_DEV + at, PAIRS, stride=LON_DEV), :]


def first_half_body(slots, mine_ref, own_ref, field_ref, lines_ref, names_ref):
    names = names_of(mine_ref, own_place()[0], slots)
    for j, piece in enumerate(names):
        names_ref[pl.ds(j, 1), :] = piece
    parts = both_parts(placed_lines(mine_ref, slots))
    lines_ref[...] = found_lines(onehot_of(names, own_ref[...]), parts)
    for first in range(0, LINES, CHUNK):
        onehot = onehot_of(names, sub_iota((CHUNK, LAT)) + first)
        piece = found_lines(onehot, parts).reshape(CHUNK // LON_DEV, LON_DEV, LAT)
        field_ref[first // LON_DEV : (first + CHUNK) // LON_DEV] = piece


def first_body(slots, other_ref, half_ref, half_lines_ref, mine_ref, own_ref, pick_ref, turned_ref,
               field_ref, lines_ref, out_ref, left_ref, names_ref):
    names = names_of(other_ref, 1 - own_place()[0], slots)
    for j, piece in enumerate(names):
        names_ref[pl.ds(j, 1), :] = piece
    parts = both_parts(placed_lines(other_ref, slots))
    lines = half_lines_ref[...] + found_lines(onehot_of(names, own_ref[...]), parts)
    lines_ref[...] = lines
    rays, part = jnp.zeros((RT, RAY_TILE), F32), slots * CHUNK // LINES
    zeros = jnp.zeros((PAD, LON_DEV, LAT), F32)
    field_ref[:PAD] = zeros
    field_ref[PAIRS + PAD :] = zeros
    square = jnp.zeros((8, LAT), F32)
    for first in range(0, LINES, CHUNK):
        onehot = onehot_of(names, sub_iota((CHUNK, LAT)) + first)
        count, pair = CHUNK // LON_DEV, first // LON_DEV
        piece = found_lines(onehot, parts).reshape(count, LON_DEV, LAT) + half_ref[pair : pair + count]
        field_ref[pair + PAD : pair + PAD + count] = piece
        square = square + jnp.sum(piece * piece, axis=0)
        rays = push_lines(rays, lines, turned_ref, pick_ref, first // CHUNK * part, (first // CHUNK + 1) * part)
    out_ref[:RT, :] = rays
    out_ref[RT : RT + 8, :] = jnp.broadcast_to(total(square), (8, LAT))
    odd = lax.axis_index("ray") % 2
    at = jnp.where(lax.axis_index("vox") == 0, LON_DEV - 1 - odd, odd)
    out_ref[RT + 8 :, :] = edge_of(field_ref, at)
    at = CORES * names_rows(slots)
    left = extra_row(mine_ref, slots, at) + extra_row(other_ref, slots, at)
    left_ref[...] = jnp.broadcast_to(left, (8, LAT))


def second_body(slots, mine_ref, other_ref, left_ref, weight_ref, start_ref, pick_ref, tiles_ref,
                packet_ref, rays_ref, image_ref, norm_ref):
    sub = sub_iota()
    left_sq = left_ref[...]
    norm_sq = mine_ref[RT : RT + 8, :] + other_ref[RT : RT + 8, :]
    inverse = lax.rsqrt(norm_sq)
    norm = norm_sq * inverse
    weight = weight_ref[...]
    image = (mine_ref[:RT, :] + other_ref[:RT, :]) * inverse
    image_ref[...] = image
    rays = weight * image - norm / left_sq * start_ref[...]
    rays_ref[...] = rays
    norm_ref[...] = norm
    pull_lines(weight * rays, tiles_ref, pick_ref, packet_ref, slots)
    packet_ref[slots:, :] = jnp.where(sub == 0, total(rays * rays), 0.0)


def flags():
    at, count = lax.axis_index("vox"), lax.axis_size("vox")
    return (at > 0).astype(F32), (at < count - 1).astype(F32)


def smooth_body(swapped, field_ref, low_ref, low2_ref, high_ref, high2_ref, damp_ref, norm_ref,
                smooth_ref, scaled_ref, far_ref, square_ref, near_ref):
    sub, lane = sub_iota(), lane_iota()
    has_low, has_high = flags()
    inverse = 1.0 / norm_ref[...]
    col_lane, col_sub = lane_iota((PAIRS, LAT)), sub_iota((PAIRS, LAT))
    low, low2, high, high2 = low_ref[...], low2_ref[...], high_ref[...], high2_ref[...]
    if swapped:
        odd = lax.axis_index("ray") % 2 == 1
        low, low2 = jnp.where(odd, low2, low), jnp.where(odd, low, low2)
        high, high2 = low, low2
    near_ref[0] = low * has_low
    near_ref[1] = high * has_high
    scale = damp_ref[...] * damp_ref[...] * jnp.broadcast_to(inverse[:1], (PAIRS, LAT))
    far_ref[0] = scale * has_low * column_stencil(low, low2 + edge_of(field_ref, 0), col_lane, col_sub)
    far_ref[1] = scale * has_high * column_stencil(
        high, high2 + edge_of(field_ref, LON_DEV - 1), col_lane, col_sub
    )
    zeros = jnp.zeros((PAD, LON_DEV, LAT), F32)
    scaled_ref[:PAD] = zeros
    scaled_ref[PAIRS + PAD :] = zeros

    def left(pair, square):
        damped = damp_ref[pl.ds(pair, 1), :]
        value = slab_stencil(pair, field_ref, near_ref.at[0], near_ref.at[1], sub, lane) * inverse * damped
        smooth_ref[pair] = value
        scaled_ref[pair + PAD] = value * damped
        return square + value * value

    square = lax.fori_loop(0, PAIRS, left, jnp.zeros((LON_DEV, LAT), F32), unroll=UNROLL)
    square_ref[...] = jnp.broadcast_to(total(square), (8, LAT))


def onehot_body(*refs):
    names_refs, onehot_refs = refs[: len(refs) // 2], refs[len(refs) // 2 :]
    for names_ref, onehot_ref in zip(names_refs, onehot_refs):
        pieces = [names_ref[pl.ds(j, 1), :] for j in range(onehot_ref.shape[1] // LAT)]
        for first in range(0, LINES, CHUNK):
            onehot_ref[first : first + CHUNK, :] = onehot_of(pieces, sub_iota((CHUNK, LAT)) + first)


def again_body(slots, col_ref, scaled_ref, far_ref, again_ref, lines_ref):
    sub, lane = sub_iota(), lane_iota()

    def right(pair, carry):
        again_ref[pair] = slab_stencil(pair, scaled_ref, far_ref.at[0], far_ref.at[1], sub, lane)
        return carry

    lax.fori_loop(0, PAIRS, right, 0, unroll=UNROLL)
    for k in range(slots):
        col = col_ref[k]
        lines_ref[pl.ds(k, 1), :] = again_ref[col // LON_DEV, pl.ds(col % LON_DEV, 1), :]


def third_half_body(slots, mine_ref, onehot_ref, names_ref, own_ref, again_lines_ref, again_ref,
                    half_ref, lines_ref):
    parts = both_parts(placed_lines(mine_ref, slots))
    names = [names_ref[pl.ds(j, 1), :] for j in range(onehot_ref.shape[1] // LAT)]
    lines_ref[...] = found_lines(onehot_of(names, own_ref[...]), parts) + again_lines_ref[...]
    for first in range(0, LINES, CHUNK):
        count, pair = CHUNK // LON_DEV, first // LON_DEV
        piece = found_lines(onehot_ref[first : first + CHUNK, :], parts).reshape(count, LON_DEV, LAT)
        half_ref[pair : pair + count] = piece + again_ref[pair : pair + count]


def third_body(slots, other_ref, half_ref, half_lines_ref, mine_ref, square_ref, onehot_ref, names_ref, own_ref,
               lines_ref, field_ref, norm_ref, pick_ref, turned_ref,
               next_ref, out_ref, shift_ref):
    shift = jnp.broadcast_to(extra_row(mine_ref, slots, 0) + extra_row(other_ref, slots, 0), (8, LAT))
    shift_ref[...] = shift
    inverse = 1.0 / norm_ref[...]
    back = shift * inverse
    parts = both_parts(placed_lines(other_ref, slots))
    names = [names_ref[pl.ds(j, 1), :] for j in range(onehot_ref.shape[1] // LAT)]
    lines = found_lines(onehot_of(names, own_ref[...]), parts) + half_lines_ref[...] - lines_ref[...] * back[:1]
    rays, part = jnp.zeros((RT, RAY_TILE), F32), slots * CHUNK // LINES
    zeros = jnp.zeros((PAD, LON_DEV, LAT), F32)
    next_ref[:PAD] = zeros
    next_ref[PAIRS + PAD :] = zeros
    square = jnp.zeros((8, LAT), F32)
    cross = jnp.zeros((8, LAT), F32)
    for first in range(0, LINES, CHUNK):
        count, pair = CHUNK // LON_DEV, first // LON_DEV
        piece = found_lines(onehot_ref[first : first + CHUNK, :], parts).reshape(count, LON_DEV, LAT)
        base = field_ref[pair + PAD : pair + PAD + count]
        piece = piece + half_ref[pair : pair + count] - base * back
        next_ref[pair + PAD : pair + PAD + count] = piece
        square = square + jnp.sum(piece * piece, axis=0)
        cross = cross + jnp.sum(piece * base, axis=0)
        rays = push_lines(rays, lines, turned_ref, pick_ref, first // CHUNK * part, (first // CHUNK + 1) * part)
    sub = sub_iota()
    out_ref[:RT, :] = rays
    out_ref[RT : RT + 8, :] = jnp.where(
        sub == 0, total(square), jnp.where(sub == 1, total(cross) * inverse, square_ref[...])
    )
    edge = edge_of(next_ref, jnp.where(lax.axis_index("vox") == 0, LON_DEV - 1, 0))
    half = PAIRS // 2
    out_ref[RT + 8 :, :] = jnp.where(lax.axis_index("ray") % 2 == 0, edge[:half], edge[half:])


def fourth_body(mine_ref, other_ref, shift_ref, weight_ref, rays_ref, image_ref,
                next_rays_ref, left_ref, rest_ref, norm_ref, sum_ref):
    sums = mine_ref[RT : RT + 8, :] + other_ref[RT : RT + 8, :]
    square, cross, rest = [jnp.broadcast_to(sums[j : j + 1], (8, LAT)) for j in range(3)]
    left_sq = shift_ref[...] + rest
    norm_sq = (square - 2.0 * rest * cross + rest * rest) / left_sq
    per_left = lax.rsqrt(left_sq)
    inverse = lax.rsqrt(norm_sq)
    norm = norm_sq * inverse
    rays = mine_ref[:RT, :] + other_ref[:RT, :] - rest * image_ref[...]
    rays = weight_ref[...] * rays * (per_left * inverse) - norm * per_left * rays_ref[...]
    next_rays_ref[...] = rays
    left_ref[...] = left_sq
    rest_ref[...] = rest
    norm_ref[...] = norm
    sum_ref[...] = jnp.broadcast_to(total(rays * rays), (8, LAT))


def last_smooth_body(halves, next_ref, low_ref, high_ref, damp_ref, smooth_ref, norm_ref, left_ref, rest_ref,
                     left0_ref, norm0_ref, square_ref, weights_ref, near_ref):
    sub, lane = sub_iota(), lane_iota()
    has_low, has_high = flags()
    if halves:
        odd, half = lax.axis_index("ray") % 2, PAIRS // 2
        for ref, at in ((low_ref, odd), (high_ref, 1 - odd)):
            near_ref[0, pl.ds(at * half, half), :] = ref[...] * has_low
            near_ref[1, pl.ds(at * half, half), :] = ref[...] * has_high
    else:
        near_ref[0] = low_ref[...] * has_low
        near_ref[1] = high_ref[...] * has_high
    norm, per_left = norm_ref[...], lax.rsqrt(left_ref[...])
    inverse = per_left / norm
    back = rest_ref[...] * inverse + norm * per_left

    def left(pair, square):
        damped = damp_ref[pl.ds(pair, 1), :]
        value = slab_stencil(pair, next_ref, near_ref.at[0], near_ref.at[1], sub, lane) * inverse * damped
        value = value - back * smooth_ref[pair]
        return square + value * value

    square = lax.fori_loop(0, PAIRS, left, jnp.zeros((LON_DEV, LAT), F32), unroll=UNROLL)
    square_ref[...] = jnp.broadcast_to(total(square), (8, LAT))
    left0_sq, norm0, left1_sq = left0_ref[...], norm0_ref[...], left_ref[...]
    left0, left1 = jnp.sqrt(left0_sq), jnp.sqrt(left1_sq)
    right0 = norm0 / left0
    diag1 = jnp.sqrt(right0 * right0 + left1_sq)
    cosine, sine = right0 / diag1, left1 / diag1
    coupling = sine * norm
    diag_bar = -cosine * norm
    step1, resid = cosine * left0, sine * left0
    weights_ref[0] = diag_bar * resid / (left1 * norm)
    weights_ref[1] = diag_bar * diag_bar
    weights_ref[2] = step1 / diag1 / norm0
    weights_ref[3] = (left1 * norm * coupling / diag1 + rest_ref[...]) / norm0


def end_body(share, parts, *refs):
    left2_sq = refs[0][...]
    for ref in refs[1:parts]:
        left2_sq = left2_sq + ref[...]
    weights_ref, rays_ref, field_ref, next_ref, density_ref, out_ref = refs[parts:]
    out_ref[...] = rays_ref[...] * lax.rsqrt(left2_sq)
    on_next = weights_ref[0] / (weights_ref[1] + left2_sq)
    on_first = weights_ref[2] - weights_ref[3] * on_next
    first = lax.axis_index("ray") * share + PAD
    for j in range(share):
        density_ref[j] = on_first * field_ref[first + j] + on_next * next_ref[first + j]


def on_device(
    tiles,
    tile_scale,
    tile_row,
    tile_col,
    tile_count,
    delays,
    ray_receiver,
    receiver_weight,
    smooth_scale,
):
    block = tiles[0, 0]
    slots = block.shape[0]
    rays_n = lax.axis_size("ray")
    col_index = tile_col[0, 0]
    held = (RT, RAY_TILE)
    row = ((8, LAT), F32)
    slab = ((PAIRS, LON_DEV, LAT), F32)
    padded = ((PAIRS + 2 * PAD, LON_DEV, LAT), F32)
    packet = ((slots + 8, LAT), F32)
    names_n = rays_n // CORES * slots // LAT
    extra = -(-(CORES * names_n + 1) // 8) * 8
    damp = jnp.broadcast_to(jnp.repeat(smooth_scale, EPOCHS)[:, None], (PAIRS, LAT))

    hbm = pl.BlockSpec(memory_space=pl.ANY)
    table = receiver_weight.shape[0]
    mine, weight, start, pick, own, block = local_call(
        functools.partial(start_body, slots), "start", [SM] + [hbm] * 7,
        [((slots + extra, LAT), F32), (held, F32), (held, F32), ((slots, RT, LAT), F32), ((slots, LAT), jnp.int32),
         (block.shape, BF16)],
        [pltpu.SMEM((slots,), jnp.int32), pltpu.SMEM((slots,), jnp.int32), pltpu.SMEM((slots,), F32),
         pltpu.SMEM((table,), F32), pltpu.VMEM(held, jnp.int32),
         pltpu.VMEM(held, F32), pltpu.SemaphoreType.DMA((7,))],
    )(tile_count, *(pltpu.with_memory_space_constraint(x, pltpu.MemorySpace.HBM) for x in (
        tile_row[0, 0], col_index, tile_scale[0, 0], receiver_weight,
        ray_receiver.reshape(held), delays.reshape(held), block)))
    turn = lambda given: (given, *local_call(turn_body, "turn", [VM], [(block.shape, BF16)])(block))
    near, far, (damp, turned) = gather_rays(mine, extra, (lambda _: damp, turn))
    named = ((names_n, LAT), jnp.int32)

    half, half_lines, names_a = local_call(
        functools.partial(first_half_body, slots), "first_half", [VM] * 2,
        [slab, ((slots, LAT), F32), named],
    )(near, own)
    field, lines, sums, left0, names_b = local_call(
        functools.partial(first_body, slots), "first", [VM] * 7,
        [padded, ((slots, LAT), F32), ((RT + 8 + PAIRS, LAT), F32), row, named],
    )(far, half, half_lines, near, own, pick, turned)
    others, columns, swapped = first_halo(sums, field)
    onehots = local_call(
        onehot_body, "onehot", [VM] * 2, [((LINES, names_n * LAT), BF16)] * 2,
    )(names_a, names_b)
    others, (onehot_a, onehot_b) = lax.optimization_barrier((others, onehots))

    mine, rays, image, norm0 = local_call(
        functools.partial(second_body, slots), "second", [VM] * 7, [packet, (held, F32), (held, F32), row],
    )(sums, others, left0, weight, start, pick, block)
    def smooth_step(columns):
        return local_call(
            functools.partial(smooth_body, swapped), "smooth", [VM] * 7,
            [slab, padded, ((2, PAIRS, LAT), F32), row], [pltpu.VMEM((2, PAIRS, LAT), F32)],
        )(field, *columns, damp, norm0)

    def again_step(given):
        smooth, scaled, beside, square = given
        again, again_lines = local_call(
            functools.partial(again_body, slots), "again", [SM] + [VM] * 2, [slab, ((slots, LAT), F32)],
        )(col_index, scaled, beside)
        return smooth, square, again, again_lines

    near, far, given = gather_rays(mine, 8, (lambda _: (), lambda _: columns, lambda given: again_step(smooth_step(given))))
    smooth, square, again, again_lines = given

    half, half_lines = local_call(
        functools.partial(third_half_body, slots), "third_half", [VM] * 6, [slab, ((slots, LAT), F32)],
    )(near, onehot_a, names_a, own, again_lines, again)
    following, sums, shift = local_call(
        functools.partial(third_body, slots), "third", [VM] * 13,
        [padded, ((RT + 8 + PAIRS // 2, LAT), F32), row],
    )(far, half, half_lines, near, square, onehot_b, names_b, own, lines, field, norm0, pick, turned)
    others, beside, halves = next_halo(sums, following)
    last_rays, left1, rest, norm1, ray_square = local_call(
        fourth_body, "fourth", [VM] * 6, [(held, F32), row, row, row, row],
    )(sums, others, shift, weight, rays, image)

    def last_step(beside):
        return local_call(
            functools.partial(last_smooth_body, halves), "last_smooth", [VM] * 10, [row, ((4, 8, LAT), F32)],
            [pltpu.VMEM((2, PAIRS, LAT), F32)],
        )(following, *beside, damp, smooth, norm1, left1, rest, left0, norm0)

    shares, weights = last_sums(ray_square, beside, last_step)

    share = PAIRS // rays_n
    density, rays_out = local_call(
        functools.partial(end_body, share, len(shares)), "end", [VM] * (len(shares) + 4),
        [((share, LON_DEV, LAT), F32), (held, F32)],
    )(*shares, weights, last_rays, field, following)
    return (density.reshape(ALT // rays_n, EPOCHS, LON_DEV, LAT), rays_out.reshape(-1))


def solution(mesh):
    in_specs = (
        P("ray", "vox", None, None, None),
        P("ray", "vox", None),
        P("ray", "vox", None),
        P("ray", "vox", None),
        P("ray", "vox"),
        P("ray"),
        P("ray"),
        P("ray"),
        P(),
    )
    out_specs = (P("ray", None, "vox", None), P("ray"))
    return jax.shard_map(
        on_device, mesh=mesh, in_specs=in_specs, out_specs=out_specs, check_vma=False
    )
```

```python
import functools

import jax
import jax.numpy as jnp
from jax import lax
from jax.experimental import pallas as pl
from jax.experimental.pallas import tpu as pltpu
from jax.sharding import PartitionSpec as P

ALT = 64
EPOCHS = 2
LAT = 128
LON_DEV = 8
RAY_TILE = 128
RT = 8
CORES = 2
PAIRS = ALT * EPOCHS
LINES = PAIRS * LON_DEV
PAD = EPOCHS
UNROLL = 32

LATERAL = 1.0
VERTICAL = 4.0
TEMPORAL = 0.5
CENTRE = 2.0 * (2.0 * LATERAL + VERTICAL + TEMPORAL)

F32 = jnp.float32
BF16 = jnp.bfloat16
VM = pl.BlockSpec(memory_space=pltpu.VMEM)
SM = pl.BlockSpec(memory_space=pltpu.SMEM)


def local_call(body, name, in_specs, out_shapes, scratch=()):
    return pl.pallas_call(
        body,
        name=name,
        in_specs=in_specs,
        out_specs=[VM] * len(out_shapes),
        out_shape=[jax.ShapeDtypeStruct(shape, dtype) for shape, dtype in out_shapes],
        scratch_shapes=list(scratch),
        compiler_params=pltpu.CompilerParams(vmem_limit_bytes=32 << 20),
    )


def pairs_of(count, step):
    return [(i, i ^ step) for i in range(count)]


def hops(count):
    steps = []
    while count > 1:
        count //= 2
        steps.append(count | 1)
    return steps


def gather_rays(packet, extra, during=()):
    count = lax.axis_size("ray")
    if count < 2 or count & (count - 1):
        raise ValueError("ray size")
    done, given = list(during), None
    for step in hops(count):
        other = lax.ppermute(packet, "ray", pairs_of(count, step))
        if step == 1:
            break
        joined = jnp.concatenate(
            [packet[:-extra], other[:-extra], packet[-extra:] + other[-extra:]], axis=0
        )
        if done:
            given = done.pop(0)(given)
            joined, given = lax.optimization_barrier((joined, given))
        packet = joined
    while done:
        given = done.pop(0)(given)
    return packet, other, given


def vox_others(value):
    count = lax.axis_size("vox")
    if count == 1:
        return jnp.zeros_like(value)
    if count == 2:
        return lax.ppermute(value, "vox", [(0, 1), (1, 0)])
    return lax.psum(value, "vox") - value


def last_sums(value, given, step_of):
    count, slabs = lax.axis_size("ray"), lax.axis_size("vox")
    if slabs != 2 or count & (count - 1) or count < 16:
        mine, rest = step_of(given)
        return (lax.psum(value, "ray"), mine, vox_others(mine)), rest
    for step in hops(count)[:-2]:
        value = value + lax.ppermute(value, "ray", pairs_of(count, step))
        if step == count // 4 | 1:
            given = step_of(given)
        value, given = lax.optimization_barrier((value, given))
    mine, rest = given
    both = jnp.concatenate([value, mine], axis=0)
    both = lax.ppermute(both, ("ray", "vox"), [(i, i ^ 7) for i in range(2 * count)])
    value = value + both[:8]
    return (value, lax.ppermute(value, "ray", pairs_of(count, 1)), mine, both[8:]), rest


def halo_of(low_edge, high_edge):
    count = lax.axis_size("vox")
    if count == 1:
        return jnp.zeros_like(high_edge), jnp.zeros_like(low_edge)
    forward = [(i, i + 1) for i in range(count - 1)]
    backward = [(target, source) for source, target in forward]
    return lax.ppermute(high_edge, "vox", forward), lax.ppermute(low_edge, "vox", backward)


def first_halo(sums, field):
    if lax.axis_size("vox") == 2 and lax.axis_size("ray") % 2 == 0:
        other = lax.ppermute(sums, "vox", [(0, 1), (1, 0)])
        column = other[RT + 8 :]
        partner = lax.ppermute(column, "ray", pairs_of(lax.axis_size("ray"), 1))
        return other, (column, partner, column, partner), True
    low = halo_of(field[PAD:-PAD, 0], field[PAD:-PAD, -1])
    far = halo_of(field[PAD:-PAD, 1], field[PAD:-PAD, -2])
    return vox_others(sums), (low[0], far[0], low[1], far[1]), False


def next_halo(sums, field):
    if lax.axis_size("vox") == 2 and lax.axis_size("ray") % 2 == 0:
        other = lax.ppermute(sums, "vox", [(0, 1), (1, 0)])
        half = other[RT + 8 :]
        return other, (half, lax.ppermute(half, "ray", pairs_of(lax.axis_size("ray"), 1))), True
    return vox_others(sums), halo_of(field[PAD:-PAD, 0], field[PAD:-PAD, -1]), False


def total(values):
    return jnp.sum(values, axis=(0, 1), keepdims=True)


def sub_iota(shape=(8, LAT)):
    return lax.broadcasted_iota(jnp.int32, shape, 0)


def lane_iota(shape=(8, LAT)):
    return lax.broadcasted_iota(jnp.int32, shape, 1)


def pull_lines(weighted, tiles_ref, pick_ref, out_ref, slots):
    rays = weighted.astype(BF16)
    for k in range(0, slots, 2):
        pair = jnp.concatenate([tiles_ref[k], tiles_ref[k + 1]], axis=1)
        product = jnp.dot(rays, pair, preferred_element_type=F32)
        out_ref[pl.ds(k, 1), :] = jnp.sum(pick_ref[k] * product[:, :LAT], axis=0, keepdims=True)
        out_ref[pl.ds(k + 1, 1), :] = jnp.sum(pick_ref[k + 1] * product[:, LAT:], axis=0, keepdims=True)


def push_lines(rays, lines, turned_ref, pick_ref, first, last):
    for k in range(first, last, 2):
        both = [jnp.broadcast_to(lines[j : j + 1], (RT, LAT)) for j in (k, k + 1)]
        pair = jnp.concatenate([turned_ref[k], turned_ref[k + 1]], axis=1)
        product = jnp.dot(
            jnp.concatenate(both, axis=0).astype(BF16), pair, preferred_element_type=F32
        )
        rays = rays + pick_ref[k] * product[:RT, :RAY_TILE]
        rays = rays + pick_ref[k + 1] * product[RT:, RAY_TILE:]
    return rays


def both_parts(lines):
    high = lines.astype(BF16)
    low = (lines - high.astype(F32)).astype(BF16)
    return jnp.concatenate([high, low], axis=1)


def across(values, sub, lane):
    up = jnp.where(lane == 0, 0.0, pltpu.roll(values, 1, 1))
    down = jnp.where(lane == LAT - 1, 0.0, pltpu.roll(values, LAT - 1, 1))
    return up + down


def column_stencil(column, beside, lane, sub):
    up = jnp.where(sub < EPOCHS, 0.0, pltpu.roll(column, EPOCHS, 0))
    down = jnp.where(sub >= PAIRS - EPOCHS, 0.0, pltpu.roll(column, PAIRS - EPOCHS, 0))
    later = pltpu.roll(column, PAIRS - 1, 0)
    earlier = pltpu.roll(column, 1, 0)
    epoch = jnp.where(sub % EPOCHS == 0, later, earlier)
    return (
        CENTRE * column
        - LATERAL * (beside + across(column, sub, lane))
        - VERTICAL * (up + down)
        - TEMPORAL * epoch
    )


def slab_stencil(pair, field_ref, low_ref, high_ref, sub, lane):
    here = field_ref[pair + PAD]
    below = jnp.where(sub == 0, low_ref[pl.ds(pair, 1), :], pltpu.roll(here, 1, 0))
    above = jnp.where(sub == LON_DEV - 1, high_ref[pl.ds(pair, 1), :], pltpu.roll(here, LON_DEV - 1, 0))
    epoch = field_ref[(pair ^ 1) + PAD]
    return (
        CENTRE * here
        - LATERAL * (below + above + across(here, sub, lane))
        - VERTICAL * (field_ref[pair] + field_ref[pair + 2 * PAD])
        - TEMPORAL * epoch
    )


def start_body(slots, count_ref, row_in, col_in, scale_in, table_in, receiver_in, delays_in, tiles_in,
               packet_ref, weight_ref, start_ref, pick_ref, own_ref, tiles_ref,
               row_ref, col_ref, scale_ref, table_ref, receiver_ref, delays_ref, sems):
    copies = [
        pltpu.make_async_copy(source, target, sems.at[j])
        for j, (source, target) in enumerate([
            (receiver_in, receiver_ref), (table_in, table_ref), (delays_in, delays_ref),
            (scale_in, scale_ref), (row_in, row_ref), (col_in, col_ref),
        ])
    ]
    pull = pltpu.make_async_copy(tiles_in, tiles_ref, sems.at[6])
    pull.start()
    for copy in copies:
        copy.start()
    for copy in copies:
        copy.wait()
    sub, lane = sub_iota(), lane_iota()
    receivers = receiver_ref[...]
    weight = jnp.zeros((RT, RAY_TILE), F32)
    for j in range(table_ref.shape[0]):
        weight = jnp.where(receivers == j, table_ref[j], weight)
    weight_ref[...] = weight
    start = weight * delays_ref[...]
    start_ref[...] = start
    extra = packet_ref.shape[0] - slots
    sub_x, lane_x = sub_iota((extra, LAT)), lane_iota((extra, LAT))
    side, place = own_place()
    rows, per = names_rows(slots), LAT // slots
    first = place % per * slots
    names = jnp.zeros((1, LAT), jnp.int32)
    for k in range(slots):
        live = jnp.where(k < count_ref[0, 0], scale_ref[k], 0.0)
        pick_ref[k] = jnp.where(sub == row_ref[k], live, 0.0)
        own_ref[pl.ds(k, 1), :] = jnp.full((1, LAT), col_ref[k], jnp.int32)
        names = jnp.where(lane[:1] == first + k, col_ref[k], names)
    square = total(start * start)
    packet_ref[slots:, :] = jnp.where(
        sub_x == side * rows + place // per,
        jnp.broadcast_to(names.astype(F32), (extra, LAT)),
        jnp.where(sub_x == CORES * rows, square, 0.0),
    )
    pull.wait()
    pull_lines(weight * start, tiles_ref, pick_ref, packet_ref, slots)


def turn_body(tiles_ref, turned_ref):
    for k in range(tiles_ref.shape[0]):
        turned_ref[k] = tiles_ref[k].T


def own_place():
    count, at = lax.axis_size("ray"), lax.axis_index("ray")
    side, place, bit = at % 2, 0, 1
    for step in hops(count)[:-1]:
        digit = at // (step - 1) % 2
        side = (side + digit) % 2
        place = place + bit * digit
        bit *= 2
    return side, place


def names_rows(slots):
    return lax.axis_size("ray") // CORES * slots // LAT


def names_of(ref, side, slots):
    rows = names_rows(slots)
    first = lax.axis_size("ray") // CORES * slots + side * rows
    return [ref[pl.ds(first + j, 1), :].astype(jnp.int32) for j in range(rows)]


def placed_lines(ref, slots):
    place = own_place()[1]
    return jnp.concatenate(
        [
            ref[pl.ds(pl.multiple_of((j ^ place) * slots, slots), slots), :]
            for j in range(lax.axis_size("ray") // CORES)
        ],
        axis=0,
    )


def extra_row(ref, slots, at):
    first = lax.axis_size("ray") // CORES * slots
    return ref[first + at : first + at + 1, :]


def found_lines(onehot, parts):
    found = jnp.dot(onehot, parts, preferred_element_type=F32)
    return found[:, :LAT] + found[:, LAT:]


CHUNK = 256


def onehot_of(names, ids):
    return jnp.concatenate(
        [jnp.where(ids == piece, 1.0, 0.0).astype(BF16) for piece in names], axis=1
    )


def edge_of(field_ref, at):
    flat = field_ref.reshape((PAIRS + 2 * PAD) * LON_DEV, LAT)
    return flat[pl.ds(PAD * LON_DEV + at, PAIRS, stride=LON_DEV), :]


def first_half_body(slots, mine_ref, own_ref, field_ref, lines_ref, names_ref):
    names = names_of(mine_ref, own_place()[0], slots)
    for j, piece in enumerate(names):
        names_ref[pl.ds(j, 1), :] = piece
    parts = both_parts(placed_lines(mine_ref, slots))
    lines_ref[...] = found_lines(onehot_of(names, own_ref[...]), parts)
    for first in range(0, LINES, CHUNK):
        onehot = onehot_of(names, sub_iota((CHUNK, LAT)) + first)
        piece = found_lines(onehot, parts).reshape(CHUNK // LON_DEV, LON_DEV, LAT)
        field_ref[first // LON_DEV : (first + CHUNK) // LON_DEV] = piece


def first_body(slots, other_ref, half_ref, half_lines_ref, mine_ref, own_ref, pick_ref, turned_ref,
               field_ref, lines_ref, out_ref, left_ref, names_ref):
    names = names_of(other_ref, 1 - own_place()[0], slots)
    for j, piece in enumerate(names):
        names_ref[pl.ds(j, 1), :] = piece
    parts = both_parts(placed_lines(other_ref, slots))
    lines = half_lines_ref[...] + found_lines(onehot_of(names, own_ref[...]), parts)
    lines_ref[...] = lines
    rays, part = jnp.zeros((RT, RAY_TILE), F32), slots * CHUNK // LINES
    zeros = jnp.zeros((PAD, LON_DEV, LAT), F32)
    field_ref[:PAD] = zeros
    field_ref[PAIRS + PAD :] = zeros
    square = jnp.zeros((8, LAT), F32)
    for first in range(0, LINES, CHUNK):
        onehot = onehot_of(names, sub_iota((CHUNK, LAT)) + first)
        count, pair = CHUNK // LON_DEV, first // LON_DEV
        piece = found_lines(onehot, parts).reshape(count, LON_DEV, LAT) + half_ref[pair : pair + count]
        field_ref[pair + PAD : pair + PAD + count] = piece
        square = square + jnp.sum(piece * piece, axis=0)
        rays = push_lines(rays, lines, turned_ref, pick_ref, first // CHUNK * part, (first // CHUNK + 1) * part)
    out_ref[:RT, :] = rays
    out_ref[RT : RT + 8, :] = jnp.broadcast_to(total(square), (8, LAT))
    odd = lax.axis_index("ray") % 2
    at = jnp.where(lax.axis_index("vox") == 0, LON_DEV - 1 - odd, odd)
    out_ref[RT + 8 :, :] = edge_of(field_ref, at)
    at = CORES * names_rows(slots)
    left = extra_row(mine_ref, slots, at) + extra_row(other_ref, slots, at)
    left_ref[...] = jnp.broadcast_to(left, (8, LAT))


def second_body(slots, mine_ref, other_ref, left_ref, weight_ref, start_ref, pick_ref, tiles_ref,
                packet_ref, rays_ref, image_ref, norm_ref):
    sub = sub_iota()
    left_sq = left_ref[...]
    norm_sq = mine_ref[RT : RT + 8, :] + other_ref[RT : RT + 8, :]
    inverse = lax.rsqrt(norm_sq)
    norm = norm_sq * inverse
    weight = weight_ref[...]
    image = (mine_ref[:RT, :] + other_ref[:RT, :]) * inverse
    image_ref[...] = image
    rays = weight * image - norm / left_sq * start_ref[...]
    rays_ref[...] = rays
    norm_ref[...] = norm
    pull_lines(weight * rays, tiles_ref, pick_ref, packet_ref, slots)
    packet_ref[slots:, :] = jnp.where(sub == 0, total(rays * rays), 0.0)


def flags():
    at, count = lax.axis_index("vox"), lax.axis_size("vox")
    return (at > 0).astype(F32), (at < count - 1).astype(F32)


def smooth_body(swapped, field_ref, low_ref, low2_ref, high_ref, high2_ref, damp_ref, norm_ref,
                smooth_ref, scaled_ref, far_ref, square_ref, near_ref):
    sub, lane = sub_iota(), lane_iota()
    has_low, has_high = flags()
    inverse = 1.0 / norm_ref[...]
    col_lane, col_sub = lane_iota((PAIRS, LAT)), sub_iota((PAIRS, LAT))
    low, low2, high, high2 = low_ref[...], low2_ref[...], high_ref[...], high2_ref[...]
    if swapped:
        odd = lax.axis_index("ray") % 2 == 1
        low, low2 = jnp.where(odd, low2, low), jnp.where(odd, low, low2)
        high, high2 = low, low2
    near_ref[0] = low * has_low
    near_ref[1] = high * has_high
    scale = damp_ref[...] * damp_ref[...] * jnp.broadcast_to(inverse[:1], (PAIRS, LAT))
    far_ref[0] = scale * has_low * column_stencil(low, low2 + edge_of(field_ref, 0), col_lane, col_sub)
    far_ref[1] = scale * has_high * column_stencil(
        high, high2 + edge_of(field_ref, LON_DEV - 1), col_lane, col_sub
    )
    zeros = jnp.zeros((PAD, LON_DEV, LAT), F32)
    scaled_ref[:PAD] = zeros
    scaled_ref[PAIRS + PAD :] = zeros

    def left(pair, square):
        damped = damp_ref[pl.ds(pair, 1), :]
        value = slab_stencil(pair, field_ref, near_ref.at[0], near_ref.at[1], sub, lane) * inverse * damped
        smooth_ref[pair] = value
        scaled_ref[pair + PAD] = value * damped
        return square + value * value

    square = lax.fori_loop(0, PAIRS, left, jnp.zeros((LON_DEV, LAT), F32), unroll=UNROLL)
    square_ref[...] = jnp.broadcast_to(total(square), (8, LAT))


def onehot_body(*refs):
    names_refs, onehot_refs = refs[: len(refs) // 2], refs[len(refs) // 2 :]
    for names_ref, onehot_ref in zip(names_refs, onehot_refs):
        pieces = [names_ref[pl.ds(j, 1), :] for j in range(onehot_ref.shape[1] // LAT)]
        for first in range(0, LINES, CHUNK):
            onehot_ref[first : first + CHUNK, :] = onehot_of(pieces, sub_iota((CHUNK, LAT)) + first)


def again_body(slots, col_in, scaled_ref, far_ref, again_ref, lines_ref, col_ref, sem):
    copy = pltpu.make_async_copy(col_in, col_ref, sem)
    copy.start()
    sub, lane = sub_iota(), lane_iota()

    def right(pair, carry):
        again_ref[pair] = slab_stencil(pair, scaled_ref, far_ref.at[0], far_ref.at[1], sub, lane)
        return carry

    lax.fori_loop(0, PAIRS, right, 0, unroll=UNROLL)
    copy.wait()
    for k in range(slots):
        col = col_ref[k]
        lines_ref[pl.ds(k, 1), :] = again_ref[col // LON_DEV, pl.ds(col % LON_DEV, 1), :]


def third_half_body(slots, mine_ref, onehot_ref, names_ref, own_ref, again_lines_ref, again_ref,
                    half_ref, lines_ref):
    parts = both_parts(placed_lines(mine_ref, slots))
    names = [names_ref[pl.ds(j, 1), :] for j in range(onehot_ref.shape[1] // LAT)]
    lines_ref[...] = found_lines(onehot_of(names, own_ref[...]), parts) + again_lines_ref[...]
    for first in range(0, LINES, CHUNK):
        count, pair = CHUNK // LON_DEV, first // LON_DEV
        piece = found_lines(onehot_ref[first : first + CHUNK, :], parts).reshape(count, LON_DEV, LAT)
        half_ref[pair : pair + count] = piece + again_ref[pair : pair + count]


def third_body(slots, other_ref, half_ref, half_lines_ref, mine_ref, square_ref, onehot_ref, names_ref, own_ref,
               lines_ref, field_ref, norm_ref, pick_ref, turned_ref,
               next_ref, out_ref, shift_ref):
    shift = jnp.broadcast_to(extra_row(mine_ref, slots, 0) + extra_row(other_ref, slots, 0), (8, LAT))
    shift_ref[...] = shift
    inverse = 1.0 / norm_ref[...]
    back = shift * inverse
    parts = both_parts(placed_lines(other_ref, slots))
    names = [names_ref[pl.ds(j, 1), :] for j in range(onehot_ref.shape[1] // LAT)]
    lines = found_lines(onehot_of(names, own_ref[...]), parts) + half_lines_ref[...] - lines_ref[...] * back[:1]
    rays, part = jnp.zeros((RT, RAY_TILE), F32), slots * CHUNK // LINES
    zeros = jnp.zeros((PAD, LON_DEV, LAT), F32)
    next_ref[:PAD] = zeros
    next_ref[PAIRS + PAD :] = zeros
    square = jnp.zeros((8, LAT), F32)
    cross = jnp.zeros((8, LAT), F32)
    for first in range(0, LINES, CHUNK):
        count, pair = CHUNK // LON_DEV, first // LON_DEV
        piece = found_lines(onehot_ref[first : first + CHUNK, :], parts).reshape(count, LON_DEV, LAT)
        base = field_ref[pair + PAD : pair + PAD + count]
        piece = piece + half_ref[pair : pair + count] - base * back
        next_ref[pair + PAD : pair + PAD + count] = piece
        square = square + jnp.sum(piece * piece, axis=0)
        cross = cross + jnp.sum(piece * base, axis=0)
        rays = push_lines(rays, lines, turned_ref, pick_ref, first // CHUNK * part, (first // CHUNK + 1) * part)
    sub = sub_iota()
    out_ref[:RT, :] = rays
    out_ref[RT : RT + 8, :] = jnp.where(
        sub == 0, total(square), jnp.where(sub == 1, total(cross) * inverse, square_ref[...])
    )
    edge = edge_of(next_ref, jnp.where(lax.axis_index("vox") == 0, LON_DEV - 1, 0))
    half = PAIRS // 2
    out_ref[RT + 8 :, :] = jnp.where(lax.axis_index("ray") % 2 == 0, edge[:half], edge[half:])


def fourth_body(mine_ref, other_ref, shift_ref, weight_ref, rays_ref, image_ref,
                next_rays_ref, left_ref, rest_ref, norm_ref, sum_ref):
    sums = mine_ref[RT : RT + 8, :] + other_ref[RT : RT + 8, :]
    square, cross, rest = [jnp.broadcast_to(sums[j : j + 1], (8, LAT)) for j in range(3)]
    left_sq = shift_ref[...] + rest
    norm_sq = (square - 2.0 * rest * cross + rest * rest) / left_sq
    per_left = lax.rsqrt(left_sq)
    inverse = lax.rsqrt(norm_sq)
    norm = norm_sq * inverse
    rays = mine_ref[:RT, :] + other_ref[:RT, :] - rest * image_ref[...]
    rays = weight_ref[...] * rays * (per_left * inverse) - norm * per_left * rays_ref[...]
    next_rays_ref[...] = rays
    left_ref[...] = left_sq
    rest_ref[...] = rest
    norm_ref[...] = norm
    sum_ref[...] = jnp.broadcast_to(total(rays * rays), (8, LAT))


def last_smooth_body(halves, next_ref, low_ref, high_ref, damp_ref, smooth_ref, norm_ref, left_ref, rest_ref,
                     left0_ref, norm0_ref, square_ref, weights_ref, near_ref):
    sub, lane = sub_iota(), lane_iota()
    has_low, has_high = flags()
    if halves:
        odd, half = lax.axis_index("ray") % 2, PAIRS // 2
        for ref, at in ((low_ref, odd), (high_ref, 1 - odd)):
            near_ref[0, pl.ds(at * half, half), :] = ref[...] * has_low
            near_ref[1, pl.ds(at * half, half), :] = ref[...] * has_high
    else:
        near_ref[0] = low_ref[...] * has_low
        near_ref[1] = high_ref[...] * has_high
    norm, per_left = norm_ref[...], lax.rsqrt(left_ref[...])
    inverse = per_left / norm
    back = rest_ref[...] * inverse + norm * per_left

    def left(pair, square):
        damped = damp_ref[pl.ds(pair, 1), :]
        value = slab_stencil(pair, next_ref, near_ref.at[0], near_ref.at[1], sub, lane) * inverse * damped
        value = value - back * smooth_ref[pair]
        return square + value * value

    square = lax.fori_loop(0, PAIRS, left, jnp.zeros((LON_DEV, LAT), F32), unroll=UNROLL)
    square_ref[...] = jnp.broadcast_to(total(square), (8, LAT))
    left0_sq, norm0, left1_sq = left0_ref[...], norm0_ref[...], left_ref[...]
    left0, left1 = jnp.sqrt(left0_sq), jnp.sqrt(left1_sq)
    right0 = norm0 / left0
    diag1 = jnp.sqrt(right0 * right0 + left1_sq)
    cosine, sine = right0 / diag1, left1 / diag1
    coupling = sine * norm
    diag_bar = -cosine * norm
    step1, resid = cosine * left0, sine * left0
    weights_ref[0] = diag_bar * resid / (left1 * norm)
    weights_ref[1] = diag_bar * diag_bar
    weights_ref[2] = step1 / diag1 / norm0
    weights_ref[3] = (left1 * norm * coupling / diag1 + rest_ref[...]) / norm0


def end_body(share, parts, *refs):
    left2_sq = refs[0][...]
    for ref in refs[1:parts]:
        left2_sq = left2_sq + ref[...]
    weights_ref, rays_ref, field_ref, next_ref, density_ref, out_ref = refs[parts:]
    out_ref[...] = rays_ref[...] * lax.rsqrt(left2_sq)
    on_next = weights_ref[0] / (weights_ref[1] + left2_sq)
    on_first = weights_ref[2] - weights_ref[3] * on_next
    first = lax.axis_index("ray") * share + PAD
    for j in range(share):
        density_ref[j] = on_first * field_ref[first + j] + on_next * next_ref[first + j]


def on_device(
    tiles,
    tile_scale,
    tile_row,
    tile_col,
    tile_count,
    delays,
    ray_receiver,
    receiver_weight,
    smooth_scale,
):
    block = tiles[0, 0]
    slots = block.shape[0]
    rays_n = lax.axis_size("ray")
    col_index = tile_col[0, 0]
    held = (RT, RAY_TILE)
    row = ((8, LAT), F32)
    slab = ((PAIRS, LON_DEV, LAT), F32)
    padded = ((PAIRS + 2 * PAD, LON_DEV, LAT), F32)
    packet = ((slots + 8, LAT), F32)
    names_n = rays_n // CORES * slots // LAT
    extra = -(-(CORES * names_n + 1) // 8) * 8
    damp = jnp.broadcast_to(jnp.repeat(smooth_scale, EPOCHS)[:, None], (PAIRS, LAT))

    hbm = pl.BlockSpec(memory_space=pl.ANY)
    table = receiver_weight.shape[0]
    mine, weight, start, pick, own, block = local_call(
        functools.partial(start_body, slots), "start", [SM] + [hbm] * 7,
        [((slots + extra, LAT), F32), (held, F32), (held, F32), ((slots, RT, LAT), F32), ((slots, LAT), jnp.int32),
         (block.shape, BF16)],
        [pltpu.SMEM((slots,), jnp.int32), pltpu.SMEM((slots,), jnp.int32), pltpu.SMEM((slots,), F32),
         pltpu.SMEM((table,), F32), pltpu.VMEM(held, jnp.int32),
         pltpu.VMEM(held, F32), pltpu.SemaphoreType.DMA((7,))],
    )(tile_count, *(pltpu.with_memory_space_constraint(x, pltpu.MemorySpace.HBM) for x in (
        tile_row[0, 0], col_index, tile_scale[0, 0], receiver_weight,
        ray_receiver.reshape(held), delays.reshape(held), block)))
    turn = lambda given: (given, *local_call(turn_body, "turn", [VM], [(block.shape, BF16)])(block))
    near, far, (damp, turned) = gather_rays(mine, extra, (lambda _: damp, turn))
    named = ((names_n, LAT), jnp.int32)

    half, half_lines, names_a = local_call(
        functools.partial(first_half_body, slots), "first_half", [VM] * 2,
        [slab, ((slots, LAT), F32), named],
    )(near, own)
    field, lines, sums, left0, names_b = local_call(
        functools.partial(first_body, slots), "first", [VM] * 7,
        [padded, ((slots, LAT), F32), ((RT + 8 + PAIRS, LAT), F32), row, named],
    )(far, half, half_lines, near, own, pick, turned)
    others, columns, swapped = first_halo(sums, field)
    onehots = local_call(
        onehot_body, "onehot", [VM] * 2, [((LINES, names_n * LAT), BF16)] * 2,
    )(names_a, names_b)
    others, (onehot_a, onehot_b) = lax.optimization_barrier((others, onehots))

    mine, rays, image, norm0 = local_call(
        functools.partial(second_body, slots), "second", [VM] * 7, [packet, (held, F32), (held, F32), row],
    )(sums, others, left0, weight, start, pick, block)
    def smooth_step(columns):
        return local_call(
            functools.partial(smooth_body, swapped), "smooth", [VM] * 7,
            [slab, padded, ((2, PAIRS, LAT), F32), row], [pltpu.VMEM((2, PAIRS, LAT), F32)],
        )(field, *columns, damp, norm0)

    def again_step(given):
        smooth, scaled, beside, square = given
        again, again_lines = local_call(
            functools.partial(again_body, slots), "again", [hbm] + [VM] * 2, [slab, ((slots, LAT), F32)],
            [pltpu.SMEM((slots,), jnp.int32), pltpu.SemaphoreType.DMA],
        )(pltpu.with_memory_space_constraint(col_index, pltpu.MemorySpace.HBM), scaled, beside)
        return smooth, square, again, again_lines

    near, far, given = gather_rays(mine, 8, (lambda _: (), lambda _: columns, lambda given: again_step(smooth_step(given))))
    smooth, square, again, again_lines = given

    half, half_lines = local_call(
        functools.partial(third_half_body, slots), "third_half", [VM] * 6, [slab, ((slots, LAT), F32)],
    )(near, onehot_a, names_a, own, again_lines, again)
    following, sums, shift = local_call(
        functools.partial(third_body, slots), "third", [VM] * 13,
        [padded, ((RT + 8 + PAIRS // 2, LAT), F32), row],
    )(far, half, half_lines, near, square, onehot_b, names_b, own, lines, field, norm0, pick, turned)
    others, beside, halves = next_halo(sums, following)
    last_rays, left1, rest, norm1, ray_square = local_call(
        fourth_body, "fourth", [VM] * 6, [(held, F32), row, row, row, row],
    )(sums, others, shift, weight, rays, image)

    def last_step(beside):
        return local_call(
            functools.partial(last_smooth_body, halves), "last_smooth", [VM] * 10, [row, ((4, 8, LAT), F32)],
            [pltpu.VMEM((2, PAIRS, LAT), F32)],
        )(following, *beside, damp, smooth, norm1, left1, rest, left0, norm0)

    shares, weights = last_sums(ray_square, beside, last_step)

    share = PAIRS // rays_n
    density, rays_out = local_call(
        functools.partial(end_body, share, len(shares)), "end", [VM] * (len(shares) + 4),
        [((share, LON_DEV, LAT), F32), (held, F32)],
    )(*shares, weights, last_rays, field, following)
    return (density.reshape(ALT // rays_n, EPOCHS, LON_DEV, LAT), rays_out.reshape(-1))


def solution(mesh):
    in_specs = (
        P("ray", "vox", None, None, None),
        P("ray", "vox", None),
        P("ray", "vox", None),
        P("ray", "vox", None),
        P("ray", "vox"),
        P("ray"),
        P("ray"),
        P("ray"),
        P(),
    )
    out_specs = (P("ray", None, "vox", None), P("ray"))
    return jax.shard_map(
        on_device, mesh=mesh, in_specs=in_specs, out_specs=out_specs, check_vma=False
    )
```
